128 devices in a mesh: tok: 16 (over y, z), head: 8 (over x, core).
Axes of the slice: x: 4, y: 4, z: 4, core: 2. Of those that a mesh axis runs over, the one named last changes fastest.
Arguments:
- prefill_states: bfloat16 [4, 2048, 2048], P(None, 'tok'), may hold values from -6 to 6
- decode_states: bfloat16 [128, 2048], P('tok'), may hold values from -6 to 6
- attn_gain: float32 [2048], replicated, may hold values from 0.1 to 1.9
- w_qkv: bfloat16 [2048, 3, 2048], P(None, None, 'head'), may hold values from -0.125 to 0.125
- w_out: bfloat16 [2048, 2048], P('head'), may hold values from -0.125 to 0.125
- ffn_gain: float32 [2048], replicated, may hold values from 0.1 to 1.9
- w_gate_up: bfloat16 [2048, 2, 5120], P(None, None, 'tok'), may hold values from -0.125 to 0.125
- w_down: bfloat16 [5120, 2048], P('tok'), may hold values from -0.078125 to 0.078125
- prefill_pool: bfloat16 [768, 128, 1024], P('tok', None, 'head')
- prefill_pages: int32 [16, 48], P('tok'), may hold values from 0 to 47, as said below
- prefill_lengths: int32 [4], replicated, may hold values from 1 to 6144, as said below
- prefill_home: int32 [16], replicated, may hold values from 0 to 15, each once
- decode_pool: bfloat16 [1024, 128, 4096], P('tok', None, 'head')
- decode_pages: int32 [128, 32], P('tok'), may hold values from 0 to 63, as said below
- decode_lengths: int32 [128], P('tok'), may hold values from 1 to 4096, as said below
- decode_home: int32 [128], replicated, may hold values from 0 to 127, each once
Outputs:
- prefill_out: bfloat16 [4, 2048, 2048], P(None, ('tok', 'head'))
- decode_out: bfloat16 [128, 2048], P(('tok', 'head'))
The draws below stay inside these ranges and needn't reach their ends.
Inputs may be any that keep to these rules, and one draw needn't show every extreme that they name: `prefill_pages`: each row is an ordering of all 48 pages of the prefill pool on that row's tok index. `prefill_lengths`: one prefill request has exactly 6144 cached tokens. `decode_pages`: slot s lies on tok index s // 8; within one tok index the first ceil(length / 128) pages of its slots are all different. `decode_lengths`: every tok index hosts one decode request of exactly 4096 cached tokens.
All inputs are finite; a program needn't handle non-finite values.
Results may differ from the reference program's by a relative error of at most 0.017.
The reference program's roundings to bfloat16 on the way count: a program that leaves them out, or rounds other values in their place, can miss the bound.
Values may be sent and summed in bfloat16 or wider, within the bound.
A program may use at most 128 MiB of HBM per device.

```python
import jax
import jax.numpy as jnp
from jax import lax

D = 2048
H = 32
HD = 64
FF = 5120
PAGE = 128
STRETCH = 2048
PCACHE = 6144
DEC_DEV = 8
DCACHE = 4096
HH = 4
NPRE = 4
NDEC = 128
PPD = 48
DPD = 64
DMAXP = 32
N_TOK = 16
N_HEAD = 8


def pool_values(key, rows, width):
    base = jax.random.normal(key, (rows, PAGE, width), jnp.float32)
    return base.astype(jnp.bfloat16)


def draw_prefill_pool(key, part):
    return pool_values(jax.random.fold_in(key, 21), N_TOK * PPD, N_HEAD * 2 * HD)


def draw_decode_pool(key, part):
    return pool_values(jax.random.fold_in(key, 22), N_TOK * DPD, H * 2 * HD)


def draw_prefill_pages(key, part):
    subkeys = jax.random.split(jax.random.fold_in(key, 5), N_TOK)
    return jax.vmap(lambda subkey: jax.random.permutation(subkey, PPD))(subkeys).astype(jnp.int32)


def draw_prefill_lengths(key, part):
    base = jax.random.fold_in(key, 9)
    lengths = jax.random.randint(jax.random.fold_in(base, 1), (NPRE,), 1, PCACHE + 1)
    longest = jax.random.randint(jax.random.fold_in(base, 2), (), 0, NPRE)
    return jnp.where(jnp.arange(NPRE) == longest, PCACHE, lengths).astype(jnp.int32)


def decode_layout(key):
    base = jax.random.fold_in(key, 11)
    longest = jax.random.randint(jax.random.fold_in(base, 1), (N_TOK,), 0, DEC_DEV)
    shorter = min(DCACHE, (DPD - DMAXP) // (DEC_DEV - 1) * PAGE)
    lengths = jax.random.randint(jax.random.fold_in(base, 2), (N_TOK, DEC_DEV), 1, shorter + 1)
    lengths = jnp.where(jnp.arange(DEC_DEV)[None, :] == longest[:, None], DCACHE, lengths)
    used = (lengths + PAGE - 1) // PAGE
    offset = jnp.cumsum(used, axis=1) - used
    subkeys = jax.random.split(jax.random.fold_in(base, 3), N_TOK)
    orders = jax.vmap(lambda subkey: jax.random.permutation(subkey, DPD))(subkeys)
    index = (offset[:, :, None] + jnp.arange(DMAXP)[None, None, :]) % DPD
    pages = jax.vmap(lambda order, where_at: order[where_at])(orders, index)
    return (lengths.reshape(NDEC).astype(jnp.int32), pages.reshape(NDEC, DMAXP).astype(jnp.int32))


def draw_decode_lengths(key, part):
    return decode_layout(key)[0]


def draw_decode_pages(key, part):
    return decode_layout(key)[1]


def block_levels(rng, dims, cuts, smallest, top_value):
    loudness, own = 1.0, jax.random.fold_in(rng, 6)
    for dim, parts in cuts:
        draws = jnp.exp(jax.random.uniform(jax.random.fold_in(own, dim), (parts,), jnp.float32, smallest / len(cuts), top_value / len(cuts)))
        loudness = loudness * jnp.repeat(draws, dims[dim] // parts).reshape([-1 if axis == dim else 1 for axis in range(len(dims))])
    return loudness


def gaussian(own_key, dims, spread, most, cuts=(), kind=jnp.bfloat16):
    values = jax.random.normal(own_key, dims, jnp.float32) * spread
    if len(cuts) > 0:
        values = block_levels(own_key, dims, cuts, -0.22, 0.18) * values
    return jnp.clip(values, min=-most, max=most).astype(kind)


def setup_inputs(seed: int = 0) -> dict:
    splits = jax.random.split(jax.random.key(seed), 17)
    prefill_states = gaussian(splits[0], (NPRE, STRETCH, D), 1.0, 6.0, ((1, 16),))
    decode_states = gaussian(splits[1], (NDEC, D), 1.0, 6.0, ((0, 16),))
    attn_gain = jnp.clip(1.0 + 0.18 * jax.random.normal(splits[2], (D,), jnp.float32), 0.1, 1.9)
    w_qkv = gaussian(splits[3], (D, 3, H * HD), D ** -0.5, 0.125, ((2, 8),))
    w_out = gaussian(splits[4], (H * HD, D), (H * HD) ** -0.5, 0.125, ((0, 8),))
    ffn_gain = jnp.clip(1.0 + 0.18 * jax.random.normal(splits[5], (D,), jnp.float32), 0.1, 1.9)
    w_gate_up = gaussian(splits[6], (D, 2, FF), D ** -0.5, 0.125, ((2, 16),))
    w_down = gaussian(splits[7], (FF, D), FF ** -0.5, 0.078125, ((0, 16),))
    prefill_pool = draw_prefill_pool(jax.random.fold_in(splits[16], 71), 0)
    prefill_pages = draw_prefill_pages(jax.random.fold_in(splits[16], 71), 0)
    prefill_lengths = draw_prefill_lengths(jax.random.fold_in(splits[16], 71), 0)
    prefill_home = jax.random.permutation(splits[11], N_TOK).astype(jnp.int32)
    decode_pool = draw_decode_pool(jax.random.fold_in(splits[16], 71), 0)
    decode_pages = draw_decode_pages(jax.random.fold_in(splits[16], 71), 0)
    decode_lengths = draw_decode_lengths(jax.random.fold_in(splits[16], 71), 0)
    decode_home = jax.random.permutation(splits[15], NDEC).astype(jnp.int32)
    return {"prefill_states": prefill_states, "decode_states": decode_states, "attn_gain": attn_gain, "w_qkv": w_qkv, "w_out": w_out, "ffn_gain": ffn_gain, "w_gate_up": w_gate_up, "w_down": w_down, "prefill_pool": prefill_pool, "prefill_pages": prefill_pages, "prefill_lengths": prefill_lengths, "prefill_home": prefill_home, "decode_pool": decode_pool, "decode_pages": decode_pages, "decode_lengths": decode_lengths, "decode_home": decode_home}


EPSILON = 1e-06
SCALE = 0.125
MASKED = -1e+30

def rms_norm(rows, gain):
    values = rows.astype(jnp.float32)
    inverse = lax.rsqrt(lax.optimization_barrier(jnp.mean(values * values, axis=-1, keepdims=True)) + EPSILON)
    return (values * inverse * gain.astype(jnp.float32)).astype(jnp.bfloat16)

def split_sum(left, right, groups):
    width = left.shape[1] // groups

    def add_part(index, total):
        piece_left = lax.dynamic_slice_in_dim(left, index * width, width, 1)
        piece_right = lax.dynamic_slice_in_dim(right, index * width, width, 0)
        term = jnp.dot(piece_left, piece_right, preferred_element_type=jnp.float32)
        term = lax.optimization_barrier(term.astype(jnp.bfloat16)).astype(jnp.float32)
        return total + term
    start = jnp.zeros((left.shape[0], right.shape[1]), jnp.float32)
    return lax.fori_loop(0, groups, add_part, start)

def reference(prefill_states, decode_states, attn_gain, w_qkv, w_out, ffn_gain, w_gate_up, w_down, prefill_pool, prefill_pages, prefill_lengths, prefill_home, decode_pool, decode_pages, decode_lengths, decode_home):
    weight = w_qkv.reshape(D, 3 * H * HD)
    normed_pre = rms_norm(prefill_states, attn_gain).reshape(NPRE * STRETCH, D)
    normed_dec = rms_norm(decode_states, attn_gain)
    proj_pre = jnp.dot(normed_pre, weight, preferred_element_type=jnp.float32).astype(jnp.bfloat16).reshape(NPRE, STRETCH, 3, H, HD)
    proj_dec = jnp.dot(normed_dec, weight, preferred_element_type=jnp.float32).astype(jnp.bfloat16).reshape(NDEC, 3, H, HD)
    causal = jnp.arange(STRETCH)[None, :] <= jnp.arange(STRETCH)[:, None]

    def prefill_unit(unit):
        request = unit // H
        head = unit % H
        host = prefill_home[request * HH + head % HH]
        rows = host * PPD + prefill_pages[host]
        pages = jnp.take(prefill_pool, rows, axis=0)
        cache = lax.dynamic_slice_in_dim(pages, head // HH * 2 * HD, 2 * HD, 2).reshape(PCACHE, 2 * HD)
        length = prefill_lengths[request]
        own = lax.dynamic_index_in_dim(proj_pre[request], head, axis=2, keepdims=False)
        query, key_rows, value_rows = (own[:, 0], own[:, 1], own[:, 2])
        score_cache = jnp.dot(query, cache[:, :HD].T, preferred_element_type=jnp.float32) * SCALE
        score_cache = jnp.where(jnp.arange(PCACHE)[None, :] < length, score_cache, MASKED)
        score_stretch = jnp.dot(query, key_rows.T, preferred_element_type=jnp.float32) * SCALE
        score_stretch = jnp.where(causal, score_stretch, MASKED)
        scores = jnp.concatenate([score_cache, score_stretch], axis=1)
        values = jnp.concatenate([cache[:, HD:], value_rows], axis=0)
        top = lax.optimization_barrier(jnp.max(scores, axis=1, keepdims=True))
        weights = jnp.exp(scores - top)
        total = lax.optimization_barrier(jnp.sum(weights, axis=1, keepdims=True))
        mixed = jnp.dot(weights.astype(jnp.bfloat16), values, preferred_element_type=jnp.float32)
        return (mixed / total).astype(jnp.bfloat16)
    units = lax.map(prefill_unit, jnp.arange(NPRE * H, dtype=jnp.int32))
    attn_pre = jnp.transpose(units.reshape(NPRE, H, STRETCH, HD), (0, 2, 1, 3)).reshape(NPRE * STRETCH, H * HD)

    def decode_one(request):
        slot = decode_home[request]
        host = slot // DEC_DEV
        rows = host * DPD + decode_pages[slot]
        cache = jnp.take(decode_pool, rows, axis=0).reshape(DCACHE, H, 2 * HD).astype(jnp.float32)
        length = decode_lengths[slot]
        own = proj_dec[request].astype(jnp.float32)
        scores = jnp.einsum('hd,khd->hk', own[0], cache[:, :, :HD], precision=lax.Precision.HIGHEST) * SCALE
        scores = jnp.where(jnp.arange(DCACHE)[None, :] < length, scores, MASKED)
        own_score = lax.optimization_barrier(jnp.sum(own[0] * own[1], axis=1, keepdims=True)) * SCALE
        top = jnp.maximum(lax.optimization_barrier(jnp.max(scores, axis=1, keepdims=True)), own_score)
        weights = jnp.exp(scores - top)
        own_weight = jnp.exp(own_score - top)
        total = lax.optimization_barrier(jnp.sum(weights, axis=1, keepdims=True)) + own_weight
        mixed = jnp.einsum('hk,khd->hd', weights.astype(jnp.bfloat16).astype(jnp.float32), cache[:, :, HD:], precision=lax.Precision.HIGHEST)
        mixed = mixed + own_weight.astype(jnp.bfloat16).astype(jnp.float32) * own[2]
        return (mixed / total).astype(jnp.bfloat16).reshape(H * HD)
    attn_dec = lax.map(decode_one, jnp.arange(NDEC, dtype=jnp.int32))
    attn = jnp.concatenate([attn_pre, attn_dec], axis=0)
    states = jnp.concatenate([prefill_states.reshape(NPRE * STRETCH, D), decode_states], axis=0).astype(jnp.float32)
    resid = states + split_sum(attn, w_out, N_HEAD)
    normed_mid = rms_norm(resid, ffn_gain)
    gate = jnp.dot(normed_mid, w_gate_up[:, 0], preferred_element_type=jnp.float32)
    upper = jnp.dot(normed_mid, w_gate_up[:, 1], preferred_element_type=jnp.float32)
    hidden = (jax.nn.gelu(gate, approximate=True) * upper).astype(jnp.bfloat16)
    result = (resid + split_sum(hidden, w_down, N_TOK)).astype(jnp.bfloat16)
    prefill_out = result[:NPRE * STRETCH].reshape(NPRE, STRETCH, D)
    decode_out = result[NPRE * STRETCH:]
    return (prefill_out, decode_out)
```

```python
import math

import jax
import jax.numpy as jnp
from jax import lax
from jax.experimental import pallas as pl
from jax.experimental.pallas import tpu as pltpu
from jax.sharding import PartitionSpec as P

HD = 64
EPSILON = 1e-06
SCALE = 0.125
MASKED = -1e30
PAGE = 128
F32 = jnp.float32
BF16 = jnp.bfloat16


def rms_norm(rows, gain):
    values = rows.astype(F32)
    inverse = lax.rsqrt(jnp.mean(values * values, axis=-1, keepdims=True) + EPSILON)
    return (values * inverse * gain).astype(BF16)


def dot_nt(left, right):
    return lax.dot_general(left, right, (((1,), (1,)), ((), ())), preferred_element_type=F32)


QB = 512
KC = 512


def attention_kernel(
    pages,
    length_ref,
    dpages,
    dlens,
    qkv_ref,
    mine_ref,
    pool_ref,
    dpool_hbm,
    out_ref,
    dout_ref,
    keys,
    vals,
    query,
    score,
    top_run,
    top,
    acc,
    dpool,
    dbias,
    dscore,
    count,
    owner,
    dcount,
    sem,
):
    stretch = qkv_ref.shape[0]
    span = pool_ref.shape[0]
    npages = span // PAGE
    dspan = dpool_hbm.shape[0]
    dnpages = dspan // PAGE
    slots, dmax = dpages.shape
    copy = pltpu.make_async_copy(dpool_hbm, dpool, sem)
    copy.start()

    length = length_ref[0]

    def count_page(i, _):
        count[pages[0, i]] = jnp.clip(length - i * PAGE, 0, PAGE)
        return 0

    lax.fori_loop(0, npages, count_page, 0)

    def zero_page(i, _):
        dcount[i] = 0
        owner[i] = 0
        return 0

    lax.fori_loop(0, dnpages, zero_page, 0)
    for s in range(slots):
        used = (dlens[s] + PAGE - 1) // PAGE

        def own_page(i, _):
            page = dpages[s, i]
            owner[page] = s
            dcount[page] = jnp.minimum(dlens[s] - i * PAGE, PAGE)
            return 0

        lax.fori_loop(0, used, own_page, 0)

    lane = lax.broadcasted_iota(jnp.int32, (PAGE, PAGE), 1)
    row = lax.broadcasted_iota(jnp.int32, (PAGE, PAGE), 0)

    def fill_cached(i, _):
        where_at = pl.ds(pl.multiple_of(i * PAGE, PAGE), PAGE)
        page = pool_ref[where_at, :].astype(F32)
        bias = jnp.where((lane == HD) & (row >= count[i]), MASKED, 0.0)
        keys[where_at, :] = jnp.where(lane < HD, page, bias).astype(BF16)
        vals[where_at, :] = jnp.where(lane < HD, 1.0, page).astype(BF16)
        return 0

    lax.fori_loop(0, npages, fill_cached, 0)

    def fill_own(i, _):
        source = pl.ds(pl.multiple_of(i * PAGE, PAGE), PAGE)
        target = pl.ds(pl.multiple_of(span + i * PAGE, PAGE), PAGE)
        left = qkv_ref[source, :PAGE].astype(F32)
        right = qkv_ref[source, PAGE:].astype(F32)
        query[source, :] = jnp.where(
            lane < HD, left * SCALE, jnp.where(lane == HD, 1.0, 0.0)
        ).astype(BF16)
        keys[target, :] = jnp.where(lane < HD, pltpu.roll(left, HD, 1), 0.0).astype(BF16)
        vals[target, :] = jnp.where(lane < HD, 1.0, pltpu.roll(right, HD, 1)).astype(BF16)
        return 0

    lax.fori_loop(0, stretch // PAGE, fill_own, 0)

    def fold(s):
        best = s[:, :PAGE]
        for j in range(1, s.shape[1] // PAGE):
            best = jnp.maximum(best, s[:, j * PAGE : (j + 1) * PAGE])
        return best

    def make_scores(i, c, diagonal):
        rows = query[i * QB : (i + 1) * QB, :]
        s = dot_nt(rows, keys[pl.ds(pl.multiple_of(c * KC, KC), KC), :])
        if diagonal:
            r = lax.broadcasted_iota(jnp.int32, (QB, KC), 0)
            k = lax.broadcasted_iota(jnp.int32, (QB, KC), 1)
            s = jnp.where(k <= r, s, MASKED)
        score[i % 2, c] = s
        top_run[i % 2] = jnp.maximum(top_run[i % 2], fold(s))

    def finish_top(i):
        best = jnp.max(top_run[i % 2], axis=1, keepdims=True)
        top[i % 2] = jnp.broadcast_to(best, (QB, PAGE))

    def mix(i, c):
        best = top[i % 2]
        s = score[i % 2, c]
        p = jnp.exp(s - jnp.concatenate([best] * (KC // PAGE), axis=1)).astype(BF16)
        acc[...] += jnp.dot(
            p, vals[pl.ds(pl.multiple_of(c * KC, KC), KC), :], preferred_element_type=F32
        )

    blocks = stretch // QB
    cached_chunks = span // KC

    top_run[0] = jnp.full((QB, PAGE), MASKED, F32)

    def first(c, _):
        make_scores(0, c, False)
        return 0

    lax.fori_loop(0, cached_chunks, first, 0)
    make_scores(0, cached_chunks, True)
    finish_top(0)
    for i in range(blocks):
        acc[...] = jnp.zeros_like(acc)
        chunks = cached_chunks + i + 1
        if i + 1 < blocks:
            top_run[(i + 1) % 2] = jnp.full((QB, PAGE), MASKED, F32)

            def both(c, _, i=i):
                make_scores(i + 1, c, False)
                mix(i, c)
                return 0

            lax.fori_loop(0, chunks, both, 0)
            make_scores(i + 1, chunks, True)
            finish_top(i + 1)
        else:

            def last(c, _, i=i):
                mix(i, c)
                return 0

            lax.fori_loop(0, chunks, last, 0)
        total = acc[...]
        result = pltpu.roll(total, HD, 1) / total
        out_ref[i * QB : (i + 1) * QB, :] = result[:, :HD].astype(BF16)

    slot_row = lax.broadcasted_iota(jnp.int32, (slots, PAGE), 0)
    slot_lane = lax.broadcasted_iota(jnp.int32, (slots, PAGE), 1)

    def fill_bias(i, _):
        seen = (slot_row == owner[i]) & (slot_lane < dcount[i])
        dbias[i] = jnp.where(seen, 0.0, MASKED)
        return 0

    lax.fori_loop(0, dnpages, fill_bias, 0)
    copy.wait()
    rows = mine_ref[...].astype(F32)
    heads = rows.shape[1] // (3 * HD)
    step = 1024
    per = step // PAGE
    for h in range(heads):
        block = h // 2 * PAGE
        width = heads * HD

        def part(which, left):
            piece = rows[:, which * width + block : which * width + block + PAGE]
            return pltpu.roll(piece, HD, 1) if (h % 2 == 1) == left else piece

        q = jnp.where(slot_lane < HD, part(0, True) * SCALE, 0.0)
        k = part(1, True)
        v = part(2, False)
        own = jnp.sum(q * k, axis=1, keepdims=True)
        qb = q.astype(BF16)
        best = jnp.broadcast_to(own, (slots, PAGE))
        for c in range(dspan // step):
            s = dot_nt(qb, dpool[c * step : (c + 1) * step, h * PAGE : (h + 1) * PAGE])
            s = s + jnp.concatenate([dbias[c * per + j] for j in range(per)], axis=1)
            dscore[c] = s
            best = jnp.maximum(best, fold(s))
        best = jnp.max(best, axis=1, keepdims=True)
        own_weight = jnp.exp(own - best)
        sums = jnp.zeros((slots, PAGE), F32)
        mixed = jnp.zeros((slots, PAGE), F32)
        for c in range(dspan // step):
            p = jnp.exp(dscore[c] - best)
            for j in range(per):
                sums = sums + p[:, j * PAGE : (j + 1) * PAGE]
            mixed = mixed + jnp.dot(
                p.astype(BF16),
                dpool[c * step : (c + 1) * step, h * PAGE : (h + 1) * PAGE],
                preferred_element_type=F32,
            )
        total = jnp.sum(sums, axis=1, keepdims=True) + own_weight
        mixed = (mixed + own_weight.astype(BF16).astype(F32) * v) / total
        dout_ref[:, h * HD : (h + 1) * HD] = pltpu.roll(mixed, HD, 1)[:, :HD].astype(BF16)


def attention(pages, length, dpages, dlens, qkv, mine, pool, dpool):
    stretch = qkv.shape[0]
    span = pool.shape[0]
    dspan, dwidth = dpool.shape
    slots = mine.shape[0]
    keys = span + stretch
    vmem = pl.BlockSpec(memory_space=pltpu.VMEM)
    smem = pl.BlockSpec(memory_space=pltpu.SMEM)
    return pl.pallas_call(
        attention_kernel,
        out_shape=(
            jax.ShapeDtypeStruct((stretch, HD), BF16),
            jax.ShapeDtypeStruct((slots, mine.shape[1] // 3), BF16),
        ),
        in_specs=[smem] * 4 + [vmem] * 3 + [pl.BlockSpec(memory_space=pl.ANY)],
        out_specs=(vmem, vmem),
        scratch_shapes=[
            pltpu.VMEM((keys, 2 * HD), BF16),
            pltpu.VMEM((keys, 2 * HD), BF16),
            pltpu.VMEM((stretch, 2 * HD), BF16),
            pltpu.VMEM((2, keys // KC, QB, KC), F32),
            pltpu.VMEM((2, QB, PAGE), F32),
            pltpu.VMEM((2, QB, PAGE), F32),
            pltpu.VMEM((QB, PAGE), F32),
            pltpu.VMEM((dspan, dwidth), BF16),
            pltpu.VMEM((dspan // PAGE, slots, PAGE), F32),
            pltpu.VMEM((dspan // 1024, slots, 1024), F32),
            pltpu.SMEM((span // PAGE,), jnp.int32),
            pltpu.SMEM((dspan // PAGE,), jnp.int32),
            pltpu.SMEM((dspan // PAGE,), jnp.int32),
            pltpu.SemaphoreType.DMA,
        ],
        compiler_params=pltpu.CompilerParams(vmem_limit_bytes=62 * 1024 * 1024),
        name="attention",
    )(pages, length, dpages, dlens, qkv, mine, pool, dpool)

MESH = pl.DeviceIdType.MESH
Q = 16


def ffn_kernel(
    block_ref,
    drow_ref,
    resid_ref,
    dresid_ref,
    wgu_hbm,
    wdown_hbm,
    out_ref,
    dout_ref,
    wgu,
    wdown,
    x,
    part,
    relay,
    direct,
    first,
    sums,
    relay1,
    direct1,
    xdec,
    xrows,
    pdec,
    rdec,
    wsem,
    ssem,
    rsem,
    dssem,
    drsem,
):
    me = lax.axis_index("tok")
    n_tok = lax.axis_size("tok")
    my_y, my_z = me // 4, me % 4
    barrier = pltpu.get_barrier_semaphore()
    for off in range(1, n_tok):
        pl.semaphore_signal(
            barrier,
            inc=1,
            device_id={"tok": (me + off) % n_tok},
            device_id_type=MESH,
        )
    load_gu = pltpu.make_async_copy(wgu_hbm, wgu, wsem.at[0])
    load_down = pltpu.make_async_copy(wdown_hbm, wdown, wsem.at[1])
    load_own = [
        pltpu.make_async_copy(
            block_ref.at[pl.ds(half * 2, 2)], x.at[half, 0, 0], wsem.at[2 + half]
        )
        for half in range(2)
    ]
    load_dec = pltpu.make_async_copy(drow_ref, xdec.at[0], wsem.at[4])
    for c in load_own:
        c.start()
    load_dec.start()
    load_gu.start()
    load_down.start()

    def along_z(step):
        return {"tok": my_y * 4 + (my_z + step + 4) % 4}

    def along_y(step):
        return {"tok": (my_y + step + 4) % 4 * 4 + my_z}

    axis1 = (along_z, along_y)
    axis2 = (along_y, along_z)
    used = [0]

    def send(source, target, device):
        i = used[0]
        used[0] += 1
        copy = pltpu.make_async_remote_copy(
            src_ref=source,
            dst_ref=target,
            send_sem=ssem.at[i],
            recv_sem=rsem.at[i],
            device_id=device,
            device_id_type=MESH,
        )
        copy.start()
        sent.append(copy)
        return copy

    sent = []
    for c in load_own:
        c.wait()
    load_dec.wait()
    pl.semaphore_wait(barrier, n_tok - 1)

    got = {}
    for half in range(2):
        own = x.at[half, 0, 0]
        got[half, 0, 3] = [send(own, x.at[half, 0, 3], axis1[half](1))]
        got[half, 0, 1] = [send(own, x.at[half, 0, 1], axis1[half](-1))]

    def spread(half, a1):
        own = x.at[half, 0, a1]
        got[half, 3, a1] = [send(own, x.at[half, 3, a1], axis2[half](1))]
        got[half, 1, a1] = [send(own, x.at[half, 1, a1], axis2[half](-1))]

    def relay2(half, a1):
        a = send(x.at[half, 3, a1, 0], x.at[half, 2, a1, 0], axis2[half](1))
        b = send(x.at[half, 1, a1, 1], x.at[half, 2, a1, 1], axis2[half](-1))
        got[half, 2, a1] = [a, b]

    def wait(half, a2, a1):
        for c in got[half, a2, a1]:
            c.wait_recv()

    for half in range(2):
        spread(half, 0)
    dec_copies = []
    for off in range(1, n_tok):
        copy = pltpu.make_async_remote_copy(
            src_ref=xdec.at[0],
            dst_ref=xdec.at[n_tok - off],
            send_sem=dssem.at[off],
            recv_sem=drsem.at[off],
            device_id={"tok": (me + off) % n_tok},
            device_id_type=MESH,
        )
        copy.start()
        dec_copies.append(copy)
    for half in range(2):
        wait(half, 0, 3)
        wait(half, 0, 1)
        a = send(x.at[half, 0, 3, 0], x.at[half, 0, 2, 0], axis1[half](1))
        b = send(x.at[half, 0, 1, 1], x.at[half, 0, 2, 1], axis1[half](-1))
        got[half, 0, 2] = [a, b]
        spread(half, 3)
        spread(half, 1)
    for half in range(2):
        wait(half, 3, 0)
        wait(half, 1, 0)
        relay2(half, 0)
    for half in range(2):
        wait(half, 0, 2)
        spread(half, 2)

    width = wdown.shape[0]

    def hidden_of(rows):
        both = dot_nt(rows, wgu[...])
        gate = both[:, :width]
        return (jax.nn.gelu(gate, approximate=True) * both[:, width:]).astype(BF16)

    def compute(half, a2):
        rows = x[half, a2].reshape(4 * 2 * Q, x.shape[-1])
        result = jnp.dot(hidden_of(rows), wdown[...], preferred_element_type=F32)
        part[half, a2] = result.astype(BF16).reshape(4, 2, Q, x.shape[-1])

    load_gu.wait()
    load_down.wait()

    def group0(i, _):
        compute(i, 0)
        return 0

    lax.fori_loop(0, 2, group0, 0)
    for a1 in (3, 1):
        for half in range(2):
            wait(half, 3, a1)
            wait(half, 1, a1)
            relay2(half, a1)
    for half in range(2):
        wait(half, 3, 2)
        wait(half, 1, 2)
        relay2(half, 2)

    def group13(i, _):
        compute(i % 2, 3 - 2 * (i // 2))
        return 0

    lax.fori_loop(0, 4, group13, 0)
    came = {}
    for half in range(2):
        came[half, 0, 1] = send(
            part.at[half, 1, :, 1], direct.at[half, 0, :, 1], axis2[half](1)
        )
        came[half, 1, 0] = send(
            part.at[half, 3, :, 0], direct.at[half, 1, :, 0], axis2[half](-1)
        )
    for c in dec_copies:
        c.wait_recv()
    for t in range(n_tok):
        xrows[t : t + 1, :] = xdec[t].astype(F32)
    dpart = jnp.dot(
        hidden_of(xrows[...].astype(BF16)), wdown[...], preferred_element_type=F32
    )
    for t in range(n_tok):
        pdec[t] = dpart[t : t + 1, :].astype(BF16)
    dec_back = []
    for off in range(1, n_tok):
        copy = pltpu.make_async_remote_copy(
            src_ref=pdec.at[off],
            dst_ref=rdec.at[n_tok - off],
            send_sem=dssem.at[n_tok + off],
            recv_sem=drsem.at[n_tok + off],
            device_id={"tok": (me + off) % n_tok},
            device_id_type=MESH,
        )
        copy.start()
        dec_back.append(copy)

    hop = {}
    for half in range(2):
        for a1 in range(4):
            wait(half, 2, a1)
        compute(half, 2)
        hop[half, 0] = send(part.at[half, 2, :, 0], relay.at[half, 0], axis2[half](1))
        hop[half, 1] = send(part.at[half, 2, :, 1], relay.at[half, 1], axis2[half](-1))
    for half in range(2):
        hop[half, 0].wait_recv()
        part[half, 1, :, 0] = (
            part[half, 1, :, 0].astype(F32) + relay[half, 0].astype(F32)
        ).astype(BF16)
        came[half, 0, 0] = send(
            part.at[half, 1, :, 0], direct.at[half, 0, :, 0], axis2[half](1)
        )
        hop[half, 1].wait_recv()
        part[half, 3, :, 1] = (
            part[half, 3, :, 1].astype(F32) + relay[half, 1].astype(F32)
        ).astype(BF16)
        came[half, 1, 1] = send(
            part.at[half, 3, :, 1], direct.at[half, 1, :, 1], axis2[half](-1)
        )
    dtotal = dresid_ref[...] + pdec[0].astype(F32)
    for c in dec_back:
        c.wait_recv()
    for off in range(1, n_tok):
        dtotal = dtotal + rdec[off].astype(F32)
    dout_ref[...] = dtotal.astype(BF16)
    hop1 = {}
    came1 = {}
    for half in range(2):
        for side in range(2):
            for q in range(2):
                came[half, side, q].wait_recv()
        for a1 in (2, 1, 3, 0):
            total = (
                part[half, 0, a1].astype(F32)
                + direct[half, 0, a1].astype(F32)
                + direct[half, 1, a1].astype(F32)
            )
            if a1 == 0:
                first[half] = total
            else:
                sums[half, a1] = total.astype(BF16)
            if a1 == 2:
                hop1[half, 0] = send(
                    sums.at[half, 2, 0], relay1.at[half, 0], axis1[half](1)
                )
                hop1[half, 1] = send(
                    sums.at[half, 2, 1], relay1.at[half, 1], axis1[half](-1)
                )
            if a1 == 1:
                came1[half, 0, 1] = send(
                    sums.at[half, 1, 1], direct1.at[half, 0, 1], axis1[half](1)
                )
            if a1 == 3:
                came1[half, 1, 0] = send(
                    sums.at[half, 3, 0], direct1.at[half, 1, 0], axis1[half](-1)
                )
    for half in range(2):
        hop1[half, 0].wait_recv()
        sums[half, 1, 0] = (
            sums[half, 1, 0].astype(F32) + relay1[half, 0].astype(F32)
        ).astype(BF16)
        came1[half, 0, 0] = send(
            sums.at[half, 1, 0], direct1.at[half, 0, 0], axis1[half](1)
        )
        hop1[half, 1].wait_recv()
        sums[half, 3, 1] = (
            sums[half, 3, 1].astype(F32) + relay1[half, 1].astype(F32)
        ).astype(BF16)
        came1[half, 1, 1] = send(
            sums.at[half, 3, 1], direct1.at[half, 1, 1], axis1[half](-1)
        )
    for half in range(2):
        for side in range(2):
            for q in range(2):
                came1[half, side, q].wait_recv()
        out_ref[half * 2 : half * 2 + 2] = (
            resid_ref[half * 2 : half * 2 + 2]
            + first[half]
            + direct1[half, 0].astype(F32)
            + direct1[half, 1].astype(F32)
        ).astype(BF16)
    for c in sent + dec_copies + dec_back:
        c.wait_send()


FFN_SENDS = 2 * (2 + 2 + 8 + 8 + 6 + 6)


def ffn(block, drow, resid, dresid, wgu, wdown, n_tok):
    width = block.shape[-1]
    vmem = pl.BlockSpec(memory_space=pltpu.VMEM)
    hbm = pl.BlockSpec(memory_space=pl.ANY)
    return pl.pallas_call(
        ffn_kernel,
        out_shape=(
            jax.ShapeDtypeStruct(block.shape, BF16),
            jax.ShapeDtypeStruct(drow.shape, BF16),
        ),
        in_specs=[vmem, vmem, vmem, vmem, hbm, hbm],
        out_specs=(vmem, vmem),
        scratch_shapes=[
            pltpu.VMEM(wgu.shape, BF16),
            pltpu.VMEM(wdown.shape, BF16),
            pltpu.VMEM((2, 4, 4, 2, Q, width), BF16),
            pltpu.VMEM((2, 4, 4, 2, Q, width), BF16),
            pltpu.VMEM((2, 2, 4, Q, width), BF16),
            pltpu.VMEM((2, 2, 4, 2, Q, width), BF16),
            pltpu.VMEM((2, 2, Q, width), F32),
            pltpu.VMEM((2, 4, 2, Q, width), BF16),
            pltpu.VMEM((2, 2, Q, width), BF16),
            pltpu.VMEM((2, 2, 2, Q, width), BF16),
            pltpu.VMEM((n_tok, 1, width), BF16),
            pltpu.VMEM((n_tok, width), F32),
            pltpu.VMEM((n_tok, 1, width), BF16),
            pltpu.VMEM((n_tok, 1, width), BF16),
            pltpu.SemaphoreType.DMA((5,)),
            pltpu.SemaphoreType.DMA((FFN_SENDS,)),
            pltpu.SemaphoreType.DMA((FFN_SENDS,)),
            pltpu.SemaphoreType.DMA((2 * n_tok,)),
            pltpu.SemaphoreType.DMA((2 * n_tok,)),
        ],
        compiler_params=pltpu.CompilerParams(
            collective_id=1, has_side_effects=True, vmem_limit_bytes=56 * 1024 * 1024
        ),
        name="ffn",
    )(block, drow, resid, dresid, wgu, wdown)


def shards(
    prefill_states,
    decode_states,
    attn_gain,
    w_qkv,
    w_out,
    ffn_gain,
    w_gate_up,
    w_down,
    prefill_pool,
    prefill_pages,
    prefill_lengths,
    prefill_home,
    decode_pool,
    decode_pages,
    decode_lengths,
    decode_home,
):
    n_tok = lax.axis_size("tok")
    n_head = lax.axis_size("head")
    my_tok = lax.axis_index("tok")
    my_head = lax.axis_index("head")
    requests, positions, width = prefill_states.shape
    hosted = decode_states.shape[0]
    heads_per = w_qkv.shape[2] // HD
    stretch = positions * n_tok
    units = requests * heads_per
    features = heads_per * HD
    normed_pre = rms_norm(prefill_states, attn_gain).reshape(requests * positions, width)
    normed_dec = rms_norm(decode_states, attn_gain)
    normed = jnp.concatenate([normed_pre, normed_dec], axis=0)
    projected = jnp.dot(
        normed, w_qkv.reshape(width, 3 * features), preferred_element_type=jnp.float32
    ).astype(jnp.bfloat16)
    proj_pre = projected[: requests * positions].reshape(requests, positions, 3, heads_per, HD)
    proj_dec = projected[requests * positions :]
    unit_ids = jnp.arange(units, dtype=jnp.int32)
    host_ids = jnp.arange(n_tok, dtype=jnp.int32)
    hosted_unit = jnp.sum(
        jnp.where(prefill_home[None, :] == host_ids[:, None], unit_ids[None, :], 0), axis=1
    )
    by_unit = jnp.transpose(proj_pre, (0, 3, 1, 2, 4)).reshape(units, positions * 3 * HD)
    outgoing = jnp.take(by_unit, hosted_unit, axis=0)
    pre_cols = positions * 3 * HD
    spread = jnp.broadcast_to(
        proj_dec.reshape(1, hosted * 3 * features), (n_tok, hosted * 3 * features)
    )
    outgoing = jnp.concatenate([outgoing, spread], axis=1)
    arrived = lax.all_to_all(outgoing, "tok", split_axis=0, concat_axis=0, tiled=True)
    arrived_dec = arrived[:, pre_cols:].reshape(n_tok * hosted, 3, heads_per, HD)
    arrived_pre = arrived[:, :pre_cols].reshape(stretch, 3, HD)
    my_unit = hosted_unit[my_tok]
    length = prefill_lengths[my_unit // heads_per]
    slots = my_tok * hosted + jnp.arange(hosted, dtype=jnp.int32)
    all_requests = jnp.arange(decode_home.shape[0], dtype=jnp.int32)
    anchor = jnp.sum(
        jnp.where(decode_home[None, :] == slots[:, None], all_requests[None, :], 0), axis=1
    )
    mine = jnp.take(arrived_dec, anchor, axis=0).reshape(hosted, 3 * features)
    qkv = jnp.pad(arrived_pre.reshape(stretch, 3 * HD), ((0, 0), (0, HD)))
    attn_unit, decode_attn = attention(
        prefill_pages,
        length.reshape(1),
        decode_pages,
        decode_lengths,
        qkv,
        mine,
        prefill_pool.reshape(-1, 2 * HD),
        decode_pool.reshape(-1, decode_pool.shape[2]),
    )
    backward = attn_unit.reshape(n_tok, positions * HD)
    back_cols = positions * HD
    spread_back = jnp.broadcast_to(
        decode_attn.reshape(1, hosted * features), (n_tok, hosted * features)
    )
    backward = jnp.concatenate([backward, spread_back], axis=1)
    returned = lax.all_to_all(backward, "tok", split_axis=0, concat_axis=0, tiled=True)
    by_slot = returned[:, back_cols:].reshape(n_tok * hosted, features)
    my_slots = lax.dynamic_slice_in_dim(decode_home, my_tok * hosted, hosted, 0)
    attn_dec = jnp.take(by_slot, my_slots, axis=0)
    attn_pre = jnp.take(returned[:, :back_cols], prefill_home, axis=0).reshape(
        requests, heads_per, positions, HD
    )
    block_rows = positions // n_head
    decode_share = hosted // n_head
    per = requests * block_rows + decode_share
    pre_rows = jnp.transpose(attn_pre, (0, 2, 1, 3)).reshape(requests, n_head, block_rows, features)
    pre_rows = jnp.transpose(pre_rows, (1, 0, 2, 3)).reshape(
        n_head, requests * block_rows, features
    )
    dec_rows = attn_dec.reshape(n_head, decode_share, features)
    ordered = jnp.concatenate([pre_rows, dec_rows], axis=1).reshape(n_head * per, features)
    mixed_rows = lax.psum_scatter(
        jnp.dot(ordered, w_out, preferred_element_type=jnp.float32).astype(jnp.bfloat16),
        "head",
        scatter_dimension=0,
        tiled=True,
    ).astype(jnp.float32)
    own_pre = lax.dynamic_slice_in_dim(prefill_states, my_head * block_rows, block_rows, 1).reshape(
        requests * block_rows, width
    )
    own_dec = lax.dynamic_slice_in_dim(decode_states, my_head * decode_share, decode_share, 0)
    resid = jnp.concatenate([own_pre, own_dec], axis=0).astype(jnp.float32) + mixed_rows
    normed_mid = rms_norm(resid, ffn_gain)
    rows = requests * block_rows
    prefill_out, decode_out = ffn(
        normed_mid[:rows].reshape(-1, Q, width),
        normed_mid[rows:],
        resid[:rows].reshape(-1, Q, width),
        resid[rows:],
        jnp.transpose(w_gate_up, (1, 2, 0)).reshape(-1, width),
        w_down,
        n_tok,
    )
    return (prefill_out, decode_out)


def solution(mesh):
    placed = (
        P(None, "tok", None),
        P("tok", None),
        P(),
        P(None, None, "head"),
        P("head", None),
        P(),
        P(None, None, "tok"),
        P("tok", None),
        P("tok", None, "head"),
        P("tok", None),
        P(),
        P(),
        P("tok", None, "head"),
        P("tok", None),
        P("tok"),
        P(),
    )
    return jax.shard_map(
        shards,
        mesh=mesh,
        in_specs=placed,
        out_specs=(P(None, ("tok", "head"), None), P(("tok", "head"), None)),
        check_vma=False,
    )
```

```python
import jax
import jax.numpy as jnp
from jax import lax
from jax.experimental import pallas as pl
from jax.experimental.pallas import tpu as pltpu
from jax.sharding import PartitionSpec as P

HD = 64
EPSILON = 1e-06
SCALE = 0.125
MASKED = -1e30
PAGE = 128
F32 = jnp.float32
BF16 = jnp.bfloat16


def rms_norm(rows, gain):
    values = rows.astype(F32)
    inverse = lax.rsqrt(jnp.mean(values * values, axis=-1, keepdims=True) + EPSILON)
    return (values * inverse * gain).astype(BF16)


def dot_nt(left, right):
    return lax.dot_general(left, right, (((1,), (1,)), ((), ())), preferred_element_type=F32)


QB = 512
KC = 512


def attention_kernel(
    pages,
    lengths,
    homes,
    dpages,
    dlens,
    dhomes,
    arrived,
    arrived_dec,
    pool_ref,
    dpool_hbm,
    out_ref,
    dout_ref,
    keys,
    vals,
    query,
    score,
    top_run,
    top,
    acc,
    dpool,
    dbias,
    dscore,
    drows,
    mine_ref,
    count,
    owner,
    dcount,
    anchor,
    sem,
):
    me = lax.axis_index("tok")
    n_tok = arrived.shape[0]
    positions = arrived.shape[1] // 3 * 2
    stretch = n_tok * positions
    span = pool_ref.shape[0]
    npages = span // PAGE
    dspan = dpool_hbm.shape[0]
    dnpages = dspan // PAGE
    slots, dmax = dpages.shape
    copy = pltpu.make_async_copy(dpool_hbm, dpool, sem)
    copy.start()

    my_unit = jnp.int32(0)
    for u in range(n_tok):
        my_unit = jnp.where(homes[u] == me, u, my_unit)
    length = lengths[my_unit // (n_tok // lengths.shape[0])]

    def count_page(i, _):
        count[pages[0, i]] = jnp.clip(length - i * PAGE, 0, PAGE)
        return 0

    lax.fori_loop(0, npages, count_page, 0)

    def zero_page(i, _):
        dcount[i] = 0
        owner[i] = 0
        return 0

    lax.fori_loop(0, dnpages, zero_page, 0)
    for s in range(slots):
        used = (dlens[s] + PAGE - 1) // PAGE

        def own_page(i, _):
            page = dpages[s, i]
            owner[page] = s
            dcount[page] = jnp.minimum(dlens[s] - i * PAGE, PAGE)
            return 0

        lax.fori_loop(0, used, own_page, 0)

    lane = lax.broadcasted_iota(jnp.int32, (PAGE, PAGE), 1)
    row = lax.broadcasted_iota(jnp.int32, (PAGE, PAGE), 0)

    def fill_cached(i, _):
        where_at = pl.ds(pl.multiple_of(i * PAGE, PAGE), PAGE)
        page = pool_ref[where_at, :].astype(F32)
        bias = jnp.where((lane == HD) & (row >= count[i]), MASKED, 0.0)
        keys[where_at, :] = jnp.where(lane < HD, page, bias).astype(BF16)
        vals[where_at, :] = jnp.where(lane < HD, 1.0, page).astype(BF16)
        return 0

    lax.fori_loop(0, npages, fill_cached, 0)

    half = PAGE // 2

    def fill_own(i, _):
        target = pl.ds(pl.multiple_of(span + i * PAGE, PAGE), PAGE)
        both = arrived[i, :PAGE, :].astype(F32)
        keys[target, :] = jnp.where(lane < HD, both, 0.0).astype(BF16)
        vals[target, :] = jnp.where(lane < HD, 1.0, both).astype(BF16)
        packed = arrived[i, PAGE:, :].astype(F32) * SCALE
        flag = jnp.where(lane[:half] == HD, 1.0, 0.0)
        low = jnp.where(lane[:half] < HD, packed, flag)
        high = jnp.where(lane[:half] < HD, pltpu.roll(packed, HD, 1), flag)
        at_low = pl.ds(pl.multiple_of(i * PAGE, PAGE), half)
        at_high = pl.ds(pl.multiple_of(i * PAGE + half, half), half)
        query[at_low, :] = low.astype(BF16)
        query[at_high, :] = high.astype(BF16)
        return 0

    lax.fori_loop(0, stretch // PAGE, fill_own, 0)

    def fold(s):
        best = s[:, :PAGE]
        for j in range(1, s.shape[1] // PAGE):
            best = jnp.maximum(best, s[:, j * PAGE : (j + 1) * PAGE])
        return best

    def make_scores(i, c, diagonal):
        rows = query[i * QB : (i + 1) * QB, :]
        s = dot_nt(rows, keys[pl.ds(pl.multiple_of(c * KC, KC), KC), :])
        if diagonal:
            r = lax.broadcasted_iota(jnp.int32, (QB, KC), 0)
            k = lax.broadcasted_iota(jnp.int32, (QB, KC), 1)
            s = jnp.where(k <= r, s, MASKED)
        score[i % 2, c] = s
        top_run[i % 2] = jnp.maximum(top_run[i % 2], fold(s))

    def finish_top(i):
        best = jnp.max(top_run[i % 2], axis=1, keepdims=True)
        top[i % 2] = jnp.broadcast_to(best, (QB, PAGE))

    def mix(i, c):
        best = top[i % 2]
        s = score[i % 2, c]
        p = jnp.exp(s - jnp.concatenate([best] * (KC // PAGE), axis=1)).astype(BF16)
        acc[...] += jnp.dot(
            p, vals[pl.ds(pl.multiple_of(c * KC, KC), KC), :], preferred_element_type=F32
        )

    blocks = stretch // QB
    cached_chunks = span // KC

    top_run[0] = jnp.full((QB, PAGE), MASKED, F32)

    def first(c, _):
        make_scores(0, c, False)
        return 0

    lax.fori_loop(0, cached_chunks, first, 0)
    make_scores(0, cached_chunks, True)
    finish_top(0)
    for i in range(blocks):
        acc[...] = jnp.zeros_like(acc)
        chunks = cached_chunks + i + 1
        if i + 1 < blocks:
            top_run[(i + 1) % 2] = jnp.full((QB, PAGE), MASKED, F32)

            def both(c, _, i=i):
                make_scores(i + 1, c, False)
                mix(i, c)
                return 0

            lax.fori_loop(0, chunks, both, 0)
            make_scores(i + 1, chunks, True)
            finish_top(i + 1)
        else:

            def last(c, _, i=i):
                mix(i, c)
                return 0

            lax.fori_loop(0, chunks, last, 0)
        total = acc[...]
        result = pltpu.roll(total, HD, 1) / total
        for j in range(QB // PAGE):
            tile = result[j * PAGE : (j + 1) * PAGE]
            out_ref[i * (QB // PAGE) + j] = jnp.where(
                lane[:half] < HD, tile[:half], pltpu.roll(tile[half:], HD, 1)
            ).astype(BF16)

    slot_row = lax.broadcasted_iota(jnp.int32, (slots, PAGE), 0)
    slot_lane = lax.broadcasted_iota(jnp.int32, (slots, PAGE), 1)

    def fill_bias(i, _):
        seen = (slot_row == owner[i]) & (slot_lane < dcount[i])
        dbias[i] = jnp.where(seen, 0.0, MASKED)
        return 0

    lax.fori_loop(0, dnpages, fill_bias, 0)
    for t in range(n_tok):
        drows[t * slots : (t + 1) * slots, :] = arrived_dec[t].astype(F32)

    def find(r, _):
        slot = dhomes[r] - me * slots

        @pl.when((slot >= 0) & (slot < slots))
        def _():
            anchor[slot] = r

        return 0

    lax.fori_loop(0, dhomes.shape[0], find, 0)
    for s in range(slots):
        mine_ref[s : s + 1, :] = drows[pl.ds(anchor[s], 1), :]
    copy.wait()
    rows = mine_ref[...]
    heads = rows.shape[1] // (3 * HD)
    step = 1024
    per = step // PAGE
    for h in range(heads):
        block = h // 2 * PAGE
        width = heads * HD

        def part(which, left):
            piece = rows[:, which * width + block : which * width + block + PAGE]
            return pltpu.roll(piece, HD, 1) if (h % 2 == 1) == left else piece

        q = jnp.where(slot_lane < HD, part(0, True) * SCALE, 0.0)
        k = part(1, True)
        v = part(2, False)
        own = jnp.sum(q * k, axis=1, keepdims=True)
        qb = q.astype(BF16)
        best = jnp.broadcast_to(own, (slots, PAGE))
        for c in range(dspan // step):
            s = dot_nt(qb, dpool[c * step : (c + 1) * step, h * PAGE : (h + 1) * PAGE])
            s = s + jnp.concatenate([dbias[c * per + j] for j in range(per)], axis=1)
            dscore[c] = s
            best = jnp.maximum(best, fold(s))
        best = jnp.max(best, axis=1, keepdims=True)
        own_weight = jnp.exp(own - best)
        sums = jnp.zeros((slots, PAGE), F32)
        mixed = jnp.zeros((slots, PAGE), F32)
        for c in range(dspan // step):
            p = jnp.exp(dscore[c] - best)
            for j in range(per):
                sums = sums + p[:, j * PAGE : (j + 1) * PAGE]
            mixed = mixed + jnp.dot(
                p.astype(BF16),
                dpool[c * step : (c + 1) * step, h * PAGE : (h + 1) * PAGE],
                preferred_element_type=F32,
            )
        total = jnp.sum(sums, axis=1, keepdims=True) + own_weight
        mixed = (mixed + own_weight.astype(BF16).astype(F32) * v) / total
        dout_ref[:, h * HD : (h + 1) * HD] = pltpu.roll(mixed, HD, 1)[:, :HD].astype(BF16)


def attention(
    pages, lengths, homes, dpages, dlens, dhomes, arrived, arrived_dec, pool, dpool
):
    n_tok, packed, lanes = arrived.shape
    positions = packed // 3 * 2
    stretch = n_tok * positions
    span = pool.shape[0]
    dspan, dwidth = dpool.shape
    slots, dcols = arrived_dec.shape[1:]
    keys = span + stretch
    vmem = pl.BlockSpec(memory_space=pltpu.VMEM)
    smem = pl.BlockSpec(memory_space=pltpu.SMEM)
    return pl.pallas_call(
        attention_kernel,
        out_shape=(
            jax.ShapeDtypeStruct((n_tok, positions // 2, lanes), BF16),
            jax.ShapeDtypeStruct((slots, dcols // 3), BF16),
        ),
        in_specs=[smem] * 6 + [vmem] * 3 + [pl.BlockSpec(memory_space=pl.ANY)],
        out_specs=(vmem, vmem),
        scratch_shapes=[
            pltpu.VMEM((keys, 2 * HD), BF16),
            pltpu.VMEM((keys, 2 * HD), BF16),
            pltpu.VMEM((stretch, 2 * HD), BF16),
            pltpu.VMEM((2, keys // KC, QB, KC), F32),
            pltpu.VMEM((2, QB, PAGE), F32),
            pltpu.VMEM((2, QB, PAGE), F32),
            pltpu.VMEM((QB, PAGE), F32),
            pltpu.VMEM((dspan, dwidth), BF16),
            pltpu.VMEM((dspan // PAGE, slots, PAGE), F32),
            pltpu.VMEM((dspan // 1024, slots, 1024), F32),
            pltpu.VMEM((n_tok * slots, dcols), F32),
            pltpu.VMEM((slots, dcols), F32),
            pltpu.SMEM((span // PAGE,), jnp.int32),
            pltpu.SMEM((dspan // PAGE,), jnp.int32),
            pltpu.SMEM((dspan // PAGE,), jnp.int32),
            pltpu.SMEM((slots,), jnp.int32),
            pltpu.SemaphoreType.DMA,
        ],
        compiler_params=pltpu.CompilerParams(vmem_limit_bytes=62 * 1024 * 1024),
        name="attention",
    )(pages, lengths, homes, dpages, dlens, dhomes, arrived, arrived_dec, pool, dpool)


MESH = pl.DeviceIdType.MESH
Q = 16


def ffn_kernel(
    block_ref,
    drow_ref,
    resid_ref,
    dresid_ref,
    wgu_hbm,
    wdown_hbm,
    out_ref,
    dout_ref,
    wgu,
    wdown,
    x,
    part,
    relay,
    direct,
    first,
    sums,
    relay1,
    direct1,
    xdec,
    xrows,
    pdec,
    rdec,
    wsem,
    ssem,
    rsem,
    dssem,
    drsem,
):
    me = lax.axis_index("tok")
    n_tok = lax.axis_size("tok")
    my_y, my_z = me // 4, me % 4
    barrier = pltpu.get_barrier_semaphore()
    for off in range(1, n_tok):
        pl.semaphore_signal(
            barrier,
            inc=1,
            device_id={"tok": (me + off) % n_tok},
            device_id_type=MESH,
        )
    load_gu = pltpu.make_async_copy(wgu_hbm, wgu, wsem.at[0])
    load_down = pltpu.make_async_copy(wdown_hbm, wdown, wsem.at[1])
    load_own = [
        pltpu.make_async_copy(
            block_ref.at[pl.ds(half * 2, 2)], x.at[half, 0, 0], wsem.at[2 + half]
        )
        for half in range(2)
    ]
    load_dec = pltpu.make_async_copy(drow_ref, xdec.at[0], wsem.at[4])
    for c in load_own:
        c.start()
    load_dec.start()
    load_gu.start()
    load_down.start()

    def along_z(step):
        return {"tok": my_y * 4 + (my_z + step + 4) % 4}

    def along_y(step):
        return {"tok": (my_y + step + 4) % 4 * 4 + my_z}

    axis1 = (along_z, along_y)
    axis2 = (along_y, along_z)
    used = [0]

    def send(source, target, device):
        i = used[0]
        used[0] += 1
        copy = pltpu.make_async_remote_copy(
            src_ref=source,
            dst_ref=target,
            send_sem=ssem.at[i],
            recv_sem=rsem.at[i],
            device_id=device,
            device_id_type=MESH,
        )
        copy.start()
        sent.append(copy)
        return copy

    sent = []
    for c in load_own:
        c.wait()
    load_dec.wait()
    pl.semaphore_wait(barrier, n_tok - 1)

    got = {}
    for half in range(2):
        own = x.at[half, 0, 0]
        got[half, 0, 3] = [send(own, x.at[half, 0, 3], axis1[half](1))]
        got[half, 0, 1] = [send(own, x.at[half, 0, 1], axis1[half](-1))]

    def spread(half, a1):
        own = x.at[half, 0, a1]
        got[half, 3, a1] = [send(own, x.at[half, 3, a1], axis2[half](1))]
        got[half, 1, a1] = [send(own, x.at[half, 1, a1], axis2[half](-1))]

    def relay2(half, a1):
        a = send(x.at[half, 3, a1, 0], x.at[half, 2, a1, 0], axis2[half](1))
        b = send(x.at[half, 1, a1, 1], x.at[half, 2, a1, 1], axis2[half](-1))
        got[half, 2, a1] = [a, b]

    def wait(half, a2, a1):
        for c in got[half, a2, a1]:
            c.wait_recv()

    for half in range(2):
        spread(half, 0)
    dec_copies = []
    for off in range(1, n_tok):
        copy = pltpu.make_async_remote_copy(
            src_ref=xdec.at[0],
            dst_ref=xdec.at[n_tok - off],
            send_sem=dssem.at[off],
            recv_sem=drsem.at[off],
            device_id={"tok": (me + off) % n_tok},
            device_id_type=MESH,
        )
        copy.start()
        dec_copies.append(copy)
    for half in range(2):
        wait(half, 0, 3)
        wait(half, 0, 1)
        a = send(x.at[half, 0, 3, 0], x.at[half, 0, 2, 0], axis1[half](1))
        b = send(x.at[half, 0, 1, 1], x.at[half, 0, 2, 1], axis1[half](-1))
        got[half, 0, 2] = [a, b]
        spread(half, 3)
        spread(half, 1)
    for half in range(2):
        wait(half, 3, 0)
        wait(half, 1, 0)
        relay2(half, 0)
    for half in range(2):
        wait(half, 0, 2)
        spread(half, 2)

    width = wdown.shape[0]

    def hidden_of(rows):
        both = dot_nt(rows, wgu[...])
        gate = both[:, :width]
        return (jax.nn.gelu(gate, approximate=True) * both[:, width:]).astype(BF16)

    def compute(half, a2):
        rows = x[half, a2].reshape(4 * 2 * Q, x.shape[-1])
        result = jnp.dot(hidden_of(rows), wdown[...], preferred_element_type=F32)
        part[half, a2] = result.astype(BF16).reshape(4, 2, Q, x.shape[-1])

    load_gu.wait()
    load_down.wait()

    def group0(i, _):
        compute(i, 0)
        return 0

    lax.fori_loop(0, 2, group0, 0)
    for a1 in (3, 1):
        for half in range(2):
            wait(half, 3, a1)
            wait(half, 1, a1)
            relay2(half, a1)
    for half in range(2):
        wait(half, 3, 2)
        wait(half, 1, 2)
        relay2(half, 2)

    def group13(i, _):
        compute(i % 2, 3 - 2 * (i // 2))
        return 0

    lax.fori_loop(0, 4, group13, 0)
    came = {}
    for half in range(2):
        came[half, 0, 1] = send(
            part.at[half, 1, :, 1], direct.at[half, 0, :, 1], axis2[half](1)
        )
        came[half, 1, 0] = send(
            part.at[half, 3, :, 0], direct.at[half, 1, :, 0], axis2[half](-1)
        )
    for c in dec_copies:
        c.wait_recv()
    for t in range(n_tok):
        xrows[t : t + 1, :] = xdec[t].astype(F32)
    dpart = jnp.dot(
        hidden_of(xrows[...].astype(BF16)), wdown[...], preferred_element_type=F32
    )
    for t in range(n_tok):
        pdec[t] = dpart[t : t + 1, :].astype(BF16)
    dec_back = []
    for off in range(1, n_tok):
        copy = pltpu.make_async_remote_copy(
            src_ref=pdec.at[off],
            dst_ref=rdec.at[n_tok - off],
            send_sem=dssem.at[n_tok + off],
            recv_sem=drsem.at[n_tok + off],
            device_id={"tok": (me + off) % n_tok},
            device_id_type=MESH,
        )
        copy.start()
        dec_back.append(copy)

    hop = {}
    for half in range(2):
        for a1 in range(4):
            wait(half, 2, a1)
        compute(half, 2)
        hop[half, 0] = send(part.at[half, 2, :, 0], relay.at[half, 0], axis2[half](1))
        hop[half, 1] = send(part.at[half, 2, :, 1], relay.at[half, 1], axis2[half](-1))
    for half in range(2):
        hop[half, 0].wait_recv()
        part[half, 1, :, 0] = (
            part[half, 1, :, 0].astype(F32) + relay[half, 0].astype(F32)
        ).astype(BF16)
        came[half, 0, 0] = send(
            part.at[half, 1, :, 0], direct.at[half, 0, :, 0], axis2[half](1)
        )
        hop[half, 1].wait_recv()
        part[half, 3, :, 1] = (
            part[half, 3, :, 1].astype(F32) + relay[half, 1].astype(F32)
        ).astype(BF16)
        came[half, 1, 1] = send(
            part.at[half, 3, :, 1], direct.at[half, 1, :, 1], axis2[half](-1)
        )
    dtotal = dresid_ref[...] + pdec[0].astype(F32)
    for c in dec_back:
        c.wait_recv()
    for off in range(1, n_tok):
        dtotal = dtotal + rdec[off].astype(F32)
    dout_ref[...] = dtotal.astype(BF16)
    hop1 = {}
    came1 = {}
    for half in range(2):
        for side in range(2):
            for q in range(2):
                came[half, side, q].wait_recv()
        for a1 in (2, 1, 3, 0):
            total = (
                part[half, 0, a1].astype(F32)
                + direct[half, 0, a1].astype(F32)
                + direct[half, 1, a1].astype(F32)
            )
            if a1 == 0:
                first[half] = total
            else:
                sums[half, a1] = total.astype(BF16)
            if a1 == 2:
                hop1[half, 0] = send(
                    sums.at[half, 2, 0], relay1.at[half, 0], axis1[half](1)
                )
                hop1[half, 1] = send(
                    sums.at[half, 2, 1], relay1.at[half, 1], axis1[half](-1)
                )
            if a1 == 1:
                came1[half, 0, 1] = send(
                    sums.at[half, 1, 1], direct1.at[half, 0, 1], axis1[half](1)
                )
            if a1 == 3:
                came1[half, 1, 0] = send(
                    sums.at[half, 3, 0], direct1.at[half, 1, 0], axis1[half](-1)
                )
    for half in range(2):
        hop1[half, 0].wait_recv()
        sums[half, 1, 0] = (
            sums[half, 1, 0].astype(F32) + relay1[half, 0].astype(F32)
        ).astype(BF16)
        came1[half, 0, 0] = send(
            sums.at[half, 1, 0], direct1.at[half, 0, 0], axis1[half](1)
        )
        hop1[half, 1].wait_recv()
        sums[half, 3, 1] = (
            sums[half, 3, 1].astype(F32) + relay1[half, 1].astype(F32)
        ).astype(BF16)
        came1[half, 1, 1] = send(
            sums.at[half, 3, 1], direct1.at[half, 1, 1], axis1[half](-1)
        )
    for half in range(2):
        for side in range(2):
            for q in range(2):
                came1[half, side, q].wait_recv()
        out_ref[half * 2 : half * 2 + 2] = (
            resid_ref[half * 2 : half * 2 + 2]
            + first[half]
            + direct1[half, 0].astype(F32)
            + direct1[half, 1].astype(F32)
        ).astype(BF16)
    for c in sent + dec_copies + dec_back:
        c.wait_send()


FFN_SENDS = 2 * (2 + 2 + 8 + 8 + 6 + 6)


def ffn(block, drow, resid, dresid, wgu, wdown, n_tok):
    width = block.shape[-1]
    vmem = pl.BlockSpec(memory_space=pltpu.VMEM)
    hbm = pl.BlockSpec(memory_space=pl.ANY)
    return pl.pallas_call(
        ffn_kernel,
        out_shape=(
            jax.ShapeDtypeStruct(block.shape, BF16),
            jax.ShapeDtypeStruct(drow.shape, BF16),
        ),
        in_specs=[vmem, vmem, vmem, vmem, hbm, hbm],
        out_specs=(vmem, vmem),
        scratch_shapes=[
            pltpu.VMEM(wgu.shape, BF16),
            pltpu.VMEM(wdown.shape, BF16),
            pltpu.VMEM((2, 4, 4, 2, Q, width), BF16),
            pltpu.VMEM((2, 4, 4, 2, Q, width), BF16),
            pltpu.VMEM((2, 2, 4, Q, width), BF16),
            pltpu.VMEM((2, 2, 4, 2, Q, width), BF16),
            pltpu.VMEM((2, 2, Q, width), F32),
            pltpu.VMEM((2, 4, 2, Q, width), BF16),
            pltpu.VMEM((2, 2, Q, width), BF16),
            pltpu.VMEM((2, 2, 2, Q, width), BF16),
            pltpu.VMEM((n_tok, 1, width), BF16),
            pltpu.VMEM((n_tok, width), F32),
            pltpu.VMEM((n_tok, 1, width), BF16),
            pltpu.VMEM((n_tok, 1, width), BF16),
            pltpu.SemaphoreType.DMA((5,)),
            pltpu.SemaphoreType.DMA((FFN_SENDS,)),
            pltpu.SemaphoreType.DMA((FFN_SENDS,)),
            pltpu.SemaphoreType.DMA((2 * n_tok,)),
            pltpu.SemaphoreType.DMA((2 * n_tok,)),
        ],
        compiler_params=pltpu.CompilerParams(
            collective_id=1, has_side_effects=True, vmem_limit_bytes=56 * 1024 * 1024
        ),
        name="ffn",
    )(block, drow, resid, dresid, wgu, wdown)


def project_kernel(
    states,
    dstates,
    gain_ref,
    w_hbm,
    homes,
    out_ref,
    dec_ref,
    w,
    normed,
    units,
    outgoing,
    pdec,
    wsem,
    lsem,
    ssem,
    rsem,
    dssem,
    drsem,
):
    me = lax.axis_index("tok")
    n_tok = lax.axis_size("tok")
    requests, positions, width = states.shape
    features = w.shape[2]
    per = features // HD
    barrier = pltpu.get_barrier_semaphore()
    for off in range(1, n_tok):
        pl.semaphore_signal(
            barrier, inc=1, device_id={"tok": (me + off) % n_tok}, device_id_type=MESH
        )
    load = pltpu.make_async_copy(w_hbm, w, wsem)
    load.start()
    gain = gain_ref[...]
    pdec_rows = rms_norm(dstates[...], gain)
    lane = lax.broadcasted_iota(jnp.int32, (positions, PAGE), 1)
    half = positions // 2

    strip = 64

    def norm(i, _):
        at = pl.ds(pl.multiple_of(i % (positions // strip) * strip, strip), strip)
        normed[i] = rms_norm(states[i // (positions // strip), at, :], gain)
        return 0

    lax.fori_loop(0, requests * positions // strip, norm, 0)
    load.wait()
    pl.semaphore_wait(barrier, n_tok - 1)
    for which in range(3):
        pdec[:, which * features : (which + 1) * features] = jnp.dot(
            pdec_rows, w[which], preferred_element_type=F32
        ).astype(BF16)
    copies = []
    for off in range(1, n_tok):
        copy = pltpu.make_async_remote_copy(
            src_ref=pdec,
            dst_ref=dec_ref.at[me],
            send_sem=dssem.at[off],
            recv_sem=drsem.at[off],
            device_id={"tok": (me + off) % n_tok},
            device_id_type=MESH,
        )
        copy.start()
        copies.append(copy)

    def project(r, _):
        rows = normed[pl.ds(r * (positions // strip), positions // strip)].reshape(
            positions, width
        )
        q, k, v = (jnp.dot(rows, w[i], preferred_element_type=F32) for i in range(3))
        for j in range(per):
            at = j // 2 * PAGE
            qb, kb, vb = (a[:, at : at + PAGE] for a in (q, k, v))
            if j % 2 == 0:
                both = jnp.where(lane < HD, kb, pltpu.roll(vb, HD, 1))
                pair = jnp.where(lane[:half] < HD, qb[:half], pltpu.roll(qb[half:], HD, 1))
            else:
                both = jnp.where(lane < HD, pltpu.roll(kb, HD, 1), vb)
                pair = jnp.where(lane[:half] < HD, pltpu.roll(qb[:half], HD, 1), qb[half:])
            units[r * per + j, :positions, :] = both.astype(BF16)
            units[r * per + j, positions:, :] = pair.astype(BF16)
        return 0

    lax.fori_loop(0, requests, project, 0)
    for off in range(n_tok):
        target = (me + off) % n_tok
        unit = jnp.int32(0)
        for u in range(requests * per):
            unit = jnp.where(homes[u] == target, u, unit)
        if off == 0:
            outgoing[0] = units[unit]
            own = pltpu.make_async_copy(outgoing.at[0], out_ref.at[me], lsem.at[0])
            own_dec = pltpu.make_async_copy(pdec, dec_ref.at[me], lsem.at[1])
            own.start()
            own_dec.start()
            continue
        outgoing[off] = units[unit]
        copy = pltpu.make_async_remote_copy(
            src_ref=outgoing.at[off],
            dst_ref=out_ref.at[me],
            send_sem=ssem.at[off],
            recv_sem=rsem.at[off],
            device_id={"tok": target},
            device_id_type=MESH,
        )
        copy.start()
        copies.append(copy)
    own.wait()
    own_dec.wait()
    for copy in copies:
        copy.wait()


def project(states, dstates, gain, w, homes, n_tok):
    requests, positions, width = states.shape
    hosted = dstates.shape[0]
    features = w.shape[2]
    vmem = pl.BlockSpec(memory_space=pltpu.VMEM)
    smem = pl.BlockSpec(memory_space=pltpu.SMEM)
    packed = positions // 2 * 3
    units = requests * features // HD
    return pl.pallas_call(
        project_kernel,
        out_shape=(
            jax.ShapeDtypeStruct((n_tok, packed, 2 * HD), BF16),
            jax.ShapeDtypeStruct((n_tok, hosted, 3 * features), BF16),
        ),
        in_specs=[vmem, vmem, vmem, pl.BlockSpec(memory_space=pl.ANY), smem],
        out_specs=(vmem, vmem),
        scratch_shapes=[
            pltpu.VMEM(w.shape, BF16),
            pltpu.VMEM((requests * positions // 64, 64, width), BF16),
            pltpu.VMEM((units, packed, 2 * HD), BF16),
            pltpu.VMEM((n_tok, packed, 2 * HD), BF16),
            pltpu.VMEM((hosted, 3 * features), BF16),
            pltpu.SemaphoreType.DMA,
            pltpu.SemaphoreType.DMA((2,)),
            pltpu.SemaphoreType.DMA((n_tok,)),
            pltpu.SemaphoreType.DMA((n_tok,)),
            pltpu.SemaphoreType.DMA((n_tok,)),
            pltpu.SemaphoreType.DMA((n_tok,)),
        ],
        compiler_params=pltpu.CompilerParams(
            collective_id=2, has_side_effects=True, vmem_limit_bytes=56 * 1024 * 1024
        ),
        name="project",
    )(states, dstates, gain, w, homes)


def mix_kernel(
    attn,
    dattn,
    states_hbm,
    dstates,
    gain_ref,
    w_hbm,
    homes,
    dhomes,
    normed_ref,
    dnormed_ref,
    resid_ref,
    dresid_ref,
    w,
    own,
    drows,
    got,
    gdec,
    gdec_rows,
    left,
    dleft,
    part,
    pdec,
    rdec,
    pair,
    sums,
    relay,
    direct,
    lsem,
    tssem,
    trsem,
    dssem,
    drsem,
    hssem,
    hrsem,
    ssem,
    rsem,
):
    me = lax.axis_index("tok")
    n_tok = lax.axis_size("tok")
    head = lax.axis_index("head")
    n_head = lax.axis_size("head")
    my_x, core = head // 2, head % 2
    n_x = n_head // 2
    requests, rows, width = own.shape
    positions = rows * n_head
    half = positions // 2
    hosted = dattn.shape[0]
    barrier = pltpu.get_barrier_semaphore()
    for off in range(1, n_tok):
        pl.semaphore_signal(
            barrier, inc=1, device_id={"tok": (me + off) % n_tok}, device_id_type=MESH
        )
    for off in range(1, n_head):
        pl.semaphore_signal(
            barrier, inc=1, device_id={"head": (head + off) % n_head}, device_id_type=MESH
        )
    load_w = pltpu.make_async_copy(w_hbm, w, lsem.at[0])
    load_own = pltpu.make_async_copy(
        states_hbm.at[:, pl.ds(pl.multiple_of(head * rows, rows), rows), :], own, lsem.at[1]
    )
    keep = pltpu.make_async_copy(attn.at[me], got.at[me], lsem.at[2])
    keep_dec = pltpu.make_async_copy(dattn, gdec.at[me], lsem.at[3])
    local = [load_w, load_own, keep, keep_dec]
    for c in local:
        c.start()
    pl.semaphore_wait(barrier, n_tok + n_head - 2)
    sends = []
    for off in range(1, n_tok):
        target = (me + off) % n_tok
        for source, dest, a, b in (
            (attn.at[target], got.at[me], tssem, trsem),
            (dattn, gdec.at[me], dssem, drsem),
        ):
            copy = pltpu.make_async_remote_copy(
                src_ref=source,
                dst_ref=dest,
                send_sem=a.at[off],
                recv_sem=b.at[off],
                device_id={"tok": target},
                device_id_type=MESH,
            )
            copy.start()
            sends.append(copy)
    drows[...] = dstates[...].astype(F32)
    for c in local:
        c.wait()
    for c in sends:
        c.wait_recv()
    lane = lax.broadcasted_iota(jnp.int32, (half, PAGE), 1)
    per = w.shape[0] // HD
    for r in range(requests):
        for j in range(0, per, 2):
            a = got[homes[r * per + j]].astype(F32)
            b = got[homes[r * per + j + 1]].astype(F32)
            low = jnp.where(lane < HD, a, pltpu.roll(b, HD, 1))
            high = jnp.where(lane < HD, pltpu.roll(a, HD, 1), b)
            cols = slice(j // 2 * PAGE, (j // 2 + 1) * PAGE)
            left[r, :half, cols] = low.astype(BF16)
            left[r, half:, cols] = high.astype(BF16)
    for t in range(n_tok):
        gdec_rows[t * hosted : (t + 1) * hosted, :] = gdec[t].astype(F32)
    for i in range(hosted):
        dleft[i : i + 1, :] = gdec_rows[pl.ds(dhomes[me * hosted + i], 1), :]

    def project(r, _):
        result = jnp.dot(left[r], w[...], preferred_element_type=F32).astype(BF16)
        for k in range(n_head):
            part[k % 2, r, k // 2] = result[k * rows : (k + 1) * rows]
        return 0

    lax.fori_loop(0, requests, project, 0)
    used = [0]
    ring = []

    def send(source, target, device):
        i = used[0]
        used[0] += 1
        copy = pltpu.make_async_remote_copy(
            src_ref=source,
            dst_ref=target,
            send_sem=ssem.at[i],
            recv_sem=rsem.at[i],
            device_id={"head": device},
            device_id_type=MESH,
        )
        copy.start()
        ring.append(copy)
        return copy

    partner = my_x * 2 + 1 - core
    up = (my_x + 1) % n_x * 2 + core
    down = (my_x + n_x - 1) % n_x * 2 + core
    order = (2, 1, 3, 0)
    paired = {}
    for dx in order:
        paired[dx] = send(
            part.at[1 - core, :, (my_x + dx) % n_x], pair.at[dx], partner
        )
    dresult = jnp.dot(dleft[...].astype(BF16), w[...], preferred_element_type=F32)
    for k in range(n_head):
        pdec[k] = dresult[k : k + 1, :].astype(BF16)
    for off in range(1, n_head):
        copy = pltpu.make_async_remote_copy(
            src_ref=pdec.at[(head + off) % n_head],
            dst_ref=rdec.at[n_head - off],
            send_sem=hssem.at[off],
            recv_sem=hrsem.at[off],
            device_id={"head": (head + off) % n_head},
            device_id_type=MESH,
        )
        copy.start()
        sends.append(copy)
    hop = {}
    came = {}
    for dx in order:
        paired[dx].wait_recv()
        total = part[core, :, (my_x + dx) % n_x].astype(F32) + pair[dx].astype(F32)
        if dx == 0:
            resid_ref[...] = total + own[...].astype(F32)
        else:
            sums[dx] = total.astype(BF16)
        if dx == 2:
            hop[0] = send(sums.at[2, 0:2], relay.at[0], up)
            hop[1] = send(sums.at[2, 2:4], relay.at[1], down)
        if dx == 1:
            came[0, 1] = send(sums.at[1, 2:4], direct.at[0, 2:4], up)
        if dx == 3:
            came[1, 0] = send(sums.at[3, 0:2], direct.at[1, 0:2], down)
    hop[0].wait_recv()
    sums[1, 0:2] = (sums[1, 0:2].astype(F32) + relay[0].astype(F32)).astype(BF16)
    came[0, 0] = send(sums.at[1, 0:2], direct.at[0, 0:2], up)
    hop[1].wait_recv()
    sums[3, 2:4] = (sums[3, 2:4].astype(F32) + relay[1].astype(F32)).astype(BF16)
    came[1, 1] = send(sums.at[3, 2:4], direct.at[1, 2:4], down)
    gain = gain_ref[...]
    dtotal = drows[pl.ds(head, 1), :] + pdec[head].astype(F32)
    for c in sends[2 * (n_tok - 1) :]:
        c.wait_recv()
    for off in range(1, n_head):
        dtotal = dtotal + rdec[off].astype(F32)
    dresid_ref[...] = dtotal
    dnormed_ref[...] = rms_norm(dtotal, gain)
    for c in came.values():
        c.wait_recv()
    for r in range(requests):
        total = resid_ref[r] + direct[0, r].astype(F32) + direct[1, r].astype(F32)
        resid_ref[r] = total
        normed_ref[r] = rms_norm(total, gain)
    for c in sends + ring:
        c.wait_send()


def mix(attn, dattn, states, dstates, gain, w, homes, dhomes, n_head):
    requests, positions, width = states.shape
    n_tok, packed, lanes = attn.shape
    hosted = dattn.shape[0]
    rows = positions // n_head
    n_x = n_head // 2
    vmem = pl.BlockSpec(memory_space=pltpu.VMEM)
    smem = pl.BlockSpec(memory_space=pltpu.SMEM)
    hbm = pl.BlockSpec(memory_space=pl.ANY)
    sem = pltpu.SemaphoreType.DMA
    ring = 4 + 6
    return pl.pallas_call(
        mix_kernel,
        out_shape=(
            jax.ShapeDtypeStruct((requests, rows, width), BF16),
            jax.ShapeDtypeStruct((1, width), BF16),
            jax.ShapeDtypeStruct((requests, rows, width), F32),
            jax.ShapeDtypeStruct((1, width), F32),
        ),
        in_specs=[vmem, vmem, hbm, vmem, vmem, hbm, smem, smem],
        out_specs=(vmem, vmem, vmem, vmem),
        scratch_shapes=[
            pltpu.VMEM(w.shape, BF16),
            pltpu.VMEM((requests, rows, width), BF16),
            pltpu.VMEM((hosted, width), F32),
            pltpu.VMEM((n_tok, packed, lanes), BF16),
            pltpu.VMEM((n_tok, hosted, w.shape[0]), BF16),
            pltpu.VMEM((n_tok * hosted, w.shape[0]), F32),
            pltpu.VMEM((requests, positions, w.shape[0]), BF16),
            pltpu.VMEM((hosted, w.shape[0]), F32),
            pltpu.VMEM((2, requests, n_x, rows, width), BF16),
            pltpu.VMEM((n_head, 1, width), BF16),
            pltpu.VMEM((n_head, 1, width), BF16),
            pltpu.VMEM((n_x, requests, rows, width), BF16),
            pltpu.VMEM((n_x, requests, rows, width), BF16),
            pltpu.VMEM((2, 2, rows, width), BF16),
            pltpu.VMEM((2, requests, rows, width), BF16),
            sem((4,)),
            sem((n_tok,)),
            sem((n_tok,)),
            sem((n_tok,)),
            sem((n_tok,)),
            sem((n_head,)),
            sem((n_head,)),
            sem((ring,)),
            sem((ring,)),
        ],
        compiler_params=pltpu.CompilerParams(
            collective_id=3, has_side_effects=True, vmem_limit_bytes=56 * 1024 * 1024
        ),
        name="mix",
    )(attn, dattn, states, dstates, gain, w, homes, dhomes)


def shards(
    prefill_states,
    decode_states,
    attn_gain,
    w_qkv,
    w_out,
    ffn_gain,
    w_gate_up,
    w_down,
    prefill_pool,
    prefill_pages,
    prefill_lengths,
    prefill_home,
    decode_pool,
    decode_pages,
    decode_lengths,
    decode_home,
):
    n_tok = lax.axis_size("tok")
    n_head = lax.axis_size("head")
    width = prefill_states.shape[2]
    arrived, arrived_dec = project(
        prefill_states,
        decode_states,
        attn_gain.reshape(1, -1),
        jnp.transpose(w_qkv, (1, 0, 2)),
        prefill_home,
        n_tok,
    )
    attn, dattn = attention(
        prefill_pages,
        prefill_lengths,
        prefill_home,
        decode_pages,
        decode_lengths,
        decode_home,
        arrived,
        arrived_dec,
        prefill_pool.reshape(-1, 2 * HD),
        decode_pool.reshape(-1, decode_pool.shape[2]),
    )
    normed, dnormed, resid, dresid = mix(
        attn,
        dattn,
        prefill_states,
        decode_states,
        ffn_gain.reshape(1, -1),
        w_out,
        prefill_home,
        decode_home,
        n_head,
    )
    prefill_out, decode_out = ffn(
        normed,
        dnormed,
        resid,
        dresid,
        jnp.transpose(w_gate_up, (1, 2, 0)).reshape(-1, width),
        w_down,
        n_tok,
    )
    return (prefill_out, decode_out)


def solution(mesh):
    placed = (
        P(None, "tok", None),
        P("tok", None),
        P(),
        P(None, None, "head"),
        P("head", None),
        P(),
        P(None, None, "tok"),
        P("tok", None),
        P("tok", None, "head"),
        P("tok", None),
        P(),
        P(),
        P("tok", None, "head"),
        P("tok", None),
        P("tok"),
        P(),
    )
    return jax.shard_map(
        shards,
        mesh=mesh,
        in_specs=placed,
        out_specs=(P(None, ("tok", "head"), None), P(("tok", "head"), None)),
        check_vma=False,
    )
```

```python
import jax
import jax.numpy as jnp
from jax import lax
from jax.experimental import pallas as pl
from jax.experimental.pallas import tpu as pltpu
from jax.sharding import PartitionSpec as P

HD = 64
EPSILON = 1e-06
SCALE = 0.125
MASKED = -1e30
PAGE = 128
F32 = jnp.float32
BF16 = jnp.bfloat16


def rms_norm(rows, gain):
    values = rows.astype(F32)
    inverse = lax.rsqrt(jnp.mean(values * values, axis=-1, keepdims=True) + EPSILON)
    return (values * inverse * gain).astype(BF16)


def dot_nt(left, right):
    return lax.dot_general(left, right, (((1,), (1,)), ((), ())), preferred_element_type=F32)


QB = 512
KC = 512


def attention_kernel(
    pages,
    lengths,
    homes,
    dpages,
    dlens,
    dhomes,
    arrived,
    arrived_dec,
    pool_ref,
    dpool_hbm,
    out_ref,
    dout_ref,
    keys,
    vals,
    query,
    score,
    top_run,
    top,
    acc,
    dpool,
    dbias,
    dscore,
    drows,
    mine_ref,
    count,
    owner,
    dcount,
    anchor,
    sem,
):
    me = lax.axis_index("tok")
    n_tok = arrived.shape[0]
    positions = arrived.shape[1] // 3 * 2
    stretch = n_tok * positions
    span = pool_ref.shape[0]
    npages = span // PAGE
    dspan = dpool_hbm.shape[0]
    dnpages = dspan // PAGE
    slots, dmax = dpages.shape
    copy = pltpu.make_async_copy(dpool_hbm, dpool, sem)
    copy.start()

    my_unit = jnp.int32(0)
    for u in range(n_tok):
        my_unit = jnp.where(homes[u] == me, u, my_unit)
    length = lengths[my_unit // (n_tok // lengths.shape[0])]

    def count_page(i, _):
        count[pages[0, i]] = jnp.clip(length - i * PAGE, 0, PAGE)
        return 0

    lax.fori_loop(0, npages, count_page, 0)

    def zero_page(i, _):
        dcount[i] = 0
        owner[i] = 0
        return 0

    lax.fori_loop(0, dnpages, zero_page, 0)
    for s in range(slots):
        used = (dlens[s] + PAGE - 1) // PAGE

        def own_page(i, _):
            page = dpages[s, i]
            owner[page] = s
            dcount[page] = jnp.minimum(dlens[s] - i * PAGE, PAGE)
            return 0

        lax.fori_loop(0, used, own_page, 0)

    lane = lax.broadcasted_iota(jnp.int32, (PAGE, PAGE), 1)
    row = lax.broadcasted_iota(jnp.int32, (PAGE, PAGE), 0)

    def fill_cached(i, _):
        where_at = pl.ds(pl.multiple_of(i * PAGE, PAGE), PAGE)
        page = pool_ref[where_at, :].astype(F32)
        bias = jnp.where((lane == HD) & (row >= count[i]), MASKED, 0.0)
        keys[where_at, :] = jnp.where(lane < HD, page, bias).astype(BF16)
        vals[where_at, :] = jnp.where(lane < HD, 1.0, page).astype(BF16)
        return 0

    lax.fori_loop(0, npages, fill_cached, 0)

    half = PAGE // 2

    def fill_own(i, _):
        target = pl.ds(pl.multiple_of(span + i * PAGE, PAGE), PAGE)
        both = arrived[i, :PAGE, :].astype(F32)
        keys[target, :] = jnp.where(lane < HD, both, 0.0).astype(BF16)
        vals[target, :] = jnp.where(lane < HD, 1.0, both).astype(BF16)
        packed = arrived[i, PAGE:, :].astype(F32) * SCALE
        flag = jnp.where(lane[:half] == HD, 1.0, 0.0)
        low = jnp.where(lane[:half] < HD, packed, flag)
        high = jnp.where(lane[:half] < HD, pltpu.roll(packed, HD, 1), flag)
        at_low = pl.ds(pl.multiple_of(i * PAGE, PAGE), half)
        at_high = pl.ds(pl.multiple_of(i * PAGE + half, half), half)
        query[at_low, :] = low.astype(BF16)
        query[at_high, :] = high.astype(BF16)
        return 0

    lax.fori_loop(0, stretch // PAGE, fill_own, 0)

    def fold(s):
        best = s[:, :PAGE]
        for j in range(1, s.shape[1] // PAGE):
            best = jnp.maximum(best, s[:, j * PAGE : (j + 1) * PAGE])
        return best

    def make_scores(i, c, diagonal):
        rows = query[i * QB : (i + 1) * QB, :]
        s = dot_nt(rows, keys[pl.ds(pl.multiple_of(c * KC, KC), KC), :])
        if diagonal:
            r = lax.broadcasted_iota(jnp.int32, (QB, KC), 0)
            k = lax.broadcasted_iota(jnp.int32, (QB, KC), 1)
            s = jnp.where(k <= r, s, MASKED)
        score[i % 2, c] = s
        top_run[i % 2] = jnp.maximum(top_run[i % 2], fold(s))

    def finish_top(i):
        best = jnp.max(top_run[i % 2], axis=1, keepdims=True)
        top[i % 2] = jnp.broadcast_to(best, (QB, PAGE))

    def mix(i, c):
        best = top[i % 2]
        s = score[i % 2, c]
        p = jnp.exp(s - jnp.concatenate([best] * (KC // PAGE), axis=1)).astype(BF16)
        acc[...] += jnp.dot(
            p, vals[pl.ds(pl.multiple_of(c * KC, KC), KC), :], preferred_element_type=F32
        )

    blocks = stretch // QB
    cached_chunks = span // KC

    top_run[0] = jnp.full((QB, PAGE), MASKED, F32)

    def first(c, _):
        make_scores(0, c, False)
        return 0

    lax.fori_loop(0, cached_chunks, first, 0, unroll=4)
    make_scores(0, cached_chunks, True)
    finish_top(0)
    for i in range(blocks):
        acc[...] = jnp.zeros_like(acc)
        chunks = cached_chunks + i + 1
        if i + 1 < blocks:
            top_run[(i + 1) % 2] = jnp.full((QB, PAGE), MASKED, F32)

            def both(c, _, i=i):
                make_scores(i + 1, c, False)
                mix(i, c)
                return 0

            lax.fori_loop(0, chunks, both, 0, unroll=4)
            make_scores(i + 1, chunks, True)
            finish_top(i + 1)
        else:

            def last(c, _, i=i):
                mix(i, c)
                return 0

            lax.fori_loop(0, chunks, last, 0, unroll=4)
        total = acc[...]
        result = pltpu.roll(total, HD, 1) / total
        for j in range(QB // PAGE):
            tile = result[j * PAGE : (j + 1) * PAGE]
            out_ref[i * (QB // PAGE) + j] = jnp.where(
                lane[:half] < HD, tile[:half], pltpu.roll(tile[half:], HD, 1)
            ).astype(BF16)

    slot_row = lax.broadcasted_iota(jnp.int32, (slots, PAGE), 0)
    slot_lane = lax.broadcasted_iota(jnp.int32, (slots, PAGE), 1)

    def fill_bias(i, _):
        seen = (slot_row == owner[i]) & (slot_lane < dcount[i])
        dbias[i] = jnp.where(seen, 0.0, MASKED)
        return 0

    lax.fori_loop(0, dnpages, fill_bias, 0)
    for t in range(n_tok):
        drows[t * slots : (t + 1) * slots, :] = arrived_dec[t].astype(F32)

    def find(r, _):
        slot = dhomes[r] - me * slots

        @pl.when((slot >= 0) & (slot < slots))
        def _():
            anchor[slot] = r

        return 0

    lax.fori_loop(0, dhomes.shape[0], find, 0)
    for s in range(slots):
        mine_ref[s : s + 1, :] = drows[pl.ds(anchor[s], 1), :]
    copy.wait()
    rows = mine_ref[...]
    heads = rows.shape[1] // (3 * HD)
    step = 1024
    per = step // PAGE
    for h in range(heads):
        block = h // 2 * PAGE
        width = heads * HD

        def part(which, left):
            piece = rows[:, which * width + block : which * width + block + PAGE]
            return pltpu.roll(piece, HD, 1) if (h % 2 == 1) == left else piece

        q = jnp.where(slot_lane < HD, part(0, True) * SCALE, 0.0)
        k = part(1, True)
        v = part(2, False)
        own = jnp.sum(q * k, axis=1, keepdims=True)
        qb = q.astype(BF16)
        best = jnp.broadcast_to(own, (slots, PAGE))
        for c in range(dspan // step):
            s = dot_nt(qb, dpool[c * step : (c + 1) * step, h * PAGE : (h + 1) * PAGE])
            s = s + jnp.concatenate([dbias[c * per + j] for j in range(per)], axis=1)
            dscore[c] = s
            best = jnp.maximum(best, fold(s))
        best = jnp.max(best, axis=1, keepdims=True)
        own_weight = jnp.exp(own - best)
        sums = jnp.zeros((slots, PAGE), F32)
        mixed = jnp.zeros((slots, PAGE), F32)
        for c in range(dspan // step):
            p = jnp.exp(dscore[c] - best)
            for j in range(per):
                sums = sums + p[:, j * PAGE : (j + 1) * PAGE]
            mixed = mixed + jnp.dot(
                p.astype(BF16),
                dpool[c * step : (c + 1) * step, h * PAGE : (h + 1) * PAGE],
                preferred_element_type=F32,
            )
        total = jnp.sum(sums, axis=1, keepdims=True) + own_weight
        mixed = (mixed + own_weight.astype(BF16).astype(F32) * v) / total
        dout_ref[:, h * HD : (h + 1) * HD] = pltpu.roll(mixed, HD, 1)[:, :HD].astype(BF16)


def attention(
    pages, lengths, homes, dpages, dlens, dhomes, arrived, arrived_dec, pool, dpool
):
    n_tok, packed, lanes = arrived.shape
    positions = packed // 3 * 2
    stretch = n_tok * positions
    span = pool.shape[0]
    dspan, dwidth = dpool.shape
    slots, dcols = arrived_dec.shape[1:]
    keys = span + stretch
    vmem = pl.BlockSpec(memory_space=pltpu.VMEM)
    smem = pl.BlockSpec(memory_space=pltpu.SMEM)
    return pl.pallas_call(
        attention_kernel,
        out_shape=(
            jax.ShapeDtypeStruct((n_tok, positions // 2, lanes), BF16),
            jax.ShapeDtypeStruct((slots, dcols // 3), BF16),
        ),
        in_specs=[smem] * 6 + [vmem] * 3 + [pl.BlockSpec(memory_space=pl.ANY)],
        out_specs=(vmem, vmem),
        scratch_shapes=[
            pltpu.VMEM((keys, 2 * HD), BF16),
            pltpu.VMEM((keys, 2 * HD), BF16),
            pltpu.VMEM((stretch, 2 * HD), BF16),
            pltpu.VMEM((2, keys // KC, QB, KC), F32),
            pltpu.VMEM((2, QB, PAGE), F32),
            pltpu.VMEM((2, QB, PAGE), F32),
            pltpu.VMEM((QB, PAGE), F32),
            pltpu.VMEM((dspan, dwidth), BF16),
            pltpu.VMEM((dspan // PAGE, slots, PAGE), F32),
            pltpu.VMEM((dspan // 1024, slots, 1024), F32),
            pltpu.VMEM((n_tok * slots, dcols), F32),
            pltpu.VMEM((slots, dcols), F32),
            pltpu.SMEM((span // PAGE,), jnp.int32),
            pltpu.SMEM((dspan // PAGE,), jnp.int32),
            pltpu.SMEM((dspan // PAGE,), jnp.int32),
            pltpu.SMEM((slots,), jnp.int32),
            pltpu.SemaphoreType.DMA,
        ],
        compiler_params=pltpu.CompilerParams(vmem_limit_bytes=62 * 1024 * 1024),
        name="attention",
    )(pages, lengths, homes, dpages, dlens, dhomes, arrived, arrived_dec, pool, dpool)


MESH = pl.DeviceIdType.MESH
Q = 16


def ffn_kernel(
    block_ref,
    drow_ref,
    resid_ref,
    dresid_ref,
    wgu_hbm,
    wdown_hbm,
    out_ref,
    dout_ref,
    wgu,
    wdown,
    x,
    part,
    relay,
    direct,
    first,
    sums,
    relay1,
    direct1,
    xdec,
    xrows,
    pdec,
    rdec,
    wsem,
    ssem,
    rsem,
    dssem,
    drsem,
):
    me = lax.axis_index("tok")
    n_tok = lax.axis_size("tok")
    my_y, my_z = me // 4, me % 4
    barrier = pltpu.get_barrier_semaphore()
    for off in range(1, n_tok):
        pl.semaphore_signal(
            barrier,
            inc=1,
            device_id={"tok": (me + off) % n_tok},
            device_id_type=MESH,
        )
    load_gu = pltpu.make_async_copy(wgu_hbm, wgu, wsem.at[0])
    load_down = pltpu.make_async_copy(wdown_hbm, wdown, wsem.at[1])
    load_own = [
        pltpu.make_async_copy(
            block_ref.at[pl.ds(half * 2, 2)], x.at[half, 0, 0], wsem.at[2 + half]
        )
        for half in range(2)
    ]
    load_dec = pltpu.make_async_copy(drow_ref, xdec.at[0], wsem.at[4])
    for c in load_own:
        c.start()
    load_dec.start()
    load_gu.start()
    load_down.start()

    def along_z(step):
        return {"tok": my_y * 4 + (my_z + step + 4) % 4}

    def along_y(step):
        return {"tok": (my_y + step + 4) % 4 * 4 + my_z}

    axis1 = (along_z, along_y)
    axis2 = (along_y, along_z)
    used = [0]

    def send(source, target, device):
        i = used[0]
        used[0] += 1
        copy = pltpu.make_async_remote_copy(
            src_ref=source,
            dst_ref=target,
            send_sem=ssem.at[i],
            recv_sem=rsem.at[i],
            device_id=device,
            device_id_type=MESH,
        )
        copy.start()
        sent.append(copy)
        return copy

    sent = []
    for c in load_own:
        c.wait()
    load_dec.wait()
    pl.semaphore_wait(barrier, n_tok - 1)

    got = {}
    for half in range(2):
        own = x.at[half, 0, 0]
        got[half, 0, 3] = [send(own, x.at[half, 0, 3], axis1[half](1))]
        got[half, 0, 1] = [send(own, x.at[half, 0, 1], axis1[half](-1))]

    def spread(half, a1):
        own = x.at[half, 0, a1]
        got[half, 3, a1] = [send(own, x.at[half, 3, a1], axis2[half](1))]
        got[half, 1, a1] = [send(own, x.at[half, 1, a1], axis2[half](-1))]

    def relay2(half, a1):
        a = send(x.at[half, 3, a1, 0], x.at[half, 2, a1, 0], axis2[half](1))
        b = send(x.at[half, 1, a1, 1], x.at[half, 2, a1, 1], axis2[half](-1))
        got[half, 2, a1] = [a, b]

    def wait(half, a2, a1):
        for c in got[half, a2, a1]:
            c.wait_recv()

    for half in range(2):
        spread(half, 0)
    dec_copies = []
    for off in range(1, n_tok):
        copy = pltpu.make_async_remote_copy(
            src_ref=xdec.at[0],
            dst_ref=xdec.at[n_tok - off],
            send_sem=dssem.at[off],
            recv_sem=drsem.at[off],
            device_id={"tok": (me + off) % n_tok},
            device_id_type=MESH,
        )
        copy.start()
        dec_copies.append(copy)
    for half in range(2):
        wait(half, 0, 3)
        wait(half, 0, 1)
        a = send(x.at[half, 0, 3, 0], x.at[half, 0, 2, 0], axis1[half](1))
        b = send(x.at[half, 0, 1, 1], x.at[half, 0, 2, 1], axis1[half](-1))
        got[half, 0, 2] = [a, b]
        spread(half, 3)
        spread(half, 1)
    for half in range(2):
        wait(half, 3, 0)
        wait(half, 1, 0)
        relay2(half, 0)
    for half in range(2):
        wait(half, 0, 2)
        spread(half, 2)

    width = wdown.shape[0]

    def hidden_of(rows):
        both = dot_nt(rows, wgu[...])
        gate = both[:, :width]
        return (jax.nn.gelu(gate, approximate=True) * both[:, width:]).astype(BF16)

    def compute(a2):
        rows = x[:, a2].reshape(2 * 4 * 2 * Q, x.shape[-1])
        result = jnp.dot(hidden_of(rows), wdown[...], preferred_element_type=F32)
        part[:, a2] = result.astype(BF16).reshape(2, 4, 2, Q, x.shape[-1])

    load_gu.wait()
    load_down.wait()

    compute(0)
    for a1 in (3, 1):
        for half in range(2):
            wait(half, 3, a1)
            wait(half, 1, a1)
            relay2(half, a1)
    for half in range(2):
        wait(half, 3, 2)
        wait(half, 1, 2)
        relay2(half, 2)

    def group13(i, _):
        compute(3 - 2 * i)
        return 0

    lax.fori_loop(0, 2, group13, 0)
    came = {}
    for half in range(2):
        came[half, 0, 1] = send(
            part.at[half, 1, :, 1], direct.at[half, 0, :, 1], axis2[half](1)
        )
        came[half, 1, 0] = send(
            part.at[half, 3, :, 0], direct.at[half, 1, :, 0], axis2[half](-1)
        )
    for c in dec_copies:
        c.wait_recv()
    for t in range(n_tok):
        xrows[t : t + 1, :] = xdec[t].astype(F32)
    dpart = jnp.dot(
        hidden_of(xrows[...].astype(BF16)), wdown[...], preferred_element_type=F32
    )
    for t in range(n_tok):
        pdec[t] = dpart[t : t + 1, :].astype(BF16)
    dec_back = []
    for off in range(1, n_tok):
        copy = pltpu.make_async_remote_copy(
            src_ref=pdec.at[off],
            dst_ref=rdec.at[n_tok - off],
            send_sem=dssem.at[n_tok + off],
            recv_sem=drsem.at[n_tok + off],
            device_id={"tok": (me + off) % n_tok},
            device_id_type=MESH,
        )
        copy.start()
        dec_back.append(copy)

    hop = {}
    for half in range(2):
        for a1 in range(4):
            wait(half, 2, a1)
    compute(2)
    for half in range(2):
        hop[half, 0] = send(part.at[half, 2, :, 0], relay.at[half, 0], axis2[half](1))
        hop[half, 1] = send(part.at[half, 2, :, 1], relay.at[half, 1], axis2[half](-1))
    for half in range(2):
        hop[half, 0].wait_recv()
        part[half, 1, :, 0] = (
            part[half, 1, :, 0].astype(F32) + relay[half, 0].astype(F32)
        ).astype(BF16)
        came[half, 0, 0] = send(
            part.at[half, 1, :, 0], direct.at[half, 0, :, 0], axis2[half](1)
        )
        hop[half, 1].wait_recv()
        part[half, 3, :, 1] = (
            part[half, 3, :, 1].astype(F32) + relay[half, 1].astype(F32)
        ).astype(BF16)
        came[half, 1, 1] = send(
            part.at[half, 3, :, 1], direct.at[half, 1, :, 1], axis2[half](-1)
        )
    dtotal = dresid_ref[...] + pdec[0].astype(F32)
    for c in dec_back:
        c.wait_recv()
    for off in range(1, n_tok):
        dtotal = dtotal + rdec[off].astype(F32)
    dout_ref[...] = dtotal.astype(BF16)
    hop1 = {}
    came1 = {}
    for half in range(2):
        for side in range(2):
            for q in range(2):
                came[half, side, q].wait_recv()
        for a1 in (2, 1, 3, 0):
            total = (
                part[half, 0, a1].astype(F32)
                + direct[half, 0, a1].astype(F32)
                + direct[half, 1, a1].astype(F32)
            )
            if a1 == 0:
                first[half] = total
            else:
                sums[half, a1] = total.astype(BF16)
            if a1 == 2:
                hop1[half, 0] = send(
                    sums.at[half, 2, 0], relay1.at[half, 0], axis1[half](1)
                )
                hop1[half, 1] = send(
                    sums.at[half, 2, 1], relay1.at[half, 1], axis1[half](-1)
                )
            if a1 == 1:
                came1[half, 0, 1] = send(
                    sums.at[half, 1, 1], direct1.at[half, 0, 1], axis1[half](1)
                )
            if a1 == 3:
                came1[half, 1, 0] = send(
                    sums.at[half, 3, 0], direct1.at[half, 1, 0], axis1[half](-1)
                )
    for half in range(2):
        hop1[half, 0].wait_recv()
        sums[half, 1, 0] = (
            sums[half, 1, 0].astype(F32) + relay1[half, 0].astype(F32)
        ).astype(BF16)
        came1[half, 0, 0] = send(
            sums.at[half, 1, 0], direct1.at[half, 0, 0], axis1[half](1)
        )
        hop1[half, 1].wait_recv()
        sums[half, 3, 1] = (
            sums[half, 3, 1].astype(F32) + relay1[half, 1].astype(F32)
        ).astype(BF16)
        came1[half, 1, 1] = send(
            sums.at[half, 3, 1], direct1.at[half, 1, 1], axis1[half](-1)
        )
    for half in range(2):
        for side in range(2):
            for q in range(2):
                came1[half, side, q].wait_recv()
        out_ref[half * 2 : half * 2 + 2] = (
            resid_ref[half * 2 : half * 2 + 2]
            + first[half]
            + direct1[half, 0].astype(F32)
            + direct1[half, 1].astype(F32)
        ).astype(BF16)
    for c in sent + dec_copies + dec_back:
        c.wait_send()


FFN_SENDS = 2 * (2 + 2 + 8 + 8 + 6 + 6)


def ffn(block, drow, resid, dresid, wgu, wdown, n_tok):
    width = block.shape[-1]
    vmem = pl.BlockSpec(memory_space=pltpu.VMEM)
    hbm = pl.BlockSpec(memory_space=pl.ANY)
    return pl.pallas_call(
        ffn_kernel,
        out_shape=(
            jax.ShapeDtypeStruct(block.shape, BF16),
            jax.ShapeDtypeStruct(drow.shape, BF16),
        ),
        in_specs=[vmem, vmem, vmem, vmem, hbm, hbm],
        out_specs=(vmem, vmem),
        scratch_shapes=[
            pltpu.VMEM(wgu.shape, BF16),
            pltpu.VMEM(wdown.shape, BF16),
            pltpu.VMEM((2, 4, 4, 2, Q, width), BF16),
            pltpu.VMEM((2, 4, 4, 2, Q, width), BF16),
            pltpu.VMEM((2, 2, 4, Q, width), BF16),
            pltpu.VMEM((2, 2, 4, 2, Q, width), BF16),
            pltpu.VMEM((2, 2, Q, width), F32),
            pltpu.VMEM((2, 4, 2, Q, width), BF16),
            pltpu.VMEM((2, 2, Q, width), BF16),
            pltpu.VMEM((2, 2, 2, Q, width), BF16),
            pltpu.VMEM((n_tok, 1, width), BF16),
            pltpu.VMEM((n_tok, width), F32),
            pltpu.VMEM((n_tok, 1, width), BF16),
            pltpu.VMEM((n_tok, 1, width), BF16),
            pltpu.SemaphoreType.DMA((5,)),
            pltpu.SemaphoreType.DMA((FFN_SENDS,)),
            pltpu.SemaphoreType.DMA((FFN_SENDS,)),
            pltpu.SemaphoreType.DMA((2 * n_tok,)),
            pltpu.SemaphoreType.DMA((2 * n_tok,)),
        ],
        compiler_params=pltpu.CompilerParams(
            collective_id=1, has_side_effects=True, vmem_limit_bytes=56 * 1024 * 1024
        ),
        name="ffn",
    )(block, drow, resid, dresid, wgu, wdown)


def project_kernel(
    states,
    dstates,
    gain_ref,
    w_hbm,
    homes,
    out_ref,
    dec_ref,
    w,
    normed,
    units,
    outgoing,
    pdec,
    wsem,
    lsem,
    ssem,
    rsem,
    dssem,
    drsem,
):
    me = lax.axis_index("tok")
    n_tok = lax.axis_size("tok")
    requests, positions, width = states.shape
    features = w.shape[2]
    per = features // HD
    barrier = pltpu.get_barrier_semaphore()
    for off in range(1, n_tok):
        pl.semaphore_signal(
            barrier, inc=1, device_id={"tok": (me + off) % n_tok}, device_id_type=MESH
        )
    load = pltpu.make_async_copy(w_hbm, w, wsem)
    load.start()
    gain = gain_ref[...]
    pdec_rows = rms_norm(dstates[...], gain)
    lane = lax.broadcasted_iota(jnp.int32, (positions, PAGE), 1)
    half = positions // 2

    strip = 64

    def norm(i, _):
        at = pl.ds(pl.multiple_of(i % (positions // strip) * strip, strip), strip)
        normed[i] = rms_norm(states[i // (positions // strip), at, :], gain)
        return 0

    lax.fori_loop(0, requests * positions // strip, norm, 0)
    load.wait()
    pl.semaphore_wait(barrier, n_tok - 1)
    for which in range(3):
        pdec[:, which * features : (which + 1) * features] = jnp.dot(
            pdec_rows, w[which], preferred_element_type=F32
        ).astype(BF16)
    copies = []
    for off in range(1, n_tok):
        copy = pltpu.make_async_remote_copy(
            src_ref=pdec,
            dst_ref=dec_ref.at[me],
            send_sem=dssem.at[off],
            recv_sem=drsem.at[off],
            device_id={"tok": (me + off) % n_tok},
            device_id_type=MESH,
        )
        copy.start()
        copies.append(copy)

    def project(r, _):
        rows = normed[pl.ds(r * (positions // strip), positions // strip)].reshape(
            positions, width
        )
        q, k, v = (jnp.dot(rows, w[i], preferred_element_type=F32) for i in range(3))
        for j in range(per):
            at = j // 2 * PAGE
            qb, kb, vb = (a[:, at : at + PAGE] for a in (q, k, v))
            if j % 2 == 0:
                both = jnp.where(lane < HD, kb, pltpu.roll(vb, HD, 1))
                pair = jnp.where(lane[:half] < HD, qb[:half], pltpu.roll(qb[half:], HD, 1))
            else:
                both = jnp.where(lane < HD, pltpu.roll(kb, HD, 1), vb)
                pair = jnp.where(lane[:half] < HD, pltpu.roll(qb[:half], HD, 1), qb[half:])
            units[r * per + j, :positions, :] = both.astype(BF16)
            units[r * per + j, positions:, :] = pair.astype(BF16)
        return 0

    lax.fori_loop(0, requests, project, 0)
    for off in range(n_tok):
        target = (me + off) % n_tok
        unit = jnp.int32(0)
        for u in range(requests * per):
            unit = jnp.where(homes[u] == target, u, unit)
        if off == 0:
            outgoing[0] = units[unit]
            own = pltpu.make_async_copy(outgoing.at[0], out_ref.at[me], lsem.at[0])
            own_dec = pltpu.make_async_copy(pdec, dec_ref.at[me], lsem.at[1])
            own.start()
            own_dec.start()
            continue
        outgoing[off] = units[unit]
        copy = pltpu.make_async_remote_copy(
            src_ref=outgoing.at[off],
            dst_ref=out_ref.at[me],
            send_sem=ssem.at[off],
            recv_sem=rsem.at[off],
            device_id={"tok": target},
            device_id_type=MESH,
        )
        copy.start()
        copies.append(copy)
    own.wait()
    own_dec.wait()
    for copy in copies:
        copy.wait()


def project(states, dstates, gain, w, homes, n_tok):
    requests, positions, width = states.shape
    hosted = dstates.shape[0]
    features = w.shape[2]
    vmem = pl.BlockSpec(memory_space=pltpu.VMEM)
    smem = pl.BlockSpec(memory_space=pltpu.SMEM)
    packed = positions // 2 * 3
    units = requests * features // HD
    return pl.pallas_call(
        project_kernel,
        out_shape=(
            jax.ShapeDtypeStruct((n_tok, packed, 2 * HD), BF16),
            jax.ShapeDtypeStruct((n_tok, hosted, 3 * features), BF16),
        ),
        in_specs=[vmem, vmem, vmem, pl.BlockSpec(memory_space=pl.ANY), smem],
        out_specs=(vmem, vmem),
        scratch_shapes=[
            pltpu.VMEM(w.shape, BF16),
            pltpu.VMEM((requests * positions // 64, 64, width), BF16),
            pltpu.VMEM((units, packed, 2 * HD), BF16),
            pltpu.VMEM((n_tok, packed, 2 * HD), BF16),
            pltpu.VMEM((hosted, 3 * features), BF16),
            pltpu.SemaphoreType.DMA,
            pltpu.SemaphoreType.DMA((2,)),
            pltpu.SemaphoreType.DMA((n_tok,)),
            pltpu.SemaphoreType.DMA((n_tok,)),
            pltpu.SemaphoreType.DMA((n_tok,)),
            pltpu.SemaphoreType.DMA((n_tok,)),
        ],
        compiler_params=pltpu.CompilerParams(
            collective_id=2, has_side_effects=True, vmem_limit_bytes=56 * 1024 * 1024
        ),
        name="project",
    )(states, dstates, gain, w, homes)


def mix_kernel(
    attn,
    dattn,
    states_hbm,
    dstates,
    gain_ref,
    w_hbm,
    homes,
    dhomes,
    normed_ref,
    dnormed_ref,
    resid_ref,
    dresid_ref,
    w,
    own,
    drows,
    got,
    gdec,
    gdec_rows,
    left,
    dleft,
    part,
    pdec,
    rdec,
    pair,
    sums,
    relay,
    direct,
    lsem,
    tssem,
    trsem,
    dssem,
    drsem,
    hssem,
    hrsem,
    ssem,
    rsem,
):
    me = lax.axis_index("tok")
    n_tok = lax.axis_size("tok")
    head = lax.axis_index("head")
    n_head = lax.axis_size("head")
    my_x, core = head // 2, head % 2
    n_x = n_head // 2
    requests, rows, width = own.shape
    positions = rows * n_head
    half = positions // 2
    hosted = dattn.shape[0]
    barrier = pltpu.get_barrier_semaphore()
    for off in range(1, n_tok):
        pl.semaphore_signal(
            barrier, inc=1, device_id={"tok": (me + off) % n_tok}, device_id_type=MESH
        )
    for off in range(1, n_head):
        pl.semaphore_signal(
            barrier, inc=1, device_id={"head": (head + off) % n_head}, device_id_type=MESH
        )
    load_w = pltpu.make_async_copy(w_hbm, w, lsem.at[0])
    load_own = pltpu.make_async_copy(
        states_hbm.at[:, pl.ds(pl.multiple_of(head * rows, rows), rows), :], own, lsem.at[1]
    )
    keep = pltpu.make_async_copy(attn.at[me], got.at[me], lsem.at[2])
    keep_dec = pltpu.make_async_copy(dattn, gdec.at[me], lsem.at[3])
    local = [load_w, load_own, keep, keep_dec]
    for c in local:
        c.start()
    pl.semaphore_wait(barrier, n_tok + n_head - 2)
    sends = []
    for off in range(1, n_tok):
        target = (me + off) % n_tok
        for source, dest, a, b in (
            (attn.at[target], got.at[me], tssem, trsem),
            (dattn, gdec.at[me], dssem, drsem),
        ):
            copy = pltpu.make_async_remote_copy(
                src_ref=source,
                dst_ref=dest,
                send_sem=a.at[off],
                recv_sem=b.at[off],
                device_id={"tok": target},
                device_id_type=MESH,
            )
            copy.start()
            sends.append(copy)
    drows[...] = dstates[...].astype(F32)
    for c in local:
        c.wait()
    for c in sends:
        c.wait_recv()
    lane = lax.broadcasted_iota(jnp.int32, (half, PAGE), 1)
    per = w.shape[0] // HD
    for r in range(requests):
        for j in range(0, per, 2):
            a = got[homes[r * per + j]].astype(F32)
            b = got[homes[r * per + j + 1]].astype(F32)
            low = jnp.where(lane < HD, a, pltpu.roll(b, HD, 1))
            high = jnp.where(lane < HD, pltpu.roll(a, HD, 1), b)
            cols = slice(j // 2 * PAGE, (j // 2 + 1) * PAGE)
            left[r, :half, cols] = low.astype(BF16)
            left[r, half:, cols] = high.astype(BF16)
    for t in range(n_tok):
        gdec_rows[t * hosted : (t + 1) * hosted, :] = gdec[t].astype(F32)
    for i in range(hosted):
        dleft[i : i + 1, :] = gdec_rows[pl.ds(dhomes[me * hosted + i], 1), :]

    def project(r, _):
        result = jnp.dot(left[r], w[...], preferred_element_type=F32).astype(BF16)
        for k in range(n_head):
            part[k % 2, r, k // 2] = result[k * rows : (k + 1) * rows]
        return 0

    lax.fori_loop(0, requests, project, 0)
    used = [0]
    ring = []

    def send(source, target, device):
        i = used[0]
        used[0] += 1
        copy = pltpu.make_async_remote_copy(
            src_ref=source,
            dst_ref=target,
            send_sem=ssem.at[i],
            recv_sem=rsem.at[i],
            device_id={"head": device},
            device_id_type=MESH,
        )
        copy.start()
        ring.append(copy)
        return copy

    partner = my_x * 2 + 1 - core
    up = (my_x + 1) % n_x * 2 + core
    down = (my_x + n_x - 1) % n_x * 2 + core
    order = (2, 1, 3, 0)
    paired = {}
    for dx in order:
        paired[dx] = send(
            part.at[1 - core, :, (my_x + dx) % n_x], pair.at[dx], partner
        )
    dresult = jnp.dot(dleft[...].astype(BF16), w[...], preferred_element_type=F32)
    for k in range(n_head):
        pdec[k] = dresult[k : k + 1, :].astype(BF16)
    for off in range(1, n_head):
        copy = pltpu.make_async_remote_copy(
            src_ref=pdec.at[(head + off) % n_head],
            dst_ref=rdec.at[n_head - off],
            send_sem=hssem.at[off],
            recv_sem=hrsem.at[off],
            device_id={"head": (head + off) % n_head},
            device_id_type=MESH,
        )
        copy.start()
        sends.append(copy)
    hop = {}
    came = {}
    for dx in order:
        paired[dx].wait_recv()
        total = part[core, :, (my_x + dx) % n_x].astype(F32) + pair[dx].astype(F32)
        if dx == 0:
            resid_ref[...] = total + own[...].astype(F32)
        else:
            sums[dx] = total.astype(BF16)
        if dx == 2:
            hop[0] = send(sums.at[2, 0:2], relay.at[0], up)
            hop[1] = send(sums.at[2, 2:4], relay.at[1], down)
        if dx == 1:
            came[0, 1] = send(sums.at[1, 2:4], direct.at[0, 2:4], up)
        if dx == 3:
            came[1, 0] = send(sums.at[3, 0:2], direct.at[1, 0:2], down)
    hop[0].wait_recv()
    sums[1, 0:2] = (sums[1, 0:2].astype(F32) + relay[0].astype(F32)).astype(BF16)
    came[0, 0] = send(sums.at[1, 0:2], direct.at[0, 0:2], up)
    hop[1].wait_recv()
    sums[3, 2:4] = (sums[3, 2:4].astype(F32) + relay[1].astype(F32)).astype(BF16)
    came[1, 1] = send(sums.at[3, 2:4], direct.at[1, 2:4], down)
    gain = gain_ref[...]
    dtotal = drows[pl.ds(head, 1), :] + pdec[head].astype(F32)
    for c in sends[2 * (n_tok - 1) :]:
        c.wait_recv()
    for off in range(1, n_head):
        dtotal = dtotal + rdec[off].astype(F32)
    dresid_ref[...] = dtotal
    dnormed_ref[...] = rms_norm(dtotal, gain)
    for c in came.values():
        c.wait_recv()
    for r in range(requests):
        total = resid_ref[r] + direct[0, r].astype(F32) + direct[1, r].astype(F32)
        resid_ref[r] = total
        normed_ref[r] = rms_norm(total, gain)
    for c in sends + ring:
        c.wait_send()


def mix(attn, dattn, states, dstates, gain, w, homes, dhomes, n_head):
    requests, positions, width = states.shape
    n_tok, packed, lanes = attn.shape
    hosted = dattn.shape[0]
    rows = positions // n_head
    n_x = n_head // 2
    vmem = pl.BlockSpec(memory_space=pltpu.VMEM)
    smem = pl.BlockSpec(memory_space=pltpu.SMEM)
    hbm = pl.BlockSpec(memory_space=pl.ANY)
    sem = pltpu.SemaphoreType.DMA
    ring = 4 + 6
    return pl.pallas_call(
        mix_kernel,
        out_shape=(
            jax.ShapeDtypeStruct((requests, rows, width), BF16),
            jax.ShapeDtypeStruct((1, width), BF16),
            jax.ShapeDtypeStruct((requests, rows, width), F32),
            jax.ShapeDtypeStruct((1, width), F32),
        ),
        in_specs=[vmem, vmem, hbm, vmem, vmem, hbm, smem, smem],
        out_specs=(vmem, vmem, vmem, vmem),
        scratch_shapes=[
            pltpu.VMEM(w.shape, BF16),
            pltpu.VMEM((requests, rows, width), BF16),
            pltpu.VMEM((hosted, width), F32),
            pltpu.VMEM((n_tok, packed, lanes), BF16),
            pltpu.VMEM((n_tok, hosted, w.shape[0]), BF16),
            pltpu.VMEM((n_tok * hosted, w.shape[0]), F32),
            pltpu.VMEM((requests, positions, w.shape[0]), BF16),
            pltpu.VMEM((hosted, w.shape[0]), F32),
            pltpu.VMEM((2, requests, n_x, rows, width), BF16),
            pltpu.VMEM((n_head, 1, width), BF16),
            pltpu.VMEM((n_head, 1, width), BF16),
            pltpu.VMEM((n_x, requests, rows, width), BF16),
            pltpu.VMEM((n_x, requests, rows, width), BF16),
            pltpu.VMEM((2, 2, rows, width), BF16),
            pltpu.VMEM((2, requests, rows, width), BF16),
            sem((4,)),
            sem((n_tok,)),
            sem((n_tok,)),
            sem((n_tok,)),
            sem((n_tok,)),
            sem((n_head,)),
            sem((n_head,)),
            sem((ring,)),
            sem((ring,)),
        ],
        compiler_params=pltpu.CompilerParams(
            collective_id=3, has_side_effects=True, vmem_limit_bytes=56 * 1024 * 1024
        ),
        name="mix",
    )(attn, dattn, states, dstates, gain, w, homes, dhomes)


def shards(
    prefill_states,
    decode_states,
    attn_gain,
    w_qkv,
    w_out,
    ffn_gain,
    w_gate_up,
    w_down,
    prefill_pool,
    prefill_pages,
    prefill_lengths,
    prefill_home,
    decode_pool,
    decode_pages,
    decode_lengths,
    decode_home,
):
    n_tok = lax.axis_size("tok")
    n_head = lax.axis_size("head")
    width = prefill_states.shape[2]
    arrived, arrived_dec = project(
        prefill_states,
        decode_states,
        attn_gain.reshape(1, -1),
        jnp.transpose(w_qkv, (1, 0, 2)),
        prefill_home,
        n_tok,
    )
    attn, dattn = attention(
        prefill_pages,
        prefill_lengths,
        prefill_home,
        decode_pages,
        decode_lengths,
        decode_home,
        arrived,
        arrived_dec,
        prefill_pool.reshape(-1, 2 * HD),
        decode_pool.reshape(-1, decode_pool.shape[2]),
    )
    normed, dnormed, resid, dresid = mix(
        attn,
        dattn,
        prefill_states,
        decode_states,
        ffn_gain.reshape(1, -1),
        w_out,
        prefill_home,
        decode_home,
        n_head,
    )
    prefill_out, decode_out = ffn(
        normed,
        dnormed,
        resid,
        dresid,
        jnp.transpose(w_gate_up, (1, 2, 0)).reshape(-1, width),
        w_down,
        n_tok,
    )
    return (prefill_out, decode_out)


def solution(mesh):
    placed = (
        P(None, "tok", None),
        P("tok", None),
        P(),
        P(None, None, "head"),
        P("head", None),
        P(),
        P(None, None, "tok"),
        P("tok", None),
        P("tok", None, "head"),
        P("tok", None),
        P(),
        P(),
        P("tok", None, "head"),
        P("tok", None),
        P("tok"),
        P(),
    )
    return jax.shard_map(
        shards,
        mesh=mesh,
        in_specs=placed,
        out_specs=(P(None, ("tok", "head"), None), P(("tok", "head"), None)),
        check_vma=False,
    )
```

```python
import jax
import jax.numpy as jnp
from jax import lax
from jax.experimental import pallas as pl
from jax.experimental.pallas import tpu as pltpu
from jax.sharding import PartitionSpec as P

HD = 64
EPSILON = 1e-06
SCALE = 0.125
MASKED = -1e30
PAGE = 128
F32 = jnp.float32
BF16 = jnp.bfloat16


def rms_norm(rows, gain):
    values = rows.astype(F32)
    inverse = lax.rsqrt(jnp.mean(values * values, axis=-1, keepdims=True) + EPSILON)
    return (values * inverse * gain).astype(BF16)


def dot_nt(left, right):
    return lax.dot_general(left, right, (((1,), (1,)), ((), ())), preferred_element_type=F32)


QB = 512
KC = 512


def attention_kernel(
    pages,
    lengths,
    homes,
    dpages,
    dlens,
    dhomes,
    arrived,
    arrived_dec,
    pool_ref,
    dpool_hbm,
    out_ref,
    dout_ref,
    keys,
    vals,
    query,
    score,
    top_run,
    top,
    acc,
    dpool,
    dbias,
    dscore,
    drows,
    mine_ref,
    count,
    owner,
    dcount,
    anchor,
    sem,
):
    me = lax.axis_index("tok")
    n_tok = arrived.shape[0]
    positions = arrived.shape[1] // 3 * 2
    stretch = n_tok * positions
    span = pool_ref.shape[0]
    npages = span // PAGE
    dspan = dpool_hbm.shape[0]
    dnpages = dspan // PAGE
    slots, dmax = dpages.shape
    copy = pltpu.make_async_copy(dpool_hbm, dpool, sem)
    copy.start()

    my_unit = jnp.int32(0)
    for u in range(n_tok):
        my_unit = jnp.where(homes[u] == me, u, my_unit)
    length = lengths[my_unit // (n_tok // lengths.shape[0])]

    def count_page(i, _):
        count[pages[0, i]] = jnp.clip(length - i * PAGE, 0, PAGE)
        return 0

    lax.fori_loop(0, npages, count_page, 0)

    def zero_page(i, _):
        dcount[i] = 0
        owner[i] = 0
        return 0

    lax.fori_loop(0, dnpages, zero_page, 0)
    for s in range(slots):
        used = (dlens[s] + PAGE - 1) // PAGE

        def own_page(i, _):
            page = dpages[s, i]
            owner[page] = s
            dcount[page] = jnp.minimum(dlens[s] - i * PAGE, PAGE)
            return 0

        lax.fori_loop(0, used, own_page, 0)

    lane = lax.broadcasted_iota(jnp.int32, (PAGE, PAGE), 1)
    row = lax.broadcasted_iota(jnp.int32, (PAGE, PAGE), 0)

    def fill_cached(i, _):
        where_at = pl.ds(pl.multiple_of(i * PAGE, PAGE), PAGE)
        page = pool_ref[where_at, :].astype(F32)
        bias = jnp.where((lane == HD) & (row >= count[i]), MASKED, 0.0)
        keys[where_at, :] = jnp.where(lane < HD, page, bias).astype(BF16)
        vals[where_at, :] = jnp.where(lane < HD, 1.0, page).astype(BF16)
        return 0

    lax.fori_loop(0, npages, fill_cached, 0, unroll=4)

    half = PAGE // 2

    def fill_own(i, _):
        target = pl.ds(pl.multiple_of(span + i * PAGE, PAGE), PAGE)
        both = arrived[i, :PAGE, :].astype(F32)
        keys[target, :] = jnp.where(lane < HD, both, 0.0).astype(BF16)
        vals[target, :] = jnp.where(lane < HD, 1.0, both).astype(BF16)
        packed = arrived[i, PAGE:, :].astype(F32) * SCALE
        flag = jnp.where(lane[:half] == HD, 1.0, 0.0)
        low = jnp.where(lane[:half] < HD, packed, flag)
        high = jnp.where(lane[:half] < HD, pltpu.roll(packed, HD, 1), flag)
        at_low = pl.ds(pl.multiple_of(i * PAGE, PAGE), half)
        at_high = pl.ds(pl.multiple_of(i * PAGE + half, half), half)
        query[at_low, :] = low.astype(BF16)
        query[at_high, :] = high.astype(BF16)
        return 0

    lax.fori_loop(0, stretch // PAGE, fill_own, 0, unroll=4)

    def fold(s):
        best = s[:, :PAGE]
        for j in range(1, s.shape[1] // PAGE):
            best = jnp.maximum(best, s[:, j * PAGE : (j + 1) * PAGE])
        return best

    def make_scores(i, c, diagonal):
        rows = query[i * QB : (i + 1) * QB, :]
        s = dot_nt(rows, keys[pl.ds(pl.multiple_of(c * KC, KC), KC), :])
        if diagonal:
            r = lax.broadcasted_iota(jnp.int32, (QB, KC), 0)
            k = lax.broadcasted_iota(jnp.int32, (QB, KC), 1)
            s = jnp.where(k <= r, s, MASKED)
        score[i % 2, c] = s
        top_run[i % 2] = jnp.maximum(top_run[i % 2], fold(s))

    def finish_top(i):
        best = jnp.max(top_run[i % 2], axis=1, keepdims=True)
        top[i % 2] = jnp.broadcast_to(best, (QB, PAGE))

    def mix(i, c):
        best = top[i % 2]
        s = score[i % 2, c]
        p = jnp.exp(s - jnp.concatenate([best] * (KC // PAGE), axis=1)).astype(BF16)
        acc[...] += jnp.dot(
            p, vals[pl.ds(pl.multiple_of(c * KC, KC), KC), :], preferred_element_type=F32
        )

    blocks = stretch // QB
    cached_chunks = span // KC

    top_run[0] = jnp.full((QB, PAGE), MASKED, F32)

    def first(c, _):
        make_scores(0, c, False)
        return 0

    lax.fori_loop(0, cached_chunks, first, 0, unroll=4)
    make_scores(0, cached_chunks, True)
    finish_top(0)
    for i in range(blocks):
        acc[...] = jnp.zeros_like(acc)
        chunks = cached_chunks + i + 1
        if i + 1 < blocks:
            top_run[(i + 1) % 2] = jnp.full((QB, PAGE), MASKED, F32)

            def both(c, _, i=i):
                make_scores(i + 1, c, False)
                mix(i, c)
                return 0

            lax.fori_loop(0, chunks, both, 0, unroll=4)
            make_scores(i + 1, chunks, True)
            finish_top(i + 1)
        else:

            def last(c, _, i=i):
                mix(i, c)
                return 0

            lax.fori_loop(0, chunks, last, 0, unroll=4)
        total = acc[...]
        result = pltpu.roll(total, HD, 1) / total
        for j in range(QB // PAGE):
            tile = result[j * PAGE : (j + 1) * PAGE]
            out_ref[i * (QB // PAGE) + j] = jnp.where(
                lane[:half] < HD, tile[:half], pltpu.roll(tile[half:], HD, 1)
            ).astype(BF16)

    slot_row = lax.broadcasted_iota(jnp.int32, (slots, PAGE), 0)
    slot_lane = lax.broadcasted_iota(jnp.int32, (slots, PAGE), 1)

    def fill_bias(i, _):
        seen = (slot_row == owner[i]) & (slot_lane < dcount[i])
        dbias[i] = jnp.where(seen, 0.0, MASKED)
        return 0

    lax.fori_loop(0, dnpages, fill_bias, 0)
    for t in range(n_tok):
        drows[t * slots : (t + 1) * slots, :] = arrived_dec[t].astype(F32)

    def find(r, _):
        slot = dhomes[r] - me * slots

        @pl.when((slot >= 0) & (slot < slots))
        def _():
            anchor[slot] = r

        return 0

    lax.fori_loop(0, dhomes.shape[0], find, 0)
    for s in range(slots):
        mine_ref[s : s + 1, :] = drows[pl.ds(anchor[s], 1), :]
    copy.wait()
    rows = mine_ref[...]
    heads = rows.shape[1] // (3 * HD)
    step = 1024
    per = step // PAGE
    for h in range(heads):
        block = h // 2 * PAGE
        width = heads * HD

        def part(which, left):
            piece = rows[:, which * width + block : which * width + block + PAGE]
            return pltpu.roll(piece, HD, 1) if (h % 2 == 1) == left else piece

        q = jnp.where(slot_lane < HD, part(0, True) * SCALE, 0.0)
        k = part(1, True)
        v = part(2, False)
        own = jnp.sum(q * k, axis=1, keepdims=True)
        qb = q.astype(BF16)
        best = jnp.broadcast_to(own, (slots, PAGE))
        for c in range(dspan // step):
            s = dot_nt(qb, dpool[c * step : (c + 1) * step, h * PAGE : (h + 1) * PAGE])
            s = s + jnp.concatenate([dbias[c * per + j] for j in range(per)], axis=1)
            dscore[c] = s
            best = jnp.maximum(best, fold(s))
        best = jnp.max(best, axis=1, keepdims=True)
        own_weight = jnp.exp(own - best)
        sums = jnp.zeros((slots, PAGE), F32)
        mixed = jnp.zeros((slots, PAGE), F32)
        for c in range(dspan // step):
            p = jnp.exp(dscore[c] - best)
            for j in range(per):
                sums = sums + p[:, j * PAGE : (j + 1) * PAGE]
            mixed = mixed + jnp.dot(
                p.astype(BF16),
                dpool[c * step : (c + 1) * step, h * PAGE : (h + 1) * PAGE],
                preferred_element_type=F32,
            )
        total = jnp.sum(sums, axis=1, keepdims=True) + own_weight
        mixed = (mixed + own_weight.astype(BF16).astype(F32) * v) / total
        dout_ref[:, h * HD : (h + 1) * HD] = pltpu.roll(mixed, HD, 1)[:, :HD].astype(BF16)


def attention(
    pages, lengths, homes, dpages, dlens, dhomes, arrived, arrived_dec, pool, dpool
):
    n_tok, packed, lanes = arrived.shape
    positions = packed // 3 * 2
    stretch = n_tok * positions
    span = pool.shape[0]
    dspan, dwidth = dpool.shape
    slots, dcols = arrived_dec.shape[1:]
    keys = span + stretch
    vmem = pl.BlockSpec(memory_space=pltpu.VMEM)
    smem = pl.BlockSpec(memory_space=pltpu.SMEM)
    return pl.pallas_call(
        attention_kernel,
        out_shape=(
            jax.ShapeDtypeStruct((n_tok, positions // 2, lanes), BF16),
            jax.ShapeDtypeStruct((slots, dcols // 3), BF16),
        ),
        in_specs=[smem] * 6 + [vmem] * 3 + [pl.BlockSpec(memory_space=pl.ANY)],
        out_specs=(vmem, vmem),
        scratch_shapes=[
            pltpu.VMEM((keys, 2 * HD), BF16),
            pltpu.VMEM((keys, 2 * HD), BF16),
            pltpu.VMEM((stretch, 2 * HD), BF16),
            pltpu.VMEM((2, keys // KC, QB, KC), F32),
            pltpu.VMEM((2, QB, PAGE), F32),
            pltpu.VMEM((2, QB, PAGE), F32),
            pltpu.VMEM((QB, PAGE), F32),
            pltpu.VMEM((dspan, dwidth), BF16),
            pltpu.VMEM((dspan // PAGE, slots, PAGE), F32),
            pltpu.VMEM((dspan // 1024, slots, 1024), F32),
            pltpu.VMEM((n_tok * slots, dcols), F32),
            pltpu.VMEM((slots, dcols), F32),
            pltpu.SMEM((span // PAGE,), jnp.int32),
            pltpu.SMEM((dspan // PAGE,), jnp.int32),
            pltpu.SMEM((dspan // PAGE,), jnp.int32),
            pltpu.SMEM((slots,), jnp.int32),
            pltpu.SemaphoreType.DMA,
        ],
        compiler_params=pltpu.CompilerParams(vmem_limit_bytes=62 * 1024 * 1024),
        name="attention",
    )(pages, lengths, homes, dpages, dlens, dhomes, arrived, arrived_dec, pool, dpool)


MESH = pl.DeviceIdType.MESH
Q = 16


def ffn_kernel(
    block_ref,
    drow_ref,
    resid_ref,
    dresid_ref,
    wgu_hbm,
    wdown_hbm,
    out_ref,
    dout_ref,
    wgu,
    wdown,
    x,
    part,
    relay,
    direct,
    first,
    sums,
    relay1,
    direct1,
    xdec,
    xrows,
    pdec,
    rdec,
    wsem,
    ssem,
    rsem,
    dssem,
    drsem,
):
    me = lax.axis_index("tok")
    n_tok = lax.axis_size("tok")
    my_y, my_z = me // 4, me % 4
    barrier = pltpu.get_barrier_semaphore()
    for off in range(1, n_tok):
        pl.semaphore_signal(
            barrier,
            inc=1,
            device_id={"tok": (me + off) % n_tok},
            device_id_type=MESH,
        )
    load_gu = pltpu.make_async_copy(wgu_hbm, wgu, wsem.at[0])
    load_down = pltpu.make_async_copy(wdown_hbm, wdown, wsem.at[1])
    load_own = [
        pltpu.make_async_copy(
            block_ref.at[pl.ds(half * 2, 2)], x.at[half, 0, 0], wsem.at[2 + half]
        )
        for half in range(2)
    ]
    load_dec = pltpu.make_async_copy(drow_ref, xdec.at[0], wsem.at[4])
    for c in load_own:
        c.start()
    load_dec.start()
    load_gu.start()
    load_down.start()

    def along_z(step):
        return {"tok": my_y * 4 + (my_z + step + 4) % 4}

    def along_y(step):
        return {"tok": (my_y + step + 4) % 4 * 4 + my_z}

    axis1 = (along_z, along_y)
    axis2 = (along_y, along_z)
    used = [0]

    def send(source, target, device):
        i = used[0]
        used[0] += 1
        copy = pltpu.make_async_remote_copy(
            src_ref=source,
            dst_ref=target,
            send_sem=ssem.at[i],
            recv_sem=rsem.at[i],
            device_id=device,
            device_id_type=MESH,
        )
        copy.start()
        sent.append(copy)
        return copy

    sent = []
    for c in load_own:
        c.wait()
    load_dec.wait()
    pl.semaphore_wait(barrier, n_tok - 1)

    got = {}
    for half in range(2):
        own = x.at[half, 0, 0]
        got[half, 0, 3] = [send(own, x.at[half, 0, 3], axis1[half](1))]
        got[half, 0, 1] = [send(own, x.at[half, 0, 1], axis1[half](-1))]

    def spread(half, a1):
        own = x.at[half, 0, a1]
        got[half, 3, a1] = [send(own, x.at[half, 3, a1], axis2[half](1))]
        got[half, 1, a1] = [send(own, x.at[half, 1, a1], axis2[half](-1))]

    def relay2(half, a1):
        a = send(x.at[half, 3, a1, 0], x.at[half, 2, a1, 0], axis2[half](1))
        b = send(x.at[half, 1, a1, 1], x.at[half, 2, a1, 1], axis2[half](-1))
        got[half, 2, a1] = [a, b]

    def wait(half, a2, a1):
        for c in got[half, a2, a1]:
            c.wait_recv()

    for half in range(2):
        spread(half, 0)
    dec_copies = []
    for off in range(1, n_tok):
        copy = pltpu.make_async_remote_copy(
            src_ref=xdec.at[0],
            dst_ref=xdec.at[n_tok - off],
            send_sem=dssem.at[off],
            recv_sem=drsem.at[off],
            device_id={"tok": (me + off) % n_tok},
            device_id_type=MESH,
        )
        copy.start()
        dec_copies.append(copy)
    for half in range(2):
        wait(half, 0, 3)
        wait(half, 0, 1)
        a = send(x.at[half, 0, 3, 0], x.at[half, 0, 2, 0], axis1[half](1))
        b = send(x.at[half, 0, 1, 1], x.at[half, 0, 2, 1], axis1[half](-1))
        got[half, 0, 2] = [a, b]
        spread(half, 3)
        spread(half, 1)
    for half in range(2):
        wait(half, 3, 0)
        wait(half, 1, 0)
        relay2(half, 0)
    for half in range(2):
        wait(half, 0, 2)
        spread(half, 2)

    width = wdown.shape[0]

    def hidden_of(rows):
        both = dot_nt(rows, wgu[...])
        gate = both[:, :width]
        return (jax.nn.gelu(gate, approximate=True) * both[:, width:]).astype(BF16)

    def compute(a2):
        rows = x[:, a2].reshape(2 * 4 * 2 * Q, x.shape[-1])
        result = jnp.dot(hidden_of(rows), wdown[...], preferred_element_type=F32)
        part[:, a2] = result.astype(BF16).reshape(2, 4, 2, Q, x.shape[-1])

    load_gu.wait()
    load_down.wait()

    compute(0)
    for a1 in (3, 1):
        for half in range(2):
            wait(half, 3, a1)
            wait(half, 1, a1)
            relay2(half, a1)
    for half in range(2):
        wait(half, 3, 2)
        wait(half, 1, 2)
        relay2(half, 2)

    def group13(i, _):
        compute(3 - 2 * i)
        return 0

    lax.fori_loop(0, 2, group13, 0)
    came = {}
    for half in range(2):
        came[half, 0, 1] = send(
            part.at[half, 1, :, 1], direct.at[half, 0, :, 1], axis2[half](1)
        )
        came[half, 1, 0] = send(
            part.at[half, 3, :, 0], direct.at[half, 1, :, 0], axis2[half](-1)
        )
    for c in dec_copies:
        c.wait_recv()
    for t in range(n_tok):
        xrows[t : t + 1, :] = xdec[t].astype(F32)
    dpart = jnp.dot(
        hidden_of(xrows[...].astype(BF16)), wdown[...], preferred_element_type=F32
    )
    for t in range(n_tok):
        pdec[t] = dpart[t : t + 1, :].astype(BF16)
    dec_back = []
    for off in range(1, n_tok):
        copy = pltpu.make_async_remote_copy(
            src_ref=pdec.at[off],
            dst_ref=rdec.at[n_tok - off],
            send_sem=dssem.at[n_tok + off],
            recv_sem=drsem.at[n_tok + off],
            device_id={"tok": (me + off) % n_tok},
            device_id_type=MESH,
        )
        copy.start()
        dec_back.append(copy)

    hop = {}
    for half in range(2):
        for a1 in range(4):
            wait(half, 2, a1)
    compute(2)
    order = (2, 1, 3, 0)
    for a1 in order:
        for half in range(2):
            hop[half, 0, a1] = send(
                part.at[half, 2, a1, 0], relay.at[half, 0, a1], axis2[half](1)
            )
            hop[half, 1, a1] = send(
                part.at[half, 2, a1, 1], relay.at[half, 1, a1], axis2[half](-1)
            )
    for a1 in order:
        for half in range(2):
            hop[half, 0, a1].wait_recv()
            part[half, 1, a1, 0] = (
                part[half, 1, a1, 0].astype(F32) + relay[half, 0, a1].astype(F32)
            ).astype(BF16)
            came[half, 0, 0, a1] = send(
                part.at[half, 1, a1, 0], direct.at[half, 0, a1, 0], axis2[half](1)
            )
            hop[half, 1, a1].wait_recv()
            part[half, 3, a1, 1] = (
                part[half, 3, a1, 1].astype(F32) + relay[half, 1, a1].astype(F32)
            ).astype(BF16)
            came[half, 1, 1, a1] = send(
                part.at[half, 3, a1, 1], direct.at[half, 1, a1, 1], axis2[half](-1)
            )
    dtotal = dresid_ref[...] + pdec[0].astype(F32)
    for c in dec_back:
        c.wait_recv()
    for off in range(1, n_tok):
        dtotal = dtotal + rdec[off].astype(F32)
    dout_ref[...] = dtotal.astype(BF16)
    hop1 = {}
    came1 = {}

    def collect(half, a1):
        came[half, 0, 0, a1].wait_recv()
        came[half, 1, 1, a1].wait_recv()
        total = (
            part[half, 0, a1].astype(F32)
            + direct[half, 0, a1].astype(F32)
            + direct[half, 1, a1].astype(F32)
        )
        if a1 == 0:
            first[half] = total
        else:
            sums[half, a1] = total.astype(BF16)

    for half in range(2):
        came[half, 0, 1].wait_recv()
        came[half, 1, 0].wait_recv()
        collect(half, 2)
        hop1[half, 0] = send(sums.at[half, 2, 0], relay1.at[half, 0], axis1[half](1))
        hop1[half, 1] = send(sums.at[half, 2, 1], relay1.at[half, 1], axis1[half](-1))
    for half in range(2):
        collect(half, 1)
        came1[half, 0, 1] = send(
            sums.at[half, 1, 1], direct1.at[half, 0, 1], axis1[half](1)
        )
    for half in range(2):
        collect(half, 3)
        came1[half, 1, 0] = send(
            sums.at[half, 3, 0], direct1.at[half, 1, 0], axis1[half](-1)
        )
    for half in range(2):
        hop1[half, 0].wait_recv()
        sums[half, 1, 0] = (
            sums[half, 1, 0].astype(F32) + relay1[half, 0].astype(F32)
        ).astype(BF16)
        came1[half, 0, 0] = send(
            sums.at[half, 1, 0], direct1.at[half, 0, 0], axis1[half](1)
        )
        hop1[half, 1].wait_recv()
        sums[half, 3, 1] = (
            sums[half, 3, 1].astype(F32) + relay1[half, 1].astype(F32)
        ).astype(BF16)
        came1[half, 1, 1] = send(
            sums.at[half, 3, 1], direct1.at[half, 1, 1], axis1[half](-1)
        )
    for half in range(2):
        collect(half, 0)
    for half in range(2):
        for side in range(2):
            for q in range(2):
                came1[half, side, q].wait_recv()
        out_ref[half * 2 : half * 2 + 2] = (
            resid_ref[half * 2 : half * 2 + 2]
            + first[half]
            + direct1[half, 0].astype(F32)
            + direct1[half, 1].astype(F32)
        ).astype(BF16)
    for c in sent + dec_copies + dec_back:
        c.wait_send()


FFN_SENDS = 2 * (2 + 2 + 8 + 8 + 2 + 16 + 6)


def ffn(block, drow, resid, dresid, wgu, wdown, n_tok):
    width = block.shape[-1]
    vmem = pl.BlockSpec(memory_space=pltpu.VMEM)
    hbm = pl.BlockSpec(memory_space=pl.ANY)
    return pl.pallas_call(
        ffn_kernel,
        out_shape=(
            jax.ShapeDtypeStruct(block.shape, BF16),
            jax.ShapeDtypeStruct(drow.shape, BF16),
        ),
        in_specs=[vmem, vmem, vmem, vmem, hbm, hbm],
        out_specs=(vmem, vmem),
        scratch_shapes=[
            pltpu.VMEM(wgu.shape, BF16),
            pltpu.VMEM(wdown.shape, BF16),
            pltpu.VMEM((2, 4, 4, 2, Q, width), BF16),
            pltpu.VMEM((2, 4, 4, 2, Q, width), BF16),
            pltpu.VMEM((2, 2, 4, Q, width), BF16),
            pltpu.VMEM((2, 2, 4, 2, Q, width), BF16),
            pltpu.VMEM((2, 2, Q, width), F32),
            pltpu.VMEM((2, 4, 2, Q, width), BF16),
            pltpu.VMEM((2, 2, Q, width), BF16),
            pltpu.VMEM((2, 2, 2, Q, width), BF16),
            pltpu.VMEM((n_tok, 1, width), BF16),
            pltpu.VMEM((n_tok, width), F32),
            pltpu.VMEM((n_tok, 1, width), BF16),
            pltpu.VMEM((n_tok, 1, width), BF16),
            pltpu.SemaphoreType.DMA((5,)),
            pltpu.SemaphoreType.DMA((FFN_SENDS,)),
            pltpu.SemaphoreType.DMA((FFN_SENDS,)),
            pltpu.SemaphoreType.DMA((2 * n_tok,)),
            pltpu.SemaphoreType.DMA((2 * n_tok,)),
        ],
        compiler_params=pltpu.CompilerParams(
            collective_id=1, has_side_effects=True, vmem_limit_bytes=56 * 1024 * 1024
        ),
        name="ffn",
    )(block, drow, resid, dresid, wgu, wdown)


def project_kernel(
    states,
    dstates,
    gain_ref,
    w_hbm,
    homes,
    out_ref,
    dec_ref,
    w,
    normed,
    units,
    outgoing,
    pdec,
    wsem,
    lsem,
    ssem,
    rsem,
    dssem,
    drsem,
):
    me = lax.axis_index("tok")
    n_tok = lax.axis_size("tok")
    requests, positions, width = states.shape
    features = w.shape[2]
    per = features // HD
    barrier = pltpu.get_barrier_semaphore()
    for off in range(1, n_tok):
        pl.semaphore_signal(
            barrier, inc=1, device_id={"tok": (me + off) % n_tok}, device_id_type=MESH
        )
    load = pltpu.make_async_copy(w_hbm, w, wsem)
    load.start()
    gain = gain_ref[...]
    pdec_rows = rms_norm(dstates[...], gain)
    lane = lax.broadcasted_iota(jnp.int32, (positions, PAGE), 1)
    half = positions // 2

    strip = 64

    def norm(i, _):
        at = pl.ds(pl.multiple_of(i % (positions // strip) * strip, strip), strip)
        normed[i] = rms_norm(states[i // (positions // strip), at, :], gain)
        return 0

    lax.fori_loop(0, requests * positions // strip, norm, 0)
    load.wait()
    pl.semaphore_wait(barrier, n_tok - 1)
    for which in range(3):
        pdec[:, which * features : (which + 1) * features] = jnp.dot(
            pdec_rows, w[which], preferred_element_type=F32
        ).astype(BF16)
    copies = []
    for off in range(1, n_tok):
        copy = pltpu.make_async_remote_copy(
            src_ref=pdec,
            dst_ref=dec_ref.at[me],
            send_sem=dssem.at[off],
            recv_sem=drsem.at[off],
            device_id={"tok": (me + off) % n_tok},
            device_id_type=MESH,
        )
        copy.start()
        copies.append(copy)

    def project(r, _):
        rows = normed[pl.ds(r * (positions // strip), positions // strip)].reshape(
            positions, width
        )
        q, k, v = (jnp.dot(rows, w[i], preferred_element_type=F32) for i in range(3))
        for j in range(per):
            at = j // 2 * PAGE
            qb, kb, vb = (a[:, at : at + PAGE] for a in (q, k, v))
            if j % 2 == 0:
                both = jnp.where(lane < HD, kb, pltpu.roll(vb, HD, 1))
                pair = jnp.where(lane[:half] < HD, qb[:half], pltpu.roll(qb[half:], HD, 1))
            else:
                both = jnp.where(lane < HD, pltpu.roll(kb, HD, 1), vb)
                pair = jnp.where(lane[:half] < HD, pltpu.roll(qb[:half], HD, 1), qb[half:])
            units[r * per + j, :positions, :] = both.astype(BF16)
            units[r * per + j, positions:, :] = pair.astype(BF16)
        return 0

    lax.fori_loop(0, requests, project, 0)
    for off in range(n_tok):
        target = (me + off) % n_tok
        unit = jnp.int32(0)
        for u in range(requests * per):
            unit = jnp.where(homes[u] == target, u, unit)
        if off == 0:
            outgoing[0] = units[unit]
            own = pltpu.make_async_copy(outgoing.at[0], out_ref.at[me], lsem.at[0])
            own_dec = pltpu.make_async_copy(pdec, dec_ref.at[me], lsem.at[1])
            own.start()
            own_dec.start()
            continue
        outgoing[off] = units[unit]
        copy = pltpu.make_async_remote_copy(
            src_ref=outgoing.at[off],
            dst_ref=out_ref.at[me],
            send_sem=ssem.at[off],
            recv_sem=rsem.at[off],
            device_id={"tok": target},
            device_id_type=MESH,
        )
        copy.start()
        copies.append(copy)
    own.wait()
    own_dec.wait()
    for copy in copies:
        copy.wait()


def project(states, dstates, gain, w, homes, n_tok):
    requests, positions, width = states.shape
    hosted = dstates.shape[0]
    features = w.shape[2]
    vmem = pl.BlockSpec(memory_space=pltpu.VMEM)
    smem = pl.BlockSpec(memory_space=pltpu.SMEM)
    packed = positions // 2 * 3
    units = requests * features // HD
    return pl.pallas_call(
        project_kernel,
        out_shape=(
            jax.ShapeDtypeStruct((n_tok, packed, 2 * HD), BF16),
            jax.ShapeDtypeStruct((n_tok, hosted, 3 * features), BF16),
        ),
        in_specs=[vmem, vmem, vmem, pl.BlockSpec(memory_space=pl.ANY), smem],
        out_specs=(vmem, vmem),
        scratch_shapes=[
            pltpu.VMEM(w.shape, BF16),
            pltpu.VMEM((requests * positions // 64, 64, width), BF16),
            pltpu.VMEM((units, packed, 2 * HD), BF16),
            pltpu.VMEM((n_tok, packed, 2 * HD), BF16),
            pltpu.VMEM((hosted, 3 * features), BF16),
            pltpu.SemaphoreType.DMA,
            pltpu.SemaphoreType.DMA((2,)),
            pltpu.SemaphoreType.DMA((n_tok,)),
            pltpu.SemaphoreType.DMA((n_tok,)),
            pltpu.SemaphoreType.DMA((n_tok,)),
            pltpu.SemaphoreType.DMA((n_tok,)),
        ],
        compiler_params=pltpu.CompilerParams(
            collective_id=2, has_side_effects=True, vmem_limit_bytes=56 * 1024 * 1024
        ),
        name="project",
    )(states, dstates, gain, w, homes)


def mix_kernel(
    attn,
    dattn,
    states_hbm,
    dstates,
    gain_ref,
    w_hbm,
    homes,
    dhomes,
    normed_ref,
    dnormed_ref,
    resid_ref,
    dresid_ref,
    w,
    own,
    drows,
    got,
    gdec,
    gdec_rows,
    left,
    dleft,
    part,
    pdec,
    rdec,
    pair,
    sums,
    relay,
    direct,
    lsem,
    tssem,
    trsem,
    dssem,
    drsem,
    hssem,
    hrsem,
    ssem,
    rsem,
):
    me = lax.axis_index("tok")
    n_tok = lax.axis_size("tok")
    head = lax.axis_index("head")
    n_head = lax.axis_size("head")
    my_x, core = head // 2, head % 2
    n_x = n_head // 2
    requests, rows, width = own.shape
    positions = rows * n_head
    half = positions // 2
    hosted = dattn.shape[0]
    barrier = pltpu.get_barrier_semaphore()
    for off in range(1, n_tok):
        pl.semaphore_signal(
            barrier, inc=1, device_id={"tok": (me + off) % n_tok}, device_id_type=MESH
        )
    for off in range(1, n_head):
        pl.semaphore_signal(
            barrier, inc=1, device_id={"head": (head + off) % n_head}, device_id_type=MESH
        )
    load_w = pltpu.make_async_copy(w_hbm, w, lsem.at[0])
    load_own = pltpu.make_async_copy(
        states_hbm.at[:, pl.ds(pl.multiple_of(head * rows, rows), rows), :], own, lsem.at[1]
    )
    keep = pltpu.make_async_copy(attn.at[me], got.at[me], lsem.at[2])
    keep_dec = pltpu.make_async_copy(dattn, gdec.at[me], lsem.at[3])
    local = [load_w, load_own, keep, keep_dec]
    for c in local:
        c.start()
    pl.semaphore_wait(barrier, n_tok + n_head - 2)
    sends = []
    for off in range(1, n_tok):
        target = (me + off) % n_tok
        for source, dest, a, b in (
            (attn.at[target], got.at[me], tssem, trsem),
            (dattn, gdec.at[me], dssem, drsem),
        ):
            copy = pltpu.make_async_remote_copy(
                src_ref=source,
                dst_ref=dest,
                send_sem=a.at[off],
                recv_sem=b.at[off],
                device_id={"tok": target},
                device_id_type=MESH,
            )
            copy.start()
            sends.append(copy)
    drows[...] = dstates[...].astype(F32)
    for c in local:
        c.wait()
    for c in sends:
        c.wait_recv()
    lane = lax.broadcasted_iota(jnp.int32, (half, PAGE), 1)
    per = w.shape[0] // HD
    for r in range(requests):
        for j in range(0, per, 2):
            a = got[homes[r * per + j]].astype(F32)
            b = got[homes[r * per + j + 1]].astype(F32)
            low = jnp.where(lane < HD, a, pltpu.roll(b, HD, 1))
            high = jnp.where(lane < HD, pltpu.roll(a, HD, 1), b)
            cols = slice(j // 2 * PAGE, (j // 2 + 1) * PAGE)
            left[r, :half, cols] = low.astype(BF16)
            left[r, half:, cols] = high.astype(BF16)
    for t in range(n_tok):
        gdec_rows[t * hosted : (t + 1) * hosted, :] = gdec[t].astype(F32)
    for i in range(hosted):
        dleft[i : i + 1, :] = gdec_rows[pl.ds(dhomes[me * hosted + i], 1), :]

    def project(r, _):
        result = jnp.dot(left[r], w[...], preferred_element_type=F32).astype(BF16)
        for k in range(n_head):
            part[k % 2, r, k // 2] = result[k * rows : (k + 1) * rows]
        return 0

    lax.fori_loop(0, requests, project, 0)
    used = [0]
    ring = []

    def send(source, target, device):
        i = used[0]
        used[0] += 1
        copy = pltpu.make_async_remote_copy(
            src_ref=source,
            dst_ref=target,
            send_sem=ssem.at[i],
            recv_sem=rsem.at[i],
            device_id={"head": device},
            device_id_type=MESH,
        )
        copy.start()
        ring.append(copy)
        return copy

    partner = my_x * 2 + 1 - core
    up = (my_x + 1) % n_x * 2 + core
    down = (my_x + n_x - 1) % n_x * 2 + core
    order = (2, 1, 3, 0)
    paired = {}
    for dx in order:
        paired[dx] = send(
            part.at[1 - core, :, (my_x + dx) % n_x], pair.at[dx], partner
        )
    dresult = jnp.dot(dleft[...].astype(BF16), w[...], preferred_element_type=F32)
    for k in range(n_head):
        pdec[k] = dresult[k : k + 1, :].astype(BF16)
    for off in range(1, n_head):
        copy = pltpu.make_async_remote_copy(
            src_ref=pdec.at[(head + off) % n_head],
            dst_ref=rdec.at[n_head - off],
            send_sem=hssem.at[off],
            recv_sem=hrsem.at[off],
            device_id={"head": (head + off) % n_head},
            device_id_type=MESH,
        )
        copy.start()
        sends.append(copy)
    hop = {}
    came = {}
    for dx in order:
        paired[dx].wait_recv()
        total = part[core, :, (my_x + dx) % n_x].astype(F32) + pair[dx].astype(F32)
        if dx == 0:
            resid_ref[...] = total + own[...].astype(F32)
        else:
            sums[dx] = total.astype(BF16)
        if dx == 2:
            for i in range(2):
                hop[0, i] = send(sums.at[2, i], relay.at[0, i], up)
                hop[1, i] = send(sums.at[2, 2 + i], relay.at[1, i], down)
        if dx == 1:
            came[0, 1] = send(sums.at[1, 2:4], direct.at[0, 2:4], up)
        if dx == 3:
            came[1, 0] = send(sums.at[3, 0:2], direct.at[1, 0:2], down)
    for i in range(2):
        hop[0, i].wait_recv()
        sums[1, i] = (sums[1, i].astype(F32) + relay[0, i].astype(F32)).astype(BF16)
        came[0, 0, i] = send(sums.at[1, i], direct.at[0, i], up)
        hop[1, i].wait_recv()
        sums[3, 2 + i] = (sums[3, 2 + i].astype(F32) + relay[1, i].astype(F32)).astype(BF16)
        came[1, 1, i] = send(sums.at[3, 2 + i], direct.at[1, 2 + i], down)
    gain = gain_ref[...]
    dtotal = drows[pl.ds(head, 1), :] + pdec[head].astype(F32)
    for c in sends[2 * (n_tok - 1) :]:
        c.wait_recv()
    for off in range(1, n_head):
        dtotal = dtotal + rdec[off].astype(F32)
    dresid_ref[...] = dtotal
    dnormed_ref[...] = rms_norm(dtotal, gain)
    for c in came.values():
        c.wait_recv()
    for r in range(requests):
        total = resid_ref[r] + direct[0, r].astype(F32) + direct[1, r].astype(F32)
        resid_ref[r] = total
        normed_ref[r] = rms_norm(total, gain)
    for c in sends + ring:
        c.wait_send()


def mix(attn, dattn, states, dstates, gain, w, homes, dhomes, n_head):
    requests, positions, width = states.shape
    n_tok, packed, lanes = attn.shape
    hosted = dattn.shape[0]
    rows = positions // n_head
    n_x = n_head // 2
    vmem = pl.BlockSpec(memory_space=pltpu.VMEM)
    smem = pl.BlockSpec(memory_space=pltpu.SMEM)
    hbm = pl.BlockSpec(memory_space=pl.ANY)
    sem = pltpu.SemaphoreType.DMA
    ring = 4 + 4 + 2 + 4
    return pl.pallas_call(
        mix_kernel,
        out_shape=(
            jax.ShapeDtypeStruct((requests, rows, width), BF16),
            jax.ShapeDtypeStruct((1, width), BF16),
            jax.ShapeDtypeStruct((requests, rows, width), F32),
            jax.ShapeDtypeStruct((1, width), F32),
        ),
        in_specs=[vmem, vmem, hbm, vmem, vmem, hbm, smem, smem],
        out_specs=(vmem, vmem, vmem, vmem),
        scratch_shapes=[
            pltpu.VMEM(w.shape, BF16),
            pltpu.VMEM((requests, rows, width), BF16),
            pltpu.VMEM((hosted, width), F32),
            pltpu.VMEM((n_tok, packed, lanes), BF16),
            pltpu.VMEM((n_tok, hosted, w.shape[0]), BF16),
            pltpu.VMEM((n_tok * hosted, w.shape[0]), F32),
            pltpu.VMEM((requests, positions, w.shape[0]), BF16),
            pltpu.VMEM((hosted, w.shape[0]), F32),
            pltpu.VMEM((2, requests, n_x, rows, width), BF16),
            pltpu.VMEM((n_head, 1, width), BF16),
            pltpu.VMEM((n_head, 1, width), BF16),
            pltpu.VMEM((n_x, requests, rows, width), BF16),
            pltpu.VMEM((n_x, requests, rows, width), BF16),
            pltpu.VMEM((2, 2, rows, width), BF16),
            pltpu.VMEM((2, requests, rows, width), BF16),
            sem((4,)),
            sem((n_tok,)),
            sem((n_tok,)),
            sem((n_tok,)),
            sem((n_tok,)),
            sem((n_head,)),
            sem((n_head,)),
            sem((ring,)),
            sem((ring,)),
        ],
        compiler_params=pltpu.CompilerParams(
            collective_id=3, has_side_effects=True, vmem_limit_bytes=56 * 1024 * 1024
        ),
        name="mix",
    )(attn, dattn, states, dstates, gain, w, homes, dhomes)


def keep_kernel(left, right, left_out, right_out):
    left_out[...] = left[...]
    right_out[...] = right[...]


def keep(left, right):
    vmem = pl.BlockSpec(memory_space=pltpu.VMEM)
    return pl.pallas_call(
        keep_kernel,
        out_shape=tuple(jax.ShapeDtypeStruct(a.shape, a.dtype) for a in (left, right)),
        in_specs=[vmem, vmem],
        out_specs=(vmem, vmem),
        name="keep",
    )(left, right)


def shards(
    prefill_states,
    decode_states,
    attn_gain,
    w_qkv,
    w_out,
    ffn_gain,
    w_gate_up,
    w_down,
    prefill_pool,
    prefill_pages,
    prefill_lengths,
    prefill_home,
    decode_pool,
    decode_pages,
    decode_lengths,
    decode_home,
):
    n_tok = lax.axis_size("tok")
    n_head = lax.axis_size("head")
    width = prefill_states.shape[2]
    arrived, arrived_dec = project(
        prefill_states,
        decode_states,
        attn_gain.reshape(1, -1),
        jnp.transpose(w_qkv, (1, 0, 2)),
        prefill_home,
        n_tok,
    )
    attn, dattn = attention(
        prefill_pages,
        prefill_lengths,
        prefill_home,
        decode_pages,
        decode_lengths,
        decode_home,
        arrived,
        arrived_dec,
        prefill_pool.reshape(-1, 2 * HD),
        decode_pool.reshape(-1, decode_pool.shape[2]),
    )
    normed, dnormed, resid, dresid = mix(
        attn,
        dattn,
        prefill_states,
        decode_states,
        ffn_gain.reshape(1, -1),
        w_out,
        prefill_home,
        decode_home,
        n_head,
    )
    prefill_out, decode_out = ffn(
        normed,
        dnormed,
        resid,
        dresid,
        jnp.transpose(w_gate_up, (1, 2, 0)).reshape(-1, width),
        w_down,
        n_tok,
    )
    return keep(prefill_out, decode_out)


def solution(mesh):
    placed = (
        P(None, "tok", None),
        P("tok", None),
        P(),
        P(None, None, "head"),
        P("head", None),
        P(),
        P(None, None, "tok"),
        P("tok", None),
        P("tok", None, "head"),
        P("tok", None),
        P(),
        P(),
        P("tok", None, "head"),
        P("tok", None),
        P("tok"),
        P(),
    )
    return jax.shard_map(
        shards,
        mesh=mesh,
        in_specs=placed,
        out_specs=(P(None, ("tok", "head"), None), P(("tok", "head"), None)),
        check_vma=False,
    )
```

```python
import jax
import jax.numpy as jnp
from jax import lax
from jax.experimental import pallas as pl
from jax.experimental.pallas import tpu as pltpu
from jax.sharding import PartitionSpec as P

HD = 64
EPSILON = 1e-06
SCALE = 0.125
MASKED = -1e30
PAGE = 128
F32 = jnp.float32
BF16 = jnp.bfloat16


def rms_norm(rows, gain):
    values = rows.astype(F32)
    inverse = lax.rsqrt(jnp.mean(values * values, axis=-1, keepdims=True) + EPSILON)
    return (values * inverse * gain).astype(BF16)


def dot_nt(left, right):
    return lax.dot_general(left, right, (((1,), (1,)), ((), ())), preferred_element_type=F32)


QB = 512
KC = 512


def attention_kernel(
    pages,
    lengths,
    homes,
    dpages,
    dlens,
    dhomes,
    arrived,
    arrived_dec,
    pool_ref,
    dpool_hbm,
    out_ref,
    dout_ref,
    keys,
    vals,
    query,
    score,
    top_run,
    top,
    acc,
    dpool,
    dbias,
    dscore,
    drows,
    mine_ref,
    count,
    owner,
    dcount,
    anchor,
    sem,
):
    me = lax.axis_index("tok")
    n_tok = arrived.shape[0]
    positions = arrived.shape[1] // 3 * 2
    stretch = n_tok * positions
    span = pool_ref.shape[0]
    npages = span // PAGE
    dspan = dpool_hbm.shape[0]
    dnpages = dspan // PAGE
    slots, dmax = dpages.shape
    copy = pltpu.make_async_copy(dpool_hbm, dpool, sem)
    copy.start()

    my_unit = jnp.int32(0)
    for u in range(n_tok):
        my_unit = jnp.where(homes[u] == me, u, my_unit)
    length = lengths[my_unit // (n_tok // lengths.shape[0])]

    def count_page(i, _):
        count[pages[0, i]] = jnp.clip(length - i * PAGE, 0, PAGE)
        return 0

    lax.fori_loop(0, npages, count_page, 0)

    def zero_page(i, _):
        dcount[i] = 0
        owner[i] = 0
        return 0

    lax.fori_loop(0, dnpages, zero_page, 0)
    for s in range(slots):
        used = (dlens[s] + PAGE - 1) // PAGE

        def own_page(i, _):
            page = dpages[s, i]
            owner[page] = s
            dcount[page] = jnp.minimum(dlens[s] - i * PAGE, PAGE)
            return 0

        lax.fori_loop(0, used, own_page, 0)

    lane = lax.broadcasted_iota(jnp.int32, (PAGE, PAGE), 1)
    row = lax.broadcasted_iota(jnp.int32, (PAGE, PAGE), 0)

    def fill_cached(i, _):
        where_at = pl.ds(pl.multiple_of(i * PAGE, PAGE), PAGE)
        page = pool_ref[where_at, :].astype(F32)
        bias = jnp.where((lane == HD) & (row >= count[i]), MASKED, 0.0)
        keys[where_at, :] = jnp.where(lane < HD, page, bias).astype(BF16)
        vals[where_at, :] = jnp.where(lane < HD, 1.0, page).astype(BF16)
        return 0

    lax.fori_loop(0, npages, fill_cached, 0, unroll=4)

    half = PAGE // 2

    def fill_own(i, _):
        target = pl.ds(pl.multiple_of(span + i * PAGE, PAGE), PAGE)
        both = arrived[i, :PAGE, :].astype(F32)
        keys[target, :] = jnp.where(lane < HD, both, 0.0).astype(BF16)
        vals[target, :] = jnp.where(lane < HD, 1.0, both).astype(BF16)
        packed = arrived[i, PAGE:, :].astype(F32) * SCALE
        flag = jnp.where(lane[:half] == HD, 1.0, 0.0)
        low = jnp.where(lane[:half] < HD, packed, flag)
        high = jnp.where(lane[:half] < HD, pltpu.roll(packed, HD, 1), flag)
        at_low = pl.ds(pl.multiple_of(i * PAGE, PAGE), half)
        at_high = pl.ds(pl.multiple_of(i * PAGE + half, half), half)
        query[at_low, :] = low.astype(BF16)
        query[at_high, :] = high.astype(BF16)
        return 0

    lax.fori_loop(0, stretch // PAGE, fill_own, 0, unroll=4)

    def fold(s):
        best = s[:, :PAGE]
        for j in range(1, s.shape[1] // PAGE):
            best = jnp.maximum(best, s[:, j * PAGE : (j + 1) * PAGE])
        return best

    def make_scores(i, c, diagonal):
        rows = query[i * QB : (i + 1) * QB, :]
        s = dot_nt(rows, keys[pl.ds(pl.multiple_of(c * KC, KC), KC), :])
        if diagonal:
            r = lax.broadcasted_iota(jnp.int32, (QB, KC), 0)
            k = lax.broadcasted_iota(jnp.int32, (QB, KC), 1)
            s = jnp.where(k <= r, s, MASKED)
        score[i % 2, c] = s
        top_run[i % 2] = jnp.maximum(top_run[i % 2], fold(s))

    def finish_top(i):
        best = jnp.max(top_run[i % 2], axis=1, keepdims=True)
        top[i % 2] = jnp.broadcast_to(best, (QB, PAGE))

    def mix(i, c):
        best = top[i % 2]
        s = score[i % 2, c]
        p = jnp.exp(s - jnp.concatenate([best] * (KC // PAGE), axis=1)).astype(BF16)
        acc[...] += jnp.dot(
            p, vals[pl.ds(pl.multiple_of(c * KC, KC), KC), :], preferred_element_type=F32
        )

    blocks = stretch // QB
    cached_chunks = span // KC

    top_run[0] = jnp.full((QB, PAGE), MASKED, F32)

    def first(c, _):
        make_scores(0, c, False)
        return 0

    lax.fori_loop(0, cached_chunks, first, 0, unroll=4)
    make_scores(0, cached_chunks, True)
    finish_top(0)
    for i in range(blocks):
        acc[...] = jnp.zeros_like(acc)
        chunks = cached_chunks + i + 1
        if i + 1 < blocks:
            top_run[(i + 1) % 2] = jnp.full((QB, PAGE), MASKED, F32)

            def both(c, _, i=i):
                make_scores(i + 1, c, False)
                mix(i, c)
                return 0

            lax.fori_loop(0, chunks, both, 0, unroll=4)
            make_scores(i + 1, chunks, True)
            finish_top(i + 1)
        else:

            def last(c, _, i=i):
                mix(i, c)
                return 0

            lax.fori_loop(0, chunks, last, 0, unroll=4)
        total = acc[...]
        result = pltpu.roll(total, HD, 1) / total
        for j in range(QB // PAGE):
            tile = result[j * PAGE : (j + 1) * PAGE]
            out_ref[i * (QB // PAGE) + j] = jnp.where(
                lane[:half] < HD, tile[:half], pltpu.roll(tile[half:], HD, 1)
            ).astype(BF16)

    slot_row = lax.broadcasted_iota(jnp.int32, (slots, PAGE), 0)
    slot_lane = lax.broadcasted_iota(jnp.int32, (slots, PAGE), 1)

    def fill_bias(i, _):
        seen = (slot_row == owner[i]) & (slot_lane < dcount[i])
        dbias[i] = jnp.where(seen, 0.0, MASKED)
        return 0

    lax.fori_loop(0, dnpages, fill_bias, 0)
    for t in range(n_tok):
        drows[t * slots : (t + 1) * slots, :] = arrived_dec[t].astype(F32)

    def find(r, _):
        slot = dhomes[r] - me * slots

        @pl.when((slot >= 0) & (slot < slots))
        def _():
            anchor[slot] = r

        return 0

    lax.fori_loop(0, dhomes.shape[0], find, 0)
    for s in range(slots):
        mine_ref[s : s + 1, :] = drows[pl.ds(anchor[s], 1), :]
    copy.wait()
    rows = mine_ref[...]
    heads = rows.shape[1] // (3 * HD)
    step = 1024
    per = step // PAGE
    for h in range(heads):
        block = h // 2 * PAGE
        width = heads * HD

        def part(which, left):
            piece = rows[:, which * width + block : which * width + block + PAGE]
            return pltpu.roll(piece, HD, 1) if (h % 2 == 1) == left else piece

        q = jnp.where(slot_lane < HD, part(0, True) * SCALE, 0.0)
        k = part(1, True)
        v = part(2, False)
        own = jnp.sum(q * k, axis=1, keepdims=True)
        qb = q.astype(BF16)
        best = jnp.broadcast_to(own, (slots, PAGE))
        for c in range(dspan // step):
            s = dot_nt(qb, dpool[c * step : (c + 1) * step, h * PAGE : (h + 1) * PAGE])
            s = s + jnp.concatenate([dbias[c * per + j] for j in range(per)], axis=1)
            dscore[c] = s
            best = jnp.maximum(best, fold(s))
        best = jnp.max(best, axis=1, keepdims=True)
        own_weight = jnp.exp(own - best)
        sums = jnp.zeros((slots, PAGE), F32)
        mixed = jnp.zeros((slots, PAGE), F32)
        for c in range(dspan // step):
            p = jnp.exp(dscore[c] - best)
            for j in range(per):
                sums = sums + p[:, j * PAGE : (j + 1) * PAGE]
            mixed = mixed + jnp.dot(
                p.astype(BF16),
                dpool[c * step : (c + 1) * step, h * PAGE : (h + 1) * PAGE],
                preferred_element_type=F32,
            )
        total = jnp.sum(sums, axis=1, keepdims=True) + own_weight
        mixed = (mixed + own_weight.astype(BF16).astype(F32) * v) / total
        dout_ref[:, h * HD : (h + 1) * HD] = pltpu.roll(mixed, HD, 1)[:, :HD].astype(BF16)


def attention(
    pages, lengths, homes, dpages, dlens, dhomes, arrived, arrived_dec, pool, dpool
):
    n_tok, packed, lanes = arrived.shape
    positions = packed // 3 * 2
    stretch = n_tok * positions
    span = pool.shape[0]
    dspan, dwidth = dpool.shape
    slots, dcols = arrived_dec.shape[1:]
    keys = span + stretch
    vmem = pl.BlockSpec(memory_space=pltpu.VMEM)
    smem = pl.BlockSpec(memory_space=pltpu.SMEM)
    return pl.pallas_call(
        attention_kernel,
        out_shape=(
            jax.ShapeDtypeStruct((n_tok, positions // 2, lanes), BF16),
            jax.ShapeDtypeStruct((slots, dcols // 3), BF16),
        ),
        in_specs=[smem] * 6 + [vmem] * 3 + [pl.BlockSpec(memory_space=pl.ANY)],
        out_specs=(vmem, vmem),
        scratch_shapes=[
            pltpu.VMEM((keys, 2 * HD), BF16),
            pltpu.VMEM((keys, 2 * HD), BF16),
            pltpu.VMEM((stretch, 2 * HD), BF16),
            pltpu.VMEM((2, keys // KC, QB, KC), F32),
            pltpu.VMEM((2, QB, PAGE), F32),
            pltpu.VMEM((2, QB, PAGE), F32),
            pltpu.VMEM((QB, PAGE), F32),
            pltpu.VMEM((dspan, dwidth), BF16),
            pltpu.VMEM((dspan // PAGE, slots, PAGE), F32),
            pltpu.VMEM((dspan // 1024, slots, 1024), F32),
            pltpu.VMEM((n_tok * slots, dcols), F32),
            pltpu.VMEM((slots, dcols), F32),
            pltpu.SMEM((span // PAGE,), jnp.int32),
            pltpu.SMEM((dspan // PAGE,), jnp.int32),
            pltpu.SMEM((dspan // PAGE,), jnp.int32),
            pltpu.SMEM((slots,), jnp.int32),
            pltpu.SemaphoreType.DMA,
        ],
        compiler_params=pltpu.CompilerParams(vmem_limit_bytes=62 * 1024 * 1024),
        name="attention",
    )(pages, lengths, homes, dpages, dlens, dhomes, arrived, arrived_dec, pool, dpool)


MESH = pl.DeviceIdType.MESH
Q = 16


def ffn_kernel(
    block_ref,
    drow_ref,
    resid_ref,
    dresid_ref,
    wgu_hbm,
    wdown_hbm,
    out_ref,
    dout_ref,
    wgu,
    wdown,
    x,
    part,
    relay,
    direct,
    first,
    sums,
    relay1,
    direct1,
    xdec,
    xrows,
    pdec,
    rdec,
    wsem,
    ssem,
    rsem,
    dssem,
    drsem,
):
    me = lax.axis_index("tok")
    n_tok = lax.axis_size("tok")
    my_y, my_z = me // 4, me % 4
    barrier = pltpu.get_barrier_semaphore()
    for off in range(1, n_tok):
        pl.semaphore_signal(
            barrier,
            inc=1,
            device_id={"tok": (me + off) % n_tok},
            device_id_type=MESH,
        )
    load_gu = pltpu.make_async_copy(wgu_hbm, wgu, wsem.at[0])
    load_down = pltpu.make_async_copy(wdown_hbm, wdown, wsem.at[1])
    load_own = [
        pltpu.make_async_copy(
            block_ref.at[pl.ds(half * 2, 2)], x.at[half, 0, 0], wsem.at[2 + half]
        )
        for half in range(2)
    ]
    load_dec = pltpu.make_async_copy(drow_ref, xdec.at[0], wsem.at[4])
    for c in load_own:
        c.start()
    load_dec.start()
    load_gu.start()
    load_down.start()

    def along_z(step):
        return {"tok": my_y * 4 + (my_z + step + 4) % 4}

    def along_y(step):
        return {"tok": (my_y + step + 4) % 4 * 4 + my_z}

    axis1 = (along_z, along_y)
    axis2 = (along_y, along_z)
    used = [0]

    def send(source, target, device):
        i = used[0]
        used[0] += 1
        copy = pltpu.make_async_remote_copy(
            src_ref=source,
            dst_ref=target,
            send_sem=ssem.at[i],
            recv_sem=rsem.at[i],
            device_id=device,
            device_id_type=MESH,
        )
        copy.start()
        sent.append(copy)
        return copy

    sent = []
    for c in load_own:
        c.wait()
    load_dec.wait()
    pl.semaphore_wait(barrier, n_tok - 1)

    got = {}
    for half in range(2):
        own = x.at[half, 0, 0]
        got[half, 0, 3] = [send(own, x.at[half, 0, 3], axis1[half](1))]
        got[half, 0, 1] = [send(own, x.at[half, 0, 1], axis1[half](-1))]

    def spread(half, a1):
        own = x.at[half, 0, a1]
        got[half, 3, a1] = [send(own, x.at[half, 3, a1], axis2[half](1))]
        got[half, 1, a1] = [send(own, x.at[half, 1, a1], axis2[half](-1))]

    def relay2(half, a1):
        a = send(x.at[half, 3, a1, 0], x.at[half, 2, a1, 0], axis2[half](1))
        b = send(x.at[half, 1, a1, 1], x.at[half, 2, a1, 1], axis2[half](-1))
        got[half, 2, a1] = [a, b]

    def wait(half, a2, a1):
        for c in got[half, a2, a1]:
            c.wait_recv()

    for half in range(2):
        spread(half, 0)
    dec_copies = []
    for off in range(1, n_tok):
        copy = pltpu.make_async_remote_copy(
            src_ref=xdec.at[0],
            dst_ref=xdec.at[n_tok - off],
            send_sem=dssem.at[off],
            recv_sem=drsem.at[off],
            device_id={"tok": (me + off) % n_tok},
            device_id_type=MESH,
        )
        copy.start()
        dec_copies.append(copy)
    for half in range(2):
        wait(half, 0, 3)
        wait(half, 0, 1)
        a = send(x.at[half, 0, 3, 0], x.at[half, 0, 2, 0], axis1[half](1))
        b = send(x.at[half, 0, 1, 1], x.at[half, 0, 2, 1], axis1[half](-1))
        got[half, 0, 2] = [a, b]
        spread(half, 3)
        spread(half, 1)
    for half in range(2):
        wait(half, 3, 0)
        wait(half, 1, 0)
        relay2(half, 0)
    for half in range(2):
        wait(half, 0, 2)
        spread(half, 2)

    width = wdown.shape[0]

    def hidden_of(rows):
        both = dot_nt(rows, wgu[...])
        gate = both[:, :width]
        return (jax.nn.gelu(gate, approximate=True) * both[:, width:]).astype(BF16)

    def compute(a2):
        rows = x[:, a2].reshape(2 * 4 * 2 * Q, x.shape[-1])
        result = jnp.dot(hidden_of(rows), wdown[...], preferred_element_type=F32)
        part[:, a2] = result.astype(BF16).reshape(2, 4, 2, Q, x.shape[-1])

    load_gu.wait()
    load_down.wait()

    compute(0)
    for a1 in (3, 1):
        for half in range(2):
            wait(half, 3, a1)
            wait(half, 1, a1)
            relay2(half, a1)
    for half in range(2):
        wait(half, 3, 2)
        wait(half, 1, 2)
        relay2(half, 2)

    came = {}
    for a2, side, q, step in ((1, 0, 1, 1), (3, 1, 0, -1)):
        compute(a2)
        for half in range(2):
            came[half, side, q] = send(
                part.at[half, a2, :, q], direct.at[half, side, :, q], axis2[half](step)
            )
    for c in dec_copies:
        c.wait_recv()
    for t in range(n_tok):
        xrows[t : t + 1, :] = xdec[t].astype(F32)
    dpart = jnp.dot(
        hidden_of(xrows[...].astype(BF16)), wdown[...], preferred_element_type=F32
    )
    for t in range(n_tok):
        pdec[t] = dpart[t : t + 1, :].astype(BF16)
    dec_back = []
    for off in range(1, n_tok):
        copy = pltpu.make_async_remote_copy(
            src_ref=pdec.at[off],
            dst_ref=rdec.at[n_tok - off],
            send_sem=dssem.at[n_tok + off],
            recv_sem=drsem.at[n_tok + off],
            device_id={"tok": (me + off) % n_tok},
            device_id_type=MESH,
        )
        copy.start()
        dec_back.append(copy)

    hop = {}
    for half in range(2):
        for a1 in range(4):
            wait(half, 2, a1)
    compute(2)
    order = (2, 1, 3, 0)
    for a1 in order:
        for half in range(2):
            hop[half, 0, a1] = send(
                part.at[half, 2, a1, 0], relay.at[half, 0, a1], axis2[half](1)
            )
            hop[half, 1, a1] = send(
                part.at[half, 2, a1, 1], relay.at[half, 1, a1], axis2[half](-1)
            )
    for a1 in order:
        for half in range(2):
            hop[half, 0, a1].wait_recv()
            part[half, 1, a1, 0] = (
                part[half, 1, a1, 0].astype(F32) + relay[half, 0, a1].astype(F32)
            ).astype(BF16)
            came[half, 0, 0, a1] = send(
                part.at[half, 1, a1, 0], direct.at[half, 0, a1, 0], axis2[half](1)
            )
            hop[half, 1, a1].wait_recv()
            part[half, 3, a1, 1] = (
                part[half, 3, a1, 1].astype(F32) + relay[half, 1, a1].astype(F32)
            ).astype(BF16)
            came[half, 1, 1, a1] = send(
                part.at[half, 3, a1, 1], direct.at[half, 1, a1, 1], axis2[half](-1)
            )
    dtotal = dresid_ref[...] + pdec[0].astype(F32)
    for c in dec_back:
        c.wait_recv()
    for off in range(1, n_tok):
        dtotal = dtotal + rdec[off].astype(F32)
    dout_ref[...] = dtotal.astype(BF16)
    hop1 = {}
    came1 = {}

    def collect(half, a1):
        came[half, 0, 0, a1].wait_recv()
        came[half, 1, 1, a1].wait_recv()
        total = (
            part[half, 0, a1].astype(F32)
            + direct[half, 0, a1].astype(F32)
            + direct[half, 1, a1].astype(F32)
        )
        if a1 == 0:
            first[half] = total
        else:
            sums[half, a1] = total.astype(BF16)

    for half in range(2):
        came[half, 0, 1].wait_recv()
        came[half, 1, 0].wait_recv()
        collect(half, 2)
        hop1[half, 0] = send(sums.at[half, 2, 0], relay1.at[half, 0], axis1[half](1))
        hop1[half, 1] = send(sums.at[half, 2, 1], relay1.at[half, 1], axis1[half](-1))
    for half in range(2):
        collect(half, 1)
        came1[half, 0, 1] = send(
            sums.at[half, 1, 1], direct1.at[half, 0, 1], axis1[half](1)
        )
    for half in range(2):
        collect(half, 3)
        came1[half, 1, 0] = send(
            sums.at[half, 3, 0], direct1.at[half, 1, 0], axis1[half](-1)
        )
    for half in range(2):
        hop1[half, 0].wait_recv()
        sums[half, 1, 0] = (
            sums[half, 1, 0].astype(F32) + relay1[half, 0].astype(F32)
        ).astype(BF16)
        came1[half, 0, 0] = send(
            sums.at[half, 1, 0], direct1.at[half, 0, 0], axis1[half](1)
        )
        hop1[half, 1].wait_recv()
        sums[half, 3, 1] = (
            sums[half, 3, 1].astype(F32) + relay1[half, 1].astype(F32)
        ).astype(BF16)
        came1[half, 1, 1] = send(
            sums.at[half, 3, 1], direct1.at[half, 1, 1], axis1[half](-1)
        )
    for half in range(2):
        collect(half, 0)
    for half in range(2):
        for side in range(2):
            for q in range(2):
                came1[half, side, q].wait_recv()
        out_ref[half * 2 : half * 2 + 2] = (
            resid_ref[half * 2 : half * 2 + 2]
            + first[half]
            + direct1[half, 0].astype(F32)
            + direct1[half, 1].astype(F32)
        ).astype(BF16)
    for c in sent + dec_copies + dec_back:
        c.wait_send()


FFN_SENDS = 2 * (2 + 2 + 8 + 8 + 2 + 16 + 6)


def ffn(block, drow, resid, dresid, wgu, wdown, n_tok):
    width = block.shape[-1]
    vmem = pl.BlockSpec(memory_space=pltpu.VMEM)
    hbm = pl.BlockSpec(memory_space=pl.ANY)
    return pl.pallas_call(
        ffn_kernel,
        out_shape=(
            jax.ShapeDtypeStruct(block.shape, BF16),
            jax.ShapeDtypeStruct(drow.shape, BF16),
        ),
        in_specs=[vmem, vmem, vmem, vmem, hbm, hbm],
        out_specs=(vmem, vmem),
        scratch_shapes=[
            pltpu.VMEM(wgu.shape, BF16),
            pltpu.VMEM(wdown.shape, BF16),
            pltpu.VMEM((2, 4, 4, 2, Q, width), BF16),
            pltpu.VMEM((2, 4, 4, 2, Q, width), BF16),
            pltpu.VMEM((2, 2, 4, Q, width), BF16),
            pltpu.VMEM((2, 2, 4, 2, Q, width), BF16),
            pltpu.VMEM((2, 2, Q, width), F32),
            pltpu.VMEM((2, 4, 2, Q, width), BF16),
            pltpu.VMEM((2, 2, Q, width), BF16),
            pltpu.VMEM((2, 2, 2, Q, width), BF16),
            pltpu.VMEM((n_tok, 1, width), BF16),
            pltpu.VMEM((n_tok, width), F32),
            pltpu.VMEM((n_tok, 1, width), BF16),
            pltpu.VMEM((n_tok, 1, width), BF16),
            pltpu.SemaphoreType.DMA((5,)),
            pltpu.SemaphoreType.DMA((FFN_SENDS,)),
            pltpu.SemaphoreType.DMA((FFN_SENDS,)),
            pltpu.SemaphoreType.DMA((2 * n_tok,)),
            pltpu.SemaphoreType.DMA((2 * n_tok,)),
        ],
        compiler_params=pltpu.CompilerParams(
            collective_id=1, has_side_effects=True, vmem_limit_bytes=56 * 1024 * 1024
        ),
        name="ffn",
    )(block, drow, resid, dresid, wgu, wdown)


def project_kernel(
    states,
    dstates,
    gain_ref,
    w_hbm,
    homes,
    out_ref,
    dec_ref,
    w,
    normed,
    units,
    outgoing,
    pdec,
    wsem,
    lsem,
    ssem,
    rsem,
    dssem,
    drsem,
):
    me = lax.axis_index("tok")
    n_tok = lax.axis_size("tok")
    requests, positions, width = states.shape
    features = w.shape[2]
    per = features // HD
    barrier = pltpu.get_barrier_semaphore()
    for off in range(1, n_tok):
        pl.semaphore_signal(
            barrier, inc=1, device_id={"tok": (me + off) % n_tok}, device_id_type=MESH
        )
    load = pltpu.make_async_copy(w_hbm, w, wsem)
    load.start()
    gain = gain_ref[...]
    pdec_rows = rms_norm(dstates[...], gain)
    lane = lax.broadcasted_iota(jnp.int32, (positions, PAGE), 1)
    half = positions // 2

    strip = 64

    def norm(i, _):
        at = pl.ds(pl.multiple_of(i % (positions // strip) * strip, strip), strip)
        normed[i] = rms_norm(states[i // (positions // strip), at, :], gain)
        return 0

    lax.fori_loop(0, requests * positions // strip, norm, 0)
    load.wait()
    pl.semaphore_wait(barrier, n_tok - 1)
    for which in range(3):
        pdec[:, which * features : (which + 1) * features] = jnp.dot(
            pdec_rows, w[which], preferred_element_type=F32
        ).astype(BF16)
    copies = []
    for off in range(1, n_tok):
        copy = pltpu.make_async_remote_copy(
            src_ref=pdec,
            dst_ref=dec_ref.at[me],
            send_sem=dssem.at[off],
            recv_sem=drsem.at[off],
            device_id={"tok": (me + off) % n_tok},
            device_id_type=MESH,
        )
        copy.start()
        copies.append(copy)

    def project(r, _):
        rows = normed[pl.ds(r * (positions // strip), positions // strip)].reshape(
            positions, width
        )
        q, k, v = (jnp.dot(rows, w[i], preferred_element_type=F32) for i in range(3))
        for j in range(per):
            at = j // 2 * PAGE
            qb, kb, vb = (a[:, at : at + PAGE] for a in (q, k, v))
            if j % 2 == 0:
                both = jnp.where(lane < HD, kb, pltpu.roll(vb, HD, 1))
                pair = jnp.where(lane[:half] < HD, qb[:half], pltpu.roll(qb[half:], HD, 1))
            else:
                both = jnp.where(lane < HD, pltpu.roll(kb, HD, 1), vb)
                pair = jnp.where(lane[:half] < HD, pltpu.roll(qb[:half], HD, 1), qb[half:])
            units[r * per + j, :positions, :] = both.astype(BF16)
            units[r * per + j, positions:, :] = pair.astype(BF16)
        return 0

    lax.fori_loop(0, requests, project, 0)
    for off in range(n_tok):
        target = (me + off) % n_tok
        unit = jnp.int32(0)
        for u in range(requests * per):
            unit = jnp.where(homes[u] == target, u, unit)
        if off == 0:
            outgoing[0] = units[unit]
            own = pltpu.make_async_copy(outgoing.at[0], out_ref.at[me], lsem.at[0])
            own_dec = pltpu.make_async_copy(pdec, dec_ref.at[me], lsem.at[1])
            own.start()
            own_dec.start()
            continue
        outgoing[off] = units[unit]
        copy = pltpu.make_async_remote_copy(
            src_ref=outgoing.at[off],
            dst_ref=out_ref.at[me],
            send_sem=ssem.at[off],
            recv_sem=rsem.at[off],
            device_id={"tok": target},
            device_id_type=MESH,
        )
        copy.start()
        copies.append(copy)
    own.wait()
    own_dec.wait()
    for copy in copies:
        copy.wait()


def project(states, dstates, gain, w, homes, n_tok):
    requests, positions, width = states.shape
    hosted = dstates.shape[0]
    features = w.shape[2]
    vmem = pl.BlockSpec(memory_space=pltpu.VMEM)
    smem = pl.BlockSpec(memory_space=pltpu.SMEM)
    packed = positions // 2 * 3
    units = requests * features // HD
    return pl.pallas_call(
        project_kernel,
        out_shape=(
            jax.ShapeDtypeStruct((n_tok, packed, 2 * HD), BF16),
            jax.ShapeDtypeStruct((n_tok, hosted, 3 * features), BF16),
        ),
        in_specs=[vmem, vmem, vmem, pl.BlockSpec(memory_space=pl.ANY), smem],
        out_specs=(vmem, vmem),
        scratch_shapes=[
            pltpu.VMEM(w.shape, BF16),
            pltpu.VMEM((requests * positions // 64, 64, width), BF16),
            pltpu.VMEM((units, packed, 2 * HD), BF16),
            pltpu.VMEM((n_tok, packed, 2 * HD), BF16),
            pltpu.VMEM((hosted, 3 * features), BF16),
            pltpu.SemaphoreType.DMA,
            pltpu.SemaphoreType.DMA((2,)),
            pltpu.SemaphoreType.DMA((n_tok,)),
            pltpu.SemaphoreType.DMA((n_tok,)),
            pltpu.SemaphoreType.DMA((n_tok,)),
            pltpu.SemaphoreType.DMA((n_tok,)),
        ],
        compiler_params=pltpu.CompilerParams(
            collective_id=2, has_side_effects=True, vmem_limit_bytes=56 * 1024 * 1024
        ),
        name="project",
    )(states, dstates, gain, w, homes)


def mix_kernel(
    attn,
    dattn,
    states_hbm,
    dstates,
    gain_ref,
    w_hbm,
    homes,
    dhomes,
    normed_ref,
    dnormed_ref,
    resid_ref,
    dresid_ref,
    w,
    own,
    drows,
    got,
    gdec,
    gdec_rows,
    left,
    dleft,
    part,
    pdec,
    rdec,
    pair,
    sums,
    relay,
    direct,
    lsem,
    tssem,
    trsem,
    dssem,
    drsem,
    hssem,
    hrsem,
    ssem,
    rsem,
):
    me = lax.axis_index("tok")
    n_tok = lax.axis_size("tok")
    head = lax.axis_index("head")
    n_head = lax.axis_size("head")
    my_x, core = head // 2, head % 2
    n_x = n_head // 2
    requests, rows, width = own.shape
    positions = rows * n_head
    half = positions // 2
    hosted = dattn.shape[0]
    barrier = pltpu.get_barrier_semaphore()
    for off in range(1, n_tok):
        pl.semaphore_signal(
            barrier, inc=1, device_id={"tok": (me + off) % n_tok}, device_id_type=MESH
        )
    for off in range(1, n_head):
        pl.semaphore_signal(
            barrier, inc=1, device_id={"head": (head + off) % n_head}, device_id_type=MESH
        )
    load_w = pltpu.make_async_copy(w_hbm, w, lsem.at[0])
    load_own = pltpu.make_async_copy(
        states_hbm.at[:, pl.ds(pl.multiple_of(head * rows, rows), rows), :], own, lsem.at[1]
    )
    keep = pltpu.make_async_copy(attn.at[me], got.at[me], lsem.at[2])
    keep_dec = pltpu.make_async_copy(dattn, gdec.at[me], lsem.at[3])
    local = [load_w, load_own, keep, keep_dec]
    for c in local:
        c.start()
    pl.semaphore_wait(barrier, n_tok + n_head - 2)
    sends = []
    for off in range(1, n_tok):
        target = (me + off) % n_tok
        for source, dest, a, b in (
            (attn.at[target], got.at[me], tssem, trsem),
            (dattn, gdec.at[me], dssem, drsem),
        ):
            copy = pltpu.make_async_remote_copy(
                src_ref=source,
                dst_ref=dest,
                send_sem=a.at[off],
                recv_sem=b.at[off],
                device_id={"tok": target},
                device_id_type=MESH,
            )
            copy.start()
            sends.append(copy)
    drows[...] = dstates[...].astype(F32)
    for c in local:
        c.wait()
    for c in sends:
        c.wait_recv()
    lane = lax.broadcasted_iota(jnp.int32, (half, PAGE), 1)
    per = w.shape[0] // HD
    for r in range(requests):
        for j in range(0, per, 2):
            a = got[homes[r * per + j]].astype(F32)
            b = got[homes[r * per + j + 1]].astype(F32)
            low = jnp.where(lane < HD, a, pltpu.roll(b, HD, 1))
            high = jnp.where(lane < HD, pltpu.roll(a, HD, 1), b)
            cols = slice(j // 2 * PAGE, (j // 2 + 1) * PAGE)
            left[r, :half, cols] = low.astype(BF16)
            left[r, half:, cols] = high.astype(BF16)
    for t in range(n_tok):
        gdec_rows[t * hosted : (t + 1) * hosted, :] = gdec[t].astype(F32)
    for i in range(hosted):
        dleft[i : i + 1, :] = gdec_rows[pl.ds(dhomes[me * hosted + i], 1), :]

    def project(r, _):
        result = jnp.dot(left[r], w[...], preferred_element_type=F32).astype(BF16)
        for k in range(n_head):
            part[k % 2, r, k // 2] = result[k * rows : (k + 1) * rows]
        return 0

    lax.fori_loop(0, requests, project, 0)
    used = [0]
    ring = []

    def send(source, target, device):
        i = used[0]
        used[0] += 1
        copy = pltpu.make_async_remote_copy(
            src_ref=source,
            dst_ref=target,
            send_sem=ssem.at[i],
            recv_sem=rsem.at[i],
            device_id={"head": device},
            device_id_type=MESH,
        )
        copy.start()
        ring.append(copy)
        return copy

    partner = my_x * 2 + 1 - core
    up = (my_x + 1) % n_x * 2 + core
    down = (my_x + n_x - 1) % n_x * 2 + core
    order = (2, 1, 3, 0)
    paired = {}
    for dx in order:
        paired[dx] = send(
            part.at[1 - core, :, (my_x + dx) % n_x], pair.at[dx], partner
        )
    dresult = jnp.dot(dleft[...].astype(BF16), w[...], preferred_element_type=F32)
    for k in range(n_head):
        pdec[k] = dresult[k : k + 1, :].astype(BF16)
    for off in range(1, n_head):
        copy = pltpu.make_async_remote_copy(
            src_ref=pdec.at[(head + off) % n_head],
            dst_ref=rdec.at[n_head - off],
            send_sem=hssem.at[off],
            recv_sem=hrsem.at[off],
            device_id={"head": (head + off) % n_head},
            device_id_type=MESH,
        )
        copy.start()
        sends.append(copy)
    hop = {}
    came = {}
    for dx in order:
        paired[dx].wait_recv()
        total = part[core, :, (my_x + dx) % n_x].astype(F32) + pair[dx].astype(F32)
        if dx == 0:
            resid_ref[...] = total + own[...].astype(F32)
        else:
            sums[dx] = total.astype(BF16)
        if dx == 2:
            for i in range(2):
                hop[0, i] = send(sums.at[2, i], relay.at[0, i], up)
                hop[1, i] = send(sums.at[2, 2 + i], relay.at[1, i], down)
        if dx == 1:
            came[0, 1] = send(sums.at[1, 2:4], direct.at[0, 2:4], up)
        if dx == 3:
            came[1, 0] = send(sums.at[3, 0:2], direct.at[1, 0:2], down)
    for i in range(2):
        hop[0, i].wait_recv()
        sums[1, i] = (sums[1, i].astype(F32) + relay[0, i].astype(F32)).astype(BF16)
        came[0, 0, i] = send(sums.at[1, i], direct.at[0, i], up)
        hop[1, i].wait_recv()
        sums[3, 2 + i] = (sums[3, 2 + i].astype(F32) + relay[1, i].astype(F32)).astype(BF16)
        came[1, 1, i] = send(sums.at[3, 2 + i], direct.at[1, 2 + i], down)
    gain = gain_ref[...]
    dtotal = drows[pl.ds(head, 1), :] + pdec[head].astype(F32)
    for c in sends[2 * (n_tok - 1) :]:
        c.wait_recv()
    for off in range(1, n_head):
        dtotal = dtotal + rdec[off].astype(F32)
    dresid_ref[...] = dtotal
    dnormed_ref[...] = rms_norm(dtotal, gain)
    for c in came.values():
        c.wait_recv()
    for r in range(requests):
        total = resid_ref[r] + direct[0, r].astype(F32) + direct[1, r].astype(F32)
        resid_ref[r] = total
        normed_ref[r] = rms_norm(total, gain)
    for c in sends + ring:
        c.wait_send()


def mix(attn, dattn, states, dstates, gain, w, homes, dhomes, n_head):
    requests, positions, width = states.shape
    n_tok, packed, lanes = attn.shape
    hosted = dattn.shape[0]
    rows = positions // n_head
    n_x = n_head // 2
    vmem = pl.BlockSpec(memory_space=pltpu.VMEM)
    smem = pl.BlockSpec(memory_space=pltpu.SMEM)
    hbm = pl.BlockSpec(memory_space=pl.ANY)
    sem = pltpu.SemaphoreType.DMA
    ring = 4 + 4 + 2 + 4
    return pl.pallas_call(
        mix_kernel,
        out_shape=(
            jax.ShapeDtypeStruct((requests, rows, width), BF16),
            jax.ShapeDtypeStruct((1, width), BF16),
            jax.ShapeDtypeStruct((requests, rows, width), F32),
            jax.ShapeDtypeStruct((1, width), F32),
        ),
        in_specs=[vmem, vmem, hbm, vmem, vmem, hbm, smem, smem],
        out_specs=(vmem, vmem, vmem, vmem),
        scratch_shapes=[
            pltpu.VMEM(w.shape, BF16),
            pltpu.VMEM((requests, rows, width), BF16),
            pltpu.VMEM((hosted, width), F32),
            pltpu.VMEM((n_tok, packed, lanes), BF16),
            pltpu.VMEM((n_tok, hosted, w.shape[0]), BF16),
            pltpu.VMEM((n_tok * hosted, w.shape[0]), F32),
            pltpu.VMEM((requests, positions, w.shape[0]), BF16),
            pltpu.VMEM((hosted, w.shape[0]), F32),
            pltpu.VMEM((2, requests, n_x, rows, width), BF16),
            pltpu.VMEM((n_head, 1, width), BF16),
            pltpu.VMEM((n_head, 1, width), BF16),
            pltpu.VMEM((n_x, requests, rows, width), BF16),
            pltpu.VMEM((n_x, requests, rows, width), BF16),
            pltpu.VMEM((2, 2, rows, width), BF16),
            pltpu.VMEM((2, requests, rows, width), BF16),
            sem((4,)),
            sem((n_tok,)),
            sem((n_tok,)),
            sem((n_tok,)),
            sem((n_tok,)),
            sem((n_head,)),
            sem((n_head,)),
            sem((ring,)),
            sem((ring,)),
        ],
        compiler_params=pltpu.CompilerParams(
            collective_id=3, has_side_effects=True, vmem_limit_bytes=56 * 1024 * 1024
        ),
        name="mix",
    )(attn, dattn, states, dstates, gain, w, homes, dhomes)


def keep_kernel(left, right, left_out, right_out):
    left_out[...] = left[...]
    right_out[...] = right[...]


def keep(left, right):
    vmem = pl.BlockSpec(memory_space=pltpu.VMEM)
    return pl.pallas_call(
        keep_kernel,
        out_shape=tuple(jax.ShapeDtypeStruct(a.shape, a.dtype) for a in (left, right)),
        in_specs=[vmem, vmem],
        out_specs=(vmem, vmem),
        name="keep",
    )(left, right)


def shards(
    prefill_states,
    decode_states,
    attn_gain,
    w_qkv,
    w_out,
    ffn_gain,
    w_gate_up,
    w_down,
    prefill_pool,
    prefill_pages,
    prefill_lengths,
    prefill_home,
    decode_pool,
    decode_pages,
    decode_lengths,
    decode_home,
):
    n_tok = lax.axis_size("tok")
    n_head = lax.axis_size("head")
    width = prefill_states.shape[2]
    arrived, arrived_dec = project(
        prefill_states,
        decode_states,
        attn_gain.reshape(1, -1),
        jnp.transpose(w_qkv, (1, 0, 2)),
        prefill_home,
        n_tok,
    )
    attn, dattn = attention(
        prefill_pages,
        prefill_lengths,
        prefill_home,
        decode_pages,
        decode_lengths,
        decode_home,
        arrived,
        arrived_dec,
        prefill_pool.reshape(-1, 2 * HD),
        decode_pool.reshape(-1, decode_pool.shape[2]),
    )
    normed, dnormed, resid, dresid = mix(
        attn,
        dattn,
        prefill_states,
        decode_states,
        ffn_gain.reshape(1, -1),
        w_out,
        prefill_home,
        decode_home,
        n_head,
    )
    prefill_out, decode_out = ffn(
        normed,
        dnormed,
        resid,
        dresid,
        jnp.transpose(w_gate_up, (1, 2, 0)).reshape(-1, width),
        w_down,
        n_tok,
    )
    return keep(prefill_out, decode_out)


def solution(mesh):
    placed = (
        P(None, "tok", None),
        P("tok", None),
        P(),
        P(None, None, "head"),
        P("head", None),
        P(),
        P(None, None, "tok"),
        P("tok", None),
        P("tok", None, "head"),
        P("tok", None),
        P(),
        P(),
        P("tok", None, "head"),
        P("tok", None),
        P("tok"),
        P(),
    )
    return jax.shard_map(
        shards,
        mesh=mesh,
        in_specs=placed,
        out_specs=(P(None, ("tok", "head"), None), P(("tok", "head"), None)),
        check_vma=False,
    )
```

```python
import jax
import jax.numpy as jnp
from jax import lax
from jax.experimental import pallas as pl
from jax.experimental.pallas import tpu as pltpu
from jax.sharding import PartitionSpec as P

HD = 64
EPSILON = 1e-06
SCALE = 0.125
MASKED = -1e30
PAGE = 128
F32 = jnp.float32
BF16 = jnp.bfloat16


def rms_norm(rows, gain):
    values = rows.astype(F32)
    inverse = lax.rsqrt(jnp.mean(values * values, axis=-1, keepdims=True) + EPSILON)
    return (values * inverse * gain).astype(BF16)


def dot_nt(left, right):
    return lax.dot_general(left, right, (((1,), (1,)), ((), ())), preferred_element_type=F32)


QB = 512
KC = 512


def attention_kernel(
    pages,
    lengths,
    homes,
    dpages,
    dlens,
    dhomes,
    arrived,
    arrived_dec,
    pool_ref,
    dpool_hbm,
    out_ref,
    dout_ref,
    keys,
    vals,
    query,
    score,
    top_run,
    top,
    acc,
    dpool,
    dbias,
    dscore,
    drows,
    mine_ref,
    count,
    owner,
    dcount,
    anchor,
    sem,
):
    me = lax.axis_index("tok")
    n_tok = arrived.shape[0]
    positions = arrived.shape[1] // 3 * 2
    stretch = n_tok * positions
    span = pool_ref.shape[0]
    npages = span // PAGE
    dspan = dpool_hbm.shape[0]
    dnpages = dspan // PAGE
    slots, dmax = dpages.shape
    copy = pltpu.make_async_copy(dpool_hbm, dpool, sem)
    copy.start()

    my_unit = jnp.int32(0)
    for u in range(n_tok):
        my_unit = jnp.where(homes[u] == me, u, my_unit)
    length = lengths[my_unit // (n_tok // lengths.shape[0])]

    def count_page(i, _):
        count[pages[0, i]] = jnp.clip(length - i * PAGE, 0, PAGE)
        return 0

    lax.fori_loop(0, npages, count_page, 0)

    def zero_page(i, _):
        dcount[i] = 0
        owner[i] = 0
        return 0

    lax.fori_loop(0, dnpages, zero_page, 0)
    for s in range(slots):
        used = (dlens[s] + PAGE - 1) // PAGE

        def own_page(i, _):
            page = dpages[s, i]
            owner[page] = s
            dcount[page] = jnp.minimum(dlens[s] - i * PAGE, PAGE)
            return 0

        lax.fori_loop(0, used, own_page, 0)

    lane = lax.broadcasted_iota(jnp.int32, (PAGE, PAGE), 1)
    row = lax.broadcasted_iota(jnp.int32, (PAGE, PAGE), 0)

    def fill_cached(i, _):
        where_at = pl.ds(pl.multiple_of(i * PAGE, PAGE), PAGE)
        page = pool_ref[where_at, :].astype(F32)
        bias = jnp.where((lane == HD) & (row >= count[i]), MASKED, 0.0)
        keys[where_at, :] = jnp.where(lane < HD, page, bias).astype(BF16)
        vals[where_at, :] = jnp.where(lane < HD, 1.0, page).astype(BF16)
        return 0

    lax.fori_loop(0, npages, fill_cached, 0, unroll=4)

    half = PAGE // 2

    def fill_own(i, _):
        target = pl.ds(pl.multiple_of(span + i * PAGE, PAGE), PAGE)
        both = arrived[i, :PAGE, :].astype(F32)
        keys[target, :] = jnp.where(lane < HD, both, 0.0).astype(BF16)
        vals[target, :] = jnp.where(lane < HD, 1.0, both).astype(BF16)
        packed = arrived[i, PAGE:, :].astype(F32) * SCALE
        flag = jnp.where(lane[:half] == HD, 1.0, 0.0)
        low = jnp.where(lane[:half] < HD, packed, flag)
        high = jnp.where(lane[:half] < HD, pltpu.roll(packed, HD, 1), flag)
        at_low = pl.ds(pl.multiple_of(i * PAGE, PAGE), half)
        at_high = pl.ds(pl.multiple_of(i * PAGE + half, half), half)
        query[at_low, :] = low.astype(BF16)
        query[at_high, :] = high.astype(BF16)
        return 0

    lax.fori_loop(0, stretch // PAGE, fill_own, 0, unroll=4)

    def fold(s):
        best = s[:, :PAGE]
        for j in range(1, s.shape[1] // PAGE):
            best = jnp.maximum(best, s[:, j * PAGE : (j + 1) * PAGE])
        return best

    def make_scores(i, c, diagonal):
        rows = query[i * QB : (i + 1) * QB, :]
        s = dot_nt(rows, keys[pl.ds(pl.multiple_of(c * KC, KC), KC), :])
        if diagonal:
            r = lax.broadcasted_iota(jnp.int32, (QB, KC), 0)
            k = lax.broadcasted_iota(jnp.int32, (QB, KC), 1)
            s = jnp.where(k <= r, s, MASKED)
        score[i % 2, c] = s
        top_run[i % 2] = jnp.maximum(top_run[i % 2], fold(s))

    def finish_top(i):
        best = jnp.max(top_run[i % 2], axis=1, keepdims=True)
        top[i % 2] = jnp.broadcast_to(best, (QB, PAGE))

    def mix(i, c):
        best = top[i % 2]
        s = score[i % 2, c]
        p = jnp.exp(s - jnp.concatenate([best] * (KC // PAGE), axis=1)).astype(BF16)
        acc[...] += jnp.dot(
            p, vals[pl.ds(pl.multiple_of(c * KC, KC), KC), :], preferred_element_type=F32
        )

    blocks = stretch // QB
    cached_chunks = span // KC

    top_run[0] = jnp.full((QB, PAGE), MASKED, F32)

    def first(c, _):
        make_scores(0, c, False)
        return 0

    lax.fori_loop(0, cached_chunks, first, 0, unroll=4)
    make_scores(0, cached_chunks, True)
    finish_top(0)
    for i in range(blocks):
        acc[...] = jnp.zeros_like(acc)
        chunks = cached_chunks + i + 1
        if i + 1 < blocks:
            top_run[(i + 1) % 2] = jnp.full((QB, PAGE), MASKED, F32)

            def both(c, _, i=i):
                make_scores(i + 1, c, False)
                mix(i, c)
                return 0

            lax.fori_loop(0, chunks, both, 0, unroll=4)
            make_scores(i + 1, chunks, True)
            finish_top(i + 1)
        else:

            def last(c, _, i=i):
                mix(i, c)
                return 0

            lax.fori_loop(0, chunks, last, 0, unroll=4)
        total = acc[...]
        result = pltpu.roll(total, HD, 1) / total
        for j in range(QB // PAGE):
            tile = result[j * PAGE : (j + 1) * PAGE]
            out_ref[i * (QB // PAGE) + j] = jnp.where(
                lane[:half] < HD, tile[:half], pltpu.roll(tile[half:], HD, 1)
            ).astype(BF16)

    slot_row = lax.broadcasted_iota(jnp.int32, (slots, PAGE), 0)
    slot_lane = lax.broadcasted_iota(jnp.int32, (slots, PAGE), 1)

    def fill_bias(i, _):
        seen = (slot_row == owner[i]) & (slot_lane < dcount[i])
        dbias[i] = jnp.where(seen, 0.0, MASKED)
        return 0

    lax.fori_loop(0, dnpages, fill_bias, 0)
    for t in range(n_tok):
        drows[t * slots : (t + 1) * slots, :] = arrived_dec[t].astype(F32)

    def find(r, _):
        slot = dhomes[r] - me * slots

        @pl.when((slot >= 0) & (slot < slots))
        def _():
            anchor[slot] = r

        return 0

    lax.fori_loop(0, dhomes.shape[0], find, 0)
    for s in range(slots):
        mine_ref[s : s + 1, :] = drows[pl.ds(anchor[s], 1), :]
    copy.wait()
    rows = mine_ref[...]
    heads = rows.shape[1] // (3 * HD)
    step = 1024
    per = step // PAGE
    for h in range(heads):
        block = h // 2 * PAGE
        width = heads * HD

        def part(which, left):
            piece = rows[:, which * width + block : which * width + block + PAGE]
            return pltpu.roll(piece, HD, 1) if (h % 2 == 1) == left else piece

        q = jnp.where(slot_lane < HD, part(0, True) * SCALE, 0.0)
        k = part(1, True)
        v = part(2, False)
        own = jnp.sum(q * k, axis=1, keepdims=True)
        qb = q.astype(BF16)
        best = jnp.broadcast_to(own, (slots, PAGE))
        for c in range(dspan // step):
            s = dot_nt(qb, dpool[c * step : (c + 1) * step, h * PAGE : (h + 1) * PAGE])
            s = s + jnp.concatenate([dbias[c * per + j] for j in range(per)], axis=1)
            dscore[c] = s
            best = jnp.maximum(best, fold(s))
        best = jnp.max(best, axis=1, keepdims=True)
        own_weight = jnp.exp(own - best)
        sums = jnp.zeros((slots, PAGE), F32)
        mixed = jnp.zeros((slots, PAGE), F32)
        for c in range(dspan // step):
            p = jnp.exp(dscore[c] - best)
            for j in range(per):
                sums = sums + p[:, j * PAGE : (j + 1) * PAGE]
            mixed = mixed + jnp.dot(
                p.astype(BF16),
                dpool[c * step : (c + 1) * step, h * PAGE : (h + 1) * PAGE],
                preferred_element_type=F32,
            )
        total = jnp.sum(sums, axis=1, keepdims=True) + own_weight
        mixed = (mixed + own_weight.astype(BF16).astype(F32) * v) / total
        dout_ref[:, h * HD : (h + 1) * HD] = pltpu.roll(mixed, HD, 1)[:, :HD].astype(BF16)


def attention(
    pages, lengths, homes, dpages, dlens, dhomes, arrived, arrived_dec, pool, dpool
):
    n_tok, packed, lanes = arrived.shape
    positions = packed // 3 * 2
    stretch = n_tok * positions
    span = pool.shape[0]
    dspan, dwidth = dpool.shape
    slots, dcols = arrived_dec.shape[1:]
    keys = span + stretch
    vmem = pl.BlockSpec(memory_space=pltpu.VMEM)
    smem = pl.BlockSpec(memory_space=pltpu.SMEM)
    return pl.pallas_call(
        attention_kernel,
        out_shape=(
            jax.ShapeDtypeStruct((n_tok, positions // 2, lanes), BF16),
            jax.ShapeDtypeStruct((slots, dcols // 3), BF16),
        ),
        in_specs=[smem] * 6 + [vmem] * 3 + [pl.BlockSpec(memory_space=pl.ANY)],
        out_specs=(vmem, vmem),
        scratch_shapes=[
            pltpu.VMEM((keys, 2 * HD), BF16),
            pltpu.VMEM((keys, 2 * HD), BF16),
            pltpu.VMEM((stretch, 2 * HD), BF16),
            pltpu.VMEM((2, keys // KC, QB, KC), F32),
            pltpu.VMEM((2, QB, PAGE), F32),
            pltpu.VMEM((2, QB, PAGE), F32),
            pltpu.VMEM((QB, PAGE), F32),
            pltpu.VMEM((dspan, dwidth), BF16),
            pltpu.VMEM((dspan // PAGE, slots, PAGE), F32),
            pltpu.VMEM((dspan // 1024, slots, 1024), F32),
            pltpu.VMEM((n_tok * slots, dcols), F32),
            pltpu.VMEM((slots, dcols), F32),
            pltpu.SMEM((span // PAGE,), jnp.int32),
            pltpu.SMEM((dspan // PAGE,), jnp.int32),
            pltpu.SMEM((dspan // PAGE,), jnp.int32),
            pltpu.SMEM((slots,), jnp.int32),
            pltpu.SemaphoreType.DMA,
        ],
        compiler_params=pltpu.CompilerParams(vmem_limit_bytes=62 * 1024 * 1024),
        name="attention",
    )(pages, lengths, homes, dpages, dlens, dhomes, arrived, arrived_dec, pool, dpool)


MESH = pl.DeviceIdType.MESH
Q = 16


def ffn_kernel(
    block_ref,
    drow_ref,
    resid_ref,
    dresid_ref,
    wgu_hbm,
    wdown_hbm,
    out_ref,
    dout_ref,
    wgu,
    wdown,
    x,
    part,
    relay,
    direct,
    first,
    sums,
    relay1,
    direct1,
    xdec,
    xrows,
    pdec,
    rdec,
    wsem,
    ssem,
    rsem,
    dssem,
    drsem,
):
    me = lax.axis_index("tok")
    n_tok = lax.axis_size("tok")
    my_y, my_z = me // 4, me % 4
    barrier = pltpu.get_barrier_semaphore()
    for off in range(1, n_tok):
        pl.semaphore_signal(
            barrier,
            inc=1,
            device_id={"tok": (me + off) % n_tok},
            device_id_type=MESH,
        )
    load_gu = pltpu.make_async_copy(wgu_hbm, wgu, wsem.at[0])
    load_down = pltpu.make_async_copy(wdown_hbm, wdown, wsem.at[1])
    load_own = [
        pltpu.make_async_copy(
            block_ref.at[pl.ds(half * 2, 2)], x.at[half, 0, 0], wsem.at[2 + half]
        )
        for half in range(2)
    ]
    load_dec = pltpu.make_async_copy(drow_ref, xdec.at[0], wsem.at[4])
    for c in load_own:
        c.start()
    load_dec.start()
    load_gu.start()
    load_down.start()

    def along_z(step):
        return {"tok": my_y * 4 + (my_z + step + 4) % 4}

    def along_y(step):
        return {"tok": (my_y + step + 4) % 4 * 4 + my_z}

    axis1 = (along_z, along_y)
    axis2 = (along_y, along_z)
    used = [0]

    def send(source, target, device):
        i = used[0]
        used[0] += 1
        copy = pltpu.make_async_remote_copy(
            src_ref=source,
            dst_ref=target,
            send_sem=ssem.at[i],
            recv_sem=rsem.at[i],
            device_id=device,
            device_id_type=MESH,
        )
        copy.start()
        sent.append(copy)
        return copy

    sent = []
    for c in load_own:
        c.wait()
    load_dec.wait()
    pl.semaphore_wait(barrier, n_tok - 1)

    got = {}
    for half in range(2):
        own = x.at[half, 0, 0]
        got[half, 0, 3] = [send(own, x.at[half, 0, 3], axis1[half](1))]
        got[half, 0, 1] = [send(own, x.at[half, 0, 1], axis1[half](-1))]

    def spread(half, a1):
        own = x.at[half, 0, a1]
        got[half, 3, a1] = [send(own, x.at[half, 3, a1], axis2[half](1))]
        got[half, 1, a1] = [send(own, x.at[half, 1, a1], axis2[half](-1))]

    def relay2(half, a1):
        a = send(x.at[half, 3, a1, 0], x.at[half, 2, a1, 0], axis2[half](1))
        b = send(x.at[half, 1, a1, 1], x.at[half, 2, a1, 1], axis2[half](-1))
        got[half, 2, a1] = [a, b]

    def wait(half, a2, a1):
        for c in got[half, a2, a1]:
            c.wait_recv()

    for half in range(2):
        spread(half, 0)
    dec_copies = []
    for off in range(1, n_tok):
        copy = pltpu.make_async_remote_copy(
            src_ref=xdec.at[0],
            dst_ref=xdec.at[n_tok - off],
            send_sem=dssem.at[off],
            recv_sem=drsem.at[off],
            device_id={"tok": (me + off) % n_tok},
            device_id_type=MESH,
        )
        copy.start()
        dec_copies.append(copy)
    for half in range(2):
        wait(half, 0, 3)
        wait(half, 0, 1)
        a = send(x.at[half, 0, 3, 0], x.at[half, 0, 2, 0], axis1[half](1))
        b = send(x.at[half, 0, 1, 1], x.at[half, 0, 2, 1], axis1[half](-1))
        got[half, 0, 2] = [a, b]
        spread(half, 3)
        spread(half, 1)
    for half in range(2):
        wait(half, 3, 0)
        wait(half, 1, 0)
        relay2(half, 0)
    for half in range(2):
        wait(half, 0, 2)
        spread(half, 2)

    width = wdown.shape[0]

    def hidden_of(rows):
        both = dot_nt(rows, wgu[...])
        gate = both[:, :width]
        return (jax.nn.gelu(gate, approximate=True) * both[:, width:]).astype(BF16)

    def compute(a2):
        rows = x[:, a2].reshape(2 * 4 * 2 * Q, x.shape[-1])
        result = jnp.dot(hidden_of(rows), wdown[...], preferred_element_type=F32)
        part[:, a2] = result.astype(BF16).reshape(2, 4, 2, Q, x.shape[-1])

    load_gu.wait()
    load_down.wait()

    compute(0)
    for a1 in (3, 1):
        for half in range(2):
            wait(half, 3, a1)
            wait(half, 1, a1)
            relay2(half, a1)
    for half in range(2):
        wait(half, 3, 2)
        wait(half, 1, 2)
        relay2(half, 2)

    came = {}
    for a2, side, q, step in ((1, 0, 1, 1), (3, 1, 0, -1)):
        compute(a2)
        for half in range(2):
            came[half, side, q] = send(
                part.at[half, a2, :, q], direct.at[half, side, :, q], axis2[half](step)
            )
    for c in dec_copies:
        c.wait_recv()
    for t in range(n_tok):
        xrows[t : t + 1, :] = xdec[t].astype(F32)
    dpart = jnp.dot(
        hidden_of(xrows[...].astype(BF16)), wdown[...], preferred_element_type=F32
    )
    for t in range(n_tok):
        pdec[t] = dpart[t : t + 1, :].astype(BF16)
    dec_back = []
    for off in range(1, n_tok):
        copy = pltpu.make_async_remote_copy(
            src_ref=pdec.at[off],
            dst_ref=rdec.at[n_tok - off],
            send_sem=dssem.at[n_tok + off],
            recv_sem=drsem.at[n_tok + off],
            device_id={"tok": (me + off) % n_tok},
            device_id_type=MESH,
        )
        copy.start()
        dec_back.append(copy)

    hop = {}
    for half in range(2):
        for a1 in range(4):
            wait(half, 2, a1)
    compute(2)
    order = (2, 1, 3, 0)
    for a1 in order:
        for half in range(2):
            hop[half, 0, a1] = send(
                part.at[half, 2, a1, 0], relay.at[half, 0, a1], axis2[half](1)
            )
            hop[half, 1, a1] = send(
                part.at[half, 2, a1, 1], relay.at[half, 1, a1], axis2[half](-1)
            )
    for a1 in order:
        for half in range(2):
            hop[half, 0, a1].wait_recv()
            part[half, 1, a1, 0] = (
                part[half, 1, a1, 0].astype(F32) + relay[half, 0, a1].astype(F32)
            ).astype(BF16)
            came[half, 0, 0, a1] = send(
                part.at[half, 1, a1, 0], direct.at[half, 0, a1, 0], axis2[half](1)
            )
            hop[half, 1, a1].wait_recv()
            part[half, 3, a1, 1] = (
                part[half, 3, a1, 1].astype(F32) + relay[half, 1, a1].astype(F32)
            ).astype(BF16)
            came[half, 1, 1, a1] = send(
                part.at[half, 3, a1, 1], direct.at[half, 1, a1, 1], axis2[half](-1)
            )
    dtotal = dresid_ref[...] + pdec[0].astype(F32)
    for c in dec_back:
        c.wait_recv()
    for off in range(1, n_tok):
        dtotal = dtotal + rdec[off].astype(F32)
    dout_ref[...] = dtotal.astype(BF16)
    hop1 = {}
    came1 = {}

    def collect(half, a1):
        came[half, 0, 0, a1].wait_recv()
        came[half, 1, 1, a1].wait_recv()
        total = (
            part[half, 0, a1].astype(F32)
            + direct[half, 0, a1].astype(F32)
            + direct[half, 1, a1].astype(F32)
        )
        if a1 == 0:
            first[half] = total
        else:
            sums[half, a1] = total.astype(BF16)

    for half in range(2):
        came[half, 0, 1].wait_recv()
        came[half, 1, 0].wait_recv()
        collect(half, 2)
        hop1[half, 0] = send(sums.at[half, 2, 0], relay1.at[half, 0], axis1[half](1))
        hop1[half, 1] = send(sums.at[half, 2, 1], relay1.at[half, 1], axis1[half](-1))
    for half in range(2):
        collect(half, 1)
        came1[half, 0, 1] = send(
            sums.at[half, 1, 1], direct1.at[half, 0, 1], axis1[half](1)
        )
    for half in range(2):
        collect(half, 3)
        came1[half, 1, 0] = send(
            sums.at[half, 3, 0], direct1.at[half, 1, 0], axis1[half](-1)
        )
    for half in range(2):
        hop1[half, 0].wait_recv()
        sums[half, 1, 0] = (
            sums[half, 1, 0].astype(F32) + relay1[half, 0].astype(F32)
        ).astype(BF16)
        came1[half, 0, 0] = send(
            sums.at[half, 1, 0], direct1.at[half, 0, 0], axis1[half](1)
        )
        hop1[half, 1].wait_recv()
        sums[half, 3, 1] = (
            sums[half, 3, 1].astype(F32) + relay1[half, 1].astype(F32)
        ).astype(BF16)
        came1[half, 1, 1] = send(
            sums.at[half, 3, 1], direct1.at[half, 1, 1], axis1[half](-1)
        )
    for half in range(2):
        collect(half, 0)
    for half in range(2):
        for side in range(2):
            for q in range(2):
                came1[half, side, q].wait_recv()
        out_ref[half * 2 : half * 2 + 2] = (
            resid_ref[half * 2 : half * 2 + 2]
            + first[half]
            + direct1[half, 0].astype(F32)
            + direct1[half, 1].astype(F32)
        ).astype(BF16)
    for c in sent + dec_copies + dec_back:
        c.wait_send()


FFN_SENDS = 2 * (2 + 2 + 8 + 8 + 2 + 16 + 6)


def ffn(block, drow, resid, dresid, wgu, wdown, n_tok):
    width = block.shape[-1]
    vmem = pl.BlockSpec(memory_space=pltpu.VMEM)
    hbm = pl.BlockSpec(memory_space=pl.ANY)
    return pl.pallas_call(
        ffn_kernel,
        out_shape=(
            jax.ShapeDtypeStruct(block.shape, BF16),
            jax.ShapeDtypeStruct(drow.shape, BF16),
        ),
        in_specs=[vmem, vmem, vmem, vmem, hbm, hbm],
        out_specs=(vmem, vmem),
        scratch_shapes=[
            pltpu.VMEM(wgu.shape, BF16),
            pltpu.VMEM(wdown.shape, BF16),
            pltpu.VMEM((2, 4, 4, 2, Q, width), BF16),
            pltpu.VMEM((2, 4, 4, 2, Q, width), BF16),
            pltpu.VMEM((2, 2, 4, Q, width), BF16),
            pltpu.VMEM((2, 2, 4, 2, Q, width), BF16),
            pltpu.VMEM((2, 2, Q, width), F32),
            pltpu.VMEM((2, 4, 2, Q, width), BF16),
            pltpu.VMEM((2, 2, Q, width), BF16),
            pltpu.VMEM((2, 2, 2, Q, width), BF16),
            pltpu.VMEM((n_tok, 1, width), BF16),
            pltpu.VMEM((n_tok, width), F32),
            pltpu.VMEM((n_tok, 1, width), BF16),
            pltpu.VMEM((n_tok, 1, width), BF16),
            pltpu.SemaphoreType.DMA((5,)),
            pltpu.SemaphoreType.DMA((FFN_SENDS,)),
            pltpu.SemaphoreType.DMA((FFN_SENDS,)),
            pltpu.SemaphoreType.DMA((2 * n_tok,)),
            pltpu.SemaphoreType.DMA((2 * n_tok,)),
        ],
        compiler_params=pltpu.CompilerParams(
            collective_id=1, has_side_effects=True, vmem_limit_bytes=56 * 1024 * 1024
        ),
        name="ffn",
    )(block, drow, resid, dresid, wgu, wdown)


def project_kernel(
    states,
    dstates,
    gain_ref,
    w_hbm,
    homes,
    out_ref,
    dec_ref,
    w,
    normed,
    units,
    outgoing,
    pdec,
    wsem,
    lsem,
    ssem,
    rsem,
    dssem,
    drsem,
):
    me = lax.axis_index("tok")
    n_tok = lax.axis_size("tok")
    requests, positions, width = states.shape
    features = w.shape[2]
    per = features // HD
    barrier = pltpu.get_barrier_semaphore()
    for off in range(1, n_tok):
        pl.semaphore_signal(
            barrier, inc=1, device_id={"tok": (me + off) % n_tok}, device_id_type=MESH
        )
    load = pltpu.make_async_copy(w_hbm, w, wsem)
    load.start()
    gain = gain_ref[...]
    pdec_rows = rms_norm(dstates[...], gain)
    lane = lax.broadcasted_iota(jnp.int32, (positions, PAGE), 1)
    half = positions // 2

    strip = 64

    def norm(i, _):
        at = pl.ds(pl.multiple_of(i % (positions // strip) * strip, strip), strip)
        normed[i] = rms_norm(states[i // (positions // strip), at, :], gain)
        return 0

    lax.fori_loop(0, requests * positions // strip, norm, 0)
    load.wait()
    pl.semaphore_wait(barrier, n_tok - 1)
    for which in range(3):
        pdec[:, which * features : (which + 1) * features] = jnp.dot(
            pdec_rows, w[which], preferred_element_type=F32
        ).astype(BF16)
    copies = []
    for off in range(1, n_tok):
        copy = pltpu.make_async_remote_copy(
            src_ref=pdec,
            dst_ref=dec_ref.at[me],
            send_sem=dssem.at[off],
            recv_sem=drsem.at[off],
            device_id={"tok": (me + off) % n_tok},
            device_id_type=MESH,
        )
        copy.start()
        copies.append(copy)

    group = 2
    strips = group * positions // strip

    def project(g, _):
        rows = normed[pl.ds(g * strips, strips)].reshape(group * positions, width)
        full = [jnp.dot(rows, w[i], preferred_element_type=F32) for i in range(3)]
        for m in range(group):
            q, k, v = (a[m * positions : (m + 1) * positions] for a in full)
            for j in range(per):
                at = j // 2 * PAGE
                qb, kb, vb = (a[:, at : at + PAGE] for a in (q, k, v))
                if j % 2 == 0:
                    both = jnp.where(lane < HD, kb, pltpu.roll(vb, HD, 1))
                    turned = pltpu.roll(qb[half:], HD, 1)
                    pair = jnp.where(lane[:half] < HD, qb[:half], turned)
                else:
                    both = jnp.where(lane < HD, pltpu.roll(kb, HD, 1), vb)
                    turned = pltpu.roll(qb[:half], HD, 1)
                    pair = jnp.where(lane[:half] < HD, turned, qb[half:])
                unit = (g * group + m) * per + j
                units[unit, :positions, :] = both.astype(BF16)
                units[unit, positions:, :] = pair.astype(BF16)
        return 0

    lax.fori_loop(0, requests // group, project, 0)
    for off in range(n_tok):
        target = (me + off) % n_tok
        unit = jnp.int32(0)
        for u in range(requests * per):
            unit = jnp.where(homes[u] == target, u, unit)
        if off == 0:
            outgoing[0] = units[unit]
            own = pltpu.make_async_copy(outgoing.at[0], out_ref.at[me], lsem.at[0])
            own_dec = pltpu.make_async_copy(pdec, dec_ref.at[me], lsem.at[1])
            own.start()
            own_dec.start()
            continue
        outgoing[off] = units[unit]
        copy = pltpu.make_async_remote_copy(
            src_ref=outgoing.at[off],
            dst_ref=out_ref.at[me],
            send_sem=ssem.at[off],
            recv_sem=rsem.at[off],
            device_id={"tok": target},
            device_id_type=MESH,
        )
        copy.start()
        copies.append(copy)
    own.wait()
    own_dec.wait()
    for copy in copies:
        copy.wait()


def project(states, dstates, gain, w, homes, n_tok):
    requests, positions, width = states.shape
    hosted = dstates.shape[0]
    features = w.shape[2]
    vmem = pl.BlockSpec(memory_space=pltpu.VMEM)
    smem = pl.BlockSpec(memory_space=pltpu.SMEM)
    packed = positions // 2 * 3
    units = requests * features // HD
    return pl.pallas_call(
        project_kernel,
        out_shape=(
            jax.ShapeDtypeStruct((n_tok, packed, 2 * HD), BF16),
            jax.ShapeDtypeStruct((n_tok, hosted, 3 * features), BF16),
        ),
        in_specs=[vmem, vmem, vmem, pl.BlockSpec(memory_space=pl.ANY), smem],
        out_specs=(vmem, vmem),
        scratch_shapes=[
            pltpu.VMEM(w.shape, BF16),
            pltpu.VMEM((requests * positions // 64, 64, width), BF16),
            pltpu.VMEM((units, packed, 2 * HD), BF16),
            pltpu.VMEM((n_tok, packed, 2 * HD), BF16),
            pltpu.VMEM((hosted, 3 * features), BF16),
            pltpu.SemaphoreType.DMA,
            pltpu.SemaphoreType.DMA((2,)),
            pltpu.SemaphoreType.DMA((n_tok,)),
            pltpu.SemaphoreType.DMA((n_tok,)),
            pltpu.SemaphoreType.DMA((n_tok,)),
            pltpu.SemaphoreType.DMA((n_tok,)),
        ],
        compiler_params=pltpu.CompilerParams(
            collective_id=2, has_side_effects=True, vmem_limit_bytes=56 * 1024 * 1024
        ),
        name="project",
    )(states, dstates, gain, w, homes)


def mix_kernel(
    attn,
    dattn,
    states_hbm,
    dstates,
    gain_ref,
    w_hbm,
    homes,
    dhomes,
    normed_ref,
    dnormed_ref,
    resid_ref,
    dresid_ref,
    w,
    own,
    drows,
    got,
    gdec,
    gdec_rows,
    left,
    dleft,
    part,
    pdec,
    rdec,
    pair,
    sums,
    relay,
    direct,
    lsem,
    tssem,
    trsem,
    dssem,
    drsem,
    hssem,
    hrsem,
    ssem,
    rsem,
):
    me = lax.axis_index("tok")
    n_tok = lax.axis_size("tok")
    head = lax.axis_index("head")
    n_head = lax.axis_size("head")
    my_x, core = head // 2, head % 2
    n_x = n_head // 2
    requests, rows, width = own.shape
    positions = rows * n_head
    half = positions // 2
    hosted = dattn.shape[0]
    barrier = pltpu.get_barrier_semaphore()
    for off in range(1, n_tok):
        pl.semaphore_signal(
            barrier, inc=1, device_id={"tok": (me + off) % n_tok}, device_id_type=MESH
        )
    for off in range(1, n_head):
        pl.semaphore_signal(
            barrier, inc=1, device_id={"head": (head + off) % n_head}, device_id_type=MESH
        )
    load_w = pltpu.make_async_copy(w_hbm, w, lsem.at[0])
    load_own = pltpu.make_async_copy(
        states_hbm.at[:, pl.ds(pl.multiple_of(head * rows, rows), rows), :], own, lsem.at[1]
    )
    keep = pltpu.make_async_copy(attn.at[me], got.at[me], lsem.at[2])
    keep_dec = pltpu.make_async_copy(dattn, gdec.at[me], lsem.at[3])
    local = [load_w, load_own, keep, keep_dec]
    for c in local:
        c.start()
    pl.semaphore_wait(barrier, n_tok + n_head - 2)
    sends = []
    for off in range(1, n_tok):
        target = (me + off) % n_tok
        for source, dest, a, b in (
            (attn.at[target], got.at[me], tssem, trsem),
            (dattn, gdec.at[me], dssem, drsem),
        ):
            copy = pltpu.make_async_remote_copy(
                src_ref=source,
                dst_ref=dest,
                send_sem=a.at[off],
                recv_sem=b.at[off],
                device_id={"tok": target},
                device_id_type=MESH,
            )
            copy.start()
            sends.append(copy)
    drows[...] = dstates[...].astype(F32)
    for c in local:
        c.wait()
    for c in sends:
        c.wait_recv()
    lane = lax.broadcasted_iota(jnp.int32, (half, PAGE), 1)
    per = w.shape[0] // HD
    for r in range(requests):
        for j in range(0, per, 2):
            a = got[homes[r * per + j]].astype(F32)
            b = got[homes[r * per + j + 1]].astype(F32)
            low = jnp.where(lane < HD, a, pltpu.roll(b, HD, 1))
            high = jnp.where(lane < HD, pltpu.roll(a, HD, 1), b)
            cols = slice(j // 2 * PAGE, (j // 2 + 1) * PAGE)
            left[r, :half, cols] = low.astype(BF16)
            left[r, half:, cols] = high.astype(BF16)
    for t in range(n_tok):
        gdec_rows[t * hosted : (t + 1) * hosted, :] = gdec[t].astype(F32)
    for i in range(hosted):
        dleft[i : i + 1, :] = gdec_rows[pl.ds(dhomes[me * hosted + i], 1), :]

    used = [0]
    ring = []

    def send(source, target, device):
        i = used[0]
        used[0] += 1
        copy = pltpu.make_async_remote_copy(
            src_ref=source,
            dst_ref=target,
            send_sem=ssem.at[i],
            recv_sem=rsem.at[i],
            device_id={"head": device},
            device_id_type=MESH,
        )
        copy.start()
        ring.append(copy)
        return copy

    partner = my_x * 2 + 1 - core
    up = (my_x + 1) % n_x * 2 + core
    down = (my_x + n_x - 1) % n_x * 2 + core
    order = (2, 1, 3, 0)
    paired = []
    for r in range(requests):
        result = jnp.dot(left[r], w[...], preferred_element_type=F32).astype(BF16)
        for k in range(n_head):
            part[k % 2, r, k // 2] = result[k * rows : (k + 1) * rows]
        paired.append(send(part.at[1 - core, r], pair.at[r], partner))
    dresult = jnp.dot(dleft[...].astype(BF16), w[...], preferred_element_type=F32)
    for k in range(n_head):
        pdec[k] = dresult[k : k + 1, :].astype(BF16)
    for off in range(1, n_head):
        copy = pltpu.make_async_remote_copy(
            src_ref=pdec.at[(head + off) % n_head],
            dst_ref=rdec.at[n_head - off],
            send_sem=hssem.at[off],
            recv_sem=hrsem.at[off],
            device_id={"head": (head + off) % n_head},
            device_id_type=MESH,
        )
        copy.start()
        sends.append(copy)
    hop = {}
    came = {}
    for dx in order:
        for c in paired if dx == order[0] else ():
            c.wait_recv()
        there = (my_x + dx) % n_x
        total = part[core, :, there].astype(F32) + pair[:, there].astype(F32)
        if dx == 0:
            resid_ref[...] = total + own[...].astype(F32)
        else:
            sums[dx] = total.astype(BF16)
        if dx == 2:
            for i in range(2):
                hop[0, i] = send(sums.at[2, i], relay.at[0, i], up)
                hop[1, i] = send(sums.at[2, 2 + i], relay.at[1, i], down)
        if dx == 1:
            came[0, 1] = send(sums.at[1, 2:4], direct.at[0, 2:4], up)
        if dx == 3:
            came[1, 0] = send(sums.at[3, 0:2], direct.at[1, 0:2], down)
    for i in range(2):
        hop[0, i].wait_recv()
        sums[1, i] = (sums[1, i].astype(F32) + relay[0, i].astype(F32)).astype(BF16)
        came[0, 0, i] = send(sums.at[1, i], direct.at[0, i], up)
        hop[1, i].wait_recv()
        sums[3, 2 + i] = (sums[3, 2 + i].astype(F32) + relay[1, i].astype(F32)).astype(BF16)
        came[1, 1, i] = send(sums.at[3, 2 + i], direct.at[1, 2 + i], down)
    gain = gain_ref[...]
    dtotal = drows[pl.ds(head, 1), :] + pdec[head].astype(F32)
    for c in sends[2 * (n_tok - 1) :]:
        c.wait_recv()
    for off in range(1, n_head):
        dtotal = dtotal + rdec[off].astype(F32)
    dresid_ref[...] = dtotal
    dnormed_ref[...] = rms_norm(dtotal, gain)
    for c in came.values():
        c.wait_recv()
    for r in range(requests):
        total = resid_ref[r] + direct[0, r].astype(F32) + direct[1, r].astype(F32)
        resid_ref[r] = total
        normed_ref[r] = rms_norm(total, gain)
    for c in sends + ring:
        c.wait_send()


def mix(attn, dattn, states, dstates, gain, w, homes, dhomes, n_head):
    requests, positions, width = states.shape
    n_tok, packed, lanes = attn.shape
    hosted = dattn.shape[0]
    rows = positions // n_head
    n_x = n_head // 2
    vmem = pl.BlockSpec(memory_space=pltpu.VMEM)
    smem = pl.BlockSpec(memory_space=pltpu.SMEM)
    hbm = pl.BlockSpec(memory_space=pl.ANY)
    sem = pltpu.SemaphoreType.DMA
    ring = 4 + 4 + 2 + 4
    return pl.pallas_call(
        mix_kernel,
        out_shape=(
            jax.ShapeDtypeStruct((requests, rows, width), BF16),
            jax.ShapeDtypeStruct((1, width), BF16),
            jax.ShapeDtypeStruct((requests, rows, width), F32),
            jax.ShapeDtypeStruct((1, width), F32),
        ),
        in_specs=[vmem, vmem, hbm, vmem, vmem, hbm, smem, smem],
        out_specs=(vmem, vmem, vmem, vmem),
        scratch_shapes=[
            pltpu.VMEM(w.shape, BF16),
            pltpu.VMEM((requests, rows, width), BF16),
            pltpu.VMEM((hosted, width), F32),
            pltpu.VMEM((n_tok, packed, lanes), BF16),
            pltpu.VMEM((n_tok, hosted, w.shape[0]), BF16),
            pltpu.VMEM((n_tok * hosted, w.shape[0]), F32),
            pltpu.VMEM((requests, positions, w.shape[0]), BF16),
            pltpu.VMEM((hosted, w.shape[0]), F32),
            pltpu.VMEM((2, requests, n_x, rows, width), BF16),
            pltpu.VMEM((n_head, 1, width), BF16),
            pltpu.VMEM((n_head, 1, width), BF16),
            pltpu.VMEM((requests, n_x, rows, width), BF16),
            pltpu.VMEM((n_x, requests, rows, width), BF16),
            pltpu.VMEM((2, 2, rows, width), BF16),
            pltpu.VMEM((2, requests, rows, width), BF16),
            sem((4,)),
            sem((n_tok,)),
            sem((n_tok,)),
            sem((n_tok,)),
            sem((n_tok,)),
            sem((n_head,)),
            sem((n_head,)),
            sem((ring,)),
            sem((ring,)),
        ],
        compiler_params=pltpu.CompilerParams(
            collective_id=3, has_side_effects=True, vmem_limit_bytes=56 * 1024 * 1024
        ),
        name="mix",
    )(attn, dattn, states, dstates, gain, w, homes, dhomes)


def keep_kernel(left, right, left_out, right_out):
    left_out[...] = left[...]
    right_out[...] = right[...]


def keep(left, right):
    vmem = pl.BlockSpec(memory_space=pltpu.VMEM)
    return pl.pallas_call(
        keep_kernel,
        out_shape=tuple(jax.ShapeDtypeStruct(a.shape, a.dtype) for a in (left, right)),
        in_specs=[vmem, vmem],
        out_specs=(vmem, vmem),
        name="keep",
    )(left, right)


def shards(
    prefill_states,
    decode_states,
    attn_gain,
    w_qkv,
    w_out,
    ffn_gain,
    w_gate_up,
    w_down,
    prefill_pool,
    prefill_pages,
    prefill_lengths,
    prefill_home,
    decode_pool,
    decode_pages,
    decode_lengths,
    decode_home,
):
    n_tok = lax.axis_size("tok")
    n_head = lax.axis_size("head")
    width = prefill_states.shape[2]
    arrived, arrived_dec = project(
        prefill_states,
        decode_states,
        attn_gain.reshape(1, -1),
        jnp.transpose(w_qkv, (1, 0, 2)),
        prefill_home,
        n_tok,
    )
    attn, dattn = attention(
        prefill_pages,
        prefill_lengths,
        prefill_home,
        decode_pages,
        decode_lengths,
        decode_home,
        arrived,
        arrived_dec,
        prefill_pool.reshape(-1, 2 * HD),
        decode_pool.reshape(-1, decode_pool.shape[2]),
    )
    normed, dnormed, resid, dresid = mix(
        attn,
        dattn,
        prefill_states,
        decode_states,
        ffn_gain.reshape(1, -1),
        w_out,
        prefill_home,
        decode_home,
        n_head,
    )
    prefill_out, decode_out = ffn(
        normed,
        dnormed,
        resid,
        dresid,
        jnp.transpose(w_gate_up, (1, 2, 0)).reshape(-1, width),
        w_down,
        n_tok,
    )
    return keep(prefill_out, decode_out)


def solution(mesh):
    placed = (
        P(None, "tok", None),
        P("tok", None),
        P(),
        P(None, None, "head"),
        P("head", None),
        P(),
        P(None, None, "tok"),
        P("tok", None),
        P("tok", None, "head"),
        P("tok", None),
        P(),
        P(),
        P("tok", None, "head"),
        P("tok", None),
        P("tok"),
        P(),
    )
    return jax.shard_map(
        shards,
        mesh=mesh,
        in_specs=placed,
        out_specs=(P(None, ("tok", "head"), None), P(("tok", "head"), None)),
        check_vma=False,
    )
```
